32 devices in a mesh: dp: 8 (over z, y), tensor: 4 (over x, core).
Axes of the slice: x: 2, y: 2, z: 4, core: 2. Of those that a mesh axis runs over, the one named last changes fastest.
Arguments:
- layer_input_rows: bfloat16 [32768, 768], P(('dp', 'tensor')), may hold values from -6 to 6
- output_gradient: bfloat16 [32768, 768], P(('dp', 'tensor')), may hold values from -6 to 6
- query_weight: bfloat16 [768, 768], P('dp', 'tensor'), may hold values from -0.21875 to 0.21875
- key_weight: bfloat16 [768, 768], P('dp', 'tensor'), may hold values from -0.21875 to 0.21875
- value_weight: bfloat16 [768, 768], P('dp', 'tensor'), may hold values from -0.21875 to 0.21875
- output_weight: bfloat16 [768, 768], P('tensor', 'dp'), may hold values from -1.75 to 1.75
- up_weight: bfloat16 [768, 3072], P('dp', 'tensor'), may hold values from -0.21875 to 0.21875
- down_weight: bfloat16 [3072, 768], P('tensor', 'dp'), may hold values from -0.109375 to 0.109375
- query_bias_vector: float32 [768], P('tensor'), may hold values from -3 to 3
- value_bias_vector: float32 [768], P('tensor'), may hold values from -3 to 3
- output_bias_vector: float32 [768], replicated, may hold values from -5 to 5
- up_bias_vector: float32 [3072], P('tensor'), may hold values from -3 to 3
- down_bias_vector: float32 [768], replicated, may hold values from -2 to 2
- query_down_frozen: bfloat16 [768, 8], replicated, may hold values from -0.21875 to 0.21875
- value_down_frozen: bfloat16 [768, 8], replicated, may hold values from -0.21875 to 0.21875
- query_up_trained: bfloat16 [8, 768], P(None, 'tensor'), may hold values from -0.59765625 to 0.59765625
- value_up_trained: bfloat16 [8, 768], P(None, 'tensor'), may hold values from -0.59765625 to 0.59765625
- first_norm_gain: float32 [768], replicated, may hold values from 0.5 to 1.5
- first_norm_bias: float32 [768], replicated, may hold values from -2 to 2
- second_norm_gain: float32 [768], replicated, may hold values from 0.5 to 1.5
- second_norm_bias: float32 [768], replicated, may hold values from -2 to 2
- segments: int32 [32768], P('dp'), may hold values from 0 to 48, as said below
- sentence_row_mask: int32 [32768], P('dp'), may hold values from 0 to 1, as said below
Outputs:
- output: bfloat16 [32768, 768], P(('dp', 'tensor'))
- grad_input: bfloat16 [32768, 768], P(('dp', 'tensor'))
- grad_lora_query: float32 [8, 768], P(None, 'tensor')
- grad_lora_value: float32 [8, 768], P(None, 'tensor')
The draws below stay inside these ranges and needn't reach their ends.
Inputs may be any that keep to these rules, and one draw needn't show every extreme that they name: `segments`: ids restart at 0 in every sequence of 512 rows and rise by one at each sentence boundary; sentences hold 8 to 128 rows, and the first sentence of every sequence holds exactly 128 rows; in the first sequence of all rows every later sentence holds exactly 8 rows; the padding rows at a sequence's end share one more id. `sentence_row_mask`: in each sequence of 512 rows the rows after the last sentence that ends before row 512 are 0, from 1 to 128 of them; all others are 1.
All inputs are finite; a program needn't handle non-finite values.
Results may differ from the reference program's by a relative error of at most 0.02.
Values may be sent and summed in bfloat16 or wider, within the bound.
A program may use at most 128 MiB of HBM per device.

```python
import jax
import jax.numpy as jnp
from jax import lax

MODEL_WIDTH = 768
HEADS = 12
HEAD_DIM = 64
FF = 3072
ADAPTER_RANK = 8
ADAPTER_NUMER = 16
SEQ = 512
MAX_SENT = 128
MIN_SENT = 8
SEQS = 8
TOKENS = 32768


def sentence_layout(key):
    count = TOKENS // SEQ
    slots = SEQ // MIN_SENT
    lengths = jax.random.randint(key, (count, slots), MIN_SENT, MAX_SENT + 1)
    lengths = lengths.at[0, :].set(MIN_SENT)
    lengths = lengths.at[:, 0].set(MAX_SENT)
    ends = jnp.cumsum(lengths, axis=1)
    places = jnp.arange(SEQ)
    segment_ids = jnp.sum((ends[:, None, :] <= places[None, :, None]).astype(jnp.int32), axis=2)
    fitted = jnp.max(jnp.where(ends < SEQ, ends, 0), axis=1)
    live_flags = (places[None, :] < fitted[:, None]).astype(jnp.int32)
    return (segment_ids.reshape(TOKENS).astype(jnp.int32), live_flags.reshape(TOKENS))


def draw_segments(key, part):
    return sentence_layout(jax.random.fold_in(key, 17))[0]


def draw_sentence_row_mask(key, part):
    return sentence_layout(jax.random.fold_in(key, 17))[1]


def level_of(key, dims, split, smallest, largest):
    level, own = 1.0, jax.random.fold_in(key, 6)
    for dim, parts in split:
        draws = jnp.exp(jax.random.uniform(jax.random.fold_in(own, dim), (parts,), jnp.float32, smallest / len(split), largest / len(split)))
        level = level * jnp.repeat(draws, dims[dim] // parts).reshape([-1 if axis == dim else 1 for axis in range(len(dims))])
    return level


def normal_values(key, extent, spread, most, cuts=(), dtype=jnp.bfloat16):
    level = level_of(key, extent, cuts, -0.22, 0.18) if cuts else 1.0
    array = jax.random.normal(key, extent, jnp.float32) * spread * level
    return jnp.minimum(jnp.maximum(array, -most), most).astype(dtype)


def setup_inputs(seed: int = 0) -> dict:
    seeds = jax.random.split(jax.random.key(seed), 24)
    return {
        "layer_input_rows": normal_values(seeds[0], (TOKENS, MODEL_WIDTH), 1.0, 6.0, ((0, 32),)),
        "output_gradient": normal_values(seeds[1], (TOKENS, MODEL_WIDTH), 1.0, 6.0, ((0, 32),)),
        "query_weight": normal_values(seeds[2], (MODEL_WIDTH, MODEL_WIDTH), MODEL_WIDTH ** -0.5, 0.21875, ((0, 8), (1, 4))),
        "key_weight": normal_values(seeds[3], (MODEL_WIDTH, MODEL_WIDTH), MODEL_WIDTH ** -0.5, 0.21875, ((0, 8), (1, 4))),
        "value_weight": normal_values(seeds[4], (MODEL_WIDTH, MODEL_WIDTH), MODEL_WIDTH ** -0.5, 0.21875, ((0, 8), (1, 4))),
        "output_weight": normal_values(seeds[5], (MODEL_WIDTH, MODEL_WIDTH), (max(MODEL_WIDTH // 64, 1)) ** -0.5, 1.75, ((0, 4), (1, 8))),
        "up_weight": normal_values(seeds[6], (MODEL_WIDTH, FF), MODEL_WIDTH ** -0.5, 0.21875, ((0, 8), (1, 4))),
        "down_weight": normal_values(seeds[7], (FF, MODEL_WIDTH), FF ** -0.5, 0.109375, ((0, 4), (1, 8))),
        "query_bias_vector": normal_values(seeds[8], (MODEL_WIDTH,), 0.5, 3.0, ((0, 4),), jnp.float32),
        "value_bias_vector": normal_values(seeds[9], (MODEL_WIDTH,), 0.5, 3.0, ((0, 4),), jnp.float32),
        "output_bias_vector": normal_values(seeds[10], (MODEL_WIDTH,), 1.0, 5.0, (), jnp.float32),
        "up_bias_vector": normal_values(seeds[11], (FF,), 0.5, 3.0, ((0, 4),), jnp.float32),
        "down_bias_vector": normal_values(seeds[12], (MODEL_WIDTH,), 0.3, 2.0, (), jnp.float32),
        "query_down_frozen": normal_values(seeds[13], (MODEL_WIDTH, ADAPTER_RANK), MODEL_WIDTH ** -0.5, 0.21875),
        "value_down_frozen": normal_values(seeds[14], (MODEL_WIDTH, ADAPTER_RANK), MODEL_WIDTH ** -0.5, 0.21875),
        "query_up_trained": normal_values(seeds[15], (ADAPTER_RANK, MODEL_WIDTH), 0.1, 0.59765625, ((1, 4),)),
        "value_up_trained": normal_values(seeds[16], (ADAPTER_RANK, MODEL_WIDTH), 0.1, 0.59765625, ((1, 4),)),
        "first_norm_gain": jnp.clip(1.0 + 0.1 * jax.random.normal(seeds[17], (MODEL_WIDTH,), jnp.float32), 0.5, 1.5),
        "first_norm_bias": normal_values(seeds[18], (MODEL_WIDTH,), 0.3, 2.0, (), jnp.float32),
        "second_norm_gain": jnp.clip(1.0 + 0.1 * jax.random.normal(seeds[19], (MODEL_WIDTH,), jnp.float32), 0.5, 1.5),
        "second_norm_bias": normal_values(seeds[20], (MODEL_WIDTH,), 0.3, 2.0, (), jnp.float32),
        "segments": draw_segments(jax.random.fold_in(seeds[23], 71), 0),
        "sentence_row_mask": draw_sentence_row_mask(jax.random.fold_in(seeds[23], 71), 0),
    }


TOP_PRECISION = lax.Precision.HIGHEST
EPSILON = 1e-05
NEG_FILL = -1e+30

@jax.custom_vjp
def low_rank_rows(v):
    return lax.optimization_barrier(v.astype(jnp.bfloat16)).astype(jnp.float32)

@jax.custom_vjp
def low_rank_backward(v):
    return v

def low_keep(v):
    return (low_rank_rows(v), None)

def low_pass(kept, grad):
    return (grad,)

def back_keep(v):
    return (v, None)

def back_low(kept, grad):
    return (low_rank_rows(grad),)
low_rank_rows.defvjp(low_keep, low_pass)
low_rank_backward.defvjp(back_keep, back_low)

def matrix_multiply(left, right):
    return jnp.dot(left, right, precision=TOP_PRECISION)

def norm_rows(row_matrix, gain, shift):
    mean = lax.optimization_barrier(jnp.mean(row_matrix, axis=-1, keepdims=True))
    centered = row_matrix - mean
    variance = lax.optimization_barrier(jnp.mean(centered * centered, axis=-1, keepdims=True))
    return centered * lax.rsqrt(variance + EPSILON) * gain + shift

def attention_sequence(query_rows, keys, value_rows, segment_ids, live_flags):
    scale = HEAD_DIM ** (-0.5)
    raw = jnp.einsum('qhd,khd->hqk', query_rows, keys, precision=TOP_PRECISION)
    scores = low_rank_backward(raw * scale)
    places = jnp.arange(SEQ)
    allowed = (segment_ids[:, None] == segment_ids[None, :]) & (live_flags[None, :] == 1) | (places[:, None] == places[None, :])
    scores = jnp.where(allowed[None], scores, NEG_FILL)
    highest = lax.optimization_barrier(jnp.max(scores, axis=-1, keepdims=True))
    powers = jnp.exp(scores - highest)
    probs = low_rank_rows(powers / lax.optimization_barrier(jnp.sum(powers, axis=-1, keepdims=True)))
    return jnp.einsum('hqk,khd->qhd', probs, value_rows, precision=TOP_PRECISION)

def forward_layer_block(row_matrix, query_adapter_rows, value_adapter_rows, frozen_matrix, segment_ids, live_flags):
    query_weight, key_weight, value_weight, output_weight, up_weight, down_weight, query_bias_vector, value_bias_vector, output_bias_vector, up_bias_vector, down_bias_vector, query_down_frozen, value_down_frozen, gain1, bias1, gain2, bias2 = frozen_matrix
    adapter_scale = ADAPTER_NUMER / ADAPTER_RANK
    block_rows = row_matrix.shape[0]
    query_up_update = low_rank_rows(matrix_multiply(row_matrix, query_down_frozen))
    value_up_update = low_rank_rows(matrix_multiply(row_matrix, value_down_frozen))
    query_rows = low_rank_rows(low_rank_backward(matrix_multiply(row_matrix, query_weight) + query_bias_vector + adapter_scale * matrix_multiply(query_up_update, query_adapter_rows)))
    keys = low_rank_rows(low_rank_backward(matrix_multiply(row_matrix, key_weight)))
    value_rows = low_rank_rows(low_rank_backward(matrix_multiply(row_matrix, value_weight) + value_bias_vector + adapter_scale * matrix_multiply(value_up_update, value_adapter_rows)))
    shape = (block_rows // SEQ, SEQ, HEADS, HEAD_DIM)
    checked = jax.checkpoint(attention_sequence)
    context = lax.map(lambda item: checked(*item), (query_rows.reshape(shape), keys.reshape(shape), value_rows.reshape(shape), segment_ids.reshape(block_rows // SEQ, SEQ), live_flags.reshape(block_rows // SEQ, SEQ)))
    context = low_rank_rows(low_rank_backward(context.reshape(block_rows, MODEL_WIDTH)))
    attn_out = low_rank_backward(matrix_multiply(context, output_weight) + output_bias_vector)
    first = norm_rows(row_matrix + attn_out, gain1, bias1)
    middle = low_rank_rows(first)
    inner = low_rank_backward(matrix_multiply(middle, up_weight) + up_bias_vector)
    active = low_rank_rows(jax.nn.gelu(inner, approximate=False))
    ffn_out = low_rank_backward(matrix_multiply(active, down_weight) + down_bias_vector)
    return norm_rows(first + ffn_out, gain2, bias2)

def reference(layer_input_rows, output_gradient, query_weight, key_weight, value_weight, output_weight, up_weight, down_weight, query_bias_vector, value_bias_vector, output_bias_vector, up_bias_vector, down_bias_vector, query_down_frozen, value_down_frozen, query_up_trained, value_up_trained, first_norm_gain, first_norm_bias, second_norm_gain, second_norm_bias, segments, sentence_row_mask):
    wide_matrix = jnp.float32
    frozen_matrix = tuple((item.astype(wide_matrix) for item in (query_weight, key_weight, value_weight, output_weight, up_weight, down_weight, query_bias_vector, value_bias_vector, output_bias_vector, up_bias_vector, down_bias_vector, query_down_frozen, value_down_frozen, first_norm_gain, first_norm_bias, second_norm_gain, second_norm_bias)))
    block_rows = SEQ * SEQS
    blocks = TOKENS // block_rows
    rows_all = layer_input_rows.astype(wide_matrix).reshape(blocks, block_rows, MODEL_WIDTH)
    grads_all = output_gradient.astype(wide_matrix).reshape(blocks, block_rows, MODEL_WIDTH)
    segment_all = segments.reshape(blocks, block_rows)
    live_all = sentence_row_mask.reshape(blocks, block_rows)
    query_adapter_rows = query_up_trained.astype(wide_matrix)
    value_adapter_rows = value_up_trained.astype(wide_matrix)

    def step(carry, item):
        row_matrix, grads, segment_ids, live_flags = item

        def forward_apply(input_row_matrix, query_adapter_term, value_adapter_term):
            return forward_layer_block(input_row_matrix, query_adapter_term, value_adapter_term, frozen_matrix, segment_ids, live_flags)
        result_value, pullback_function = jax.vjp(forward_apply, row_matrix, query_adapter_rows, value_adapter_rows)
        grad_rows, grad_q, grad_v = pullback_function(grads)
        return ((carry[0] + grad_q, carry[1] + grad_v), (result_value.astype(jnp.bfloat16), grad_rows.astype(jnp.bfloat16)))
    start = (jnp.zeros((ADAPTER_RANK, MODEL_WIDTH), wide_matrix), jnp.zeros((ADAPTER_RANK, MODEL_WIDTH), wide_matrix))
    (grad_q, grad_v), (outputs, grad_rows) = lax.scan(step, start, (rows_all, grads_all, segment_all, live_all))
    return (outputs.reshape(TOKENS, MODEL_WIDTH), grad_rows.reshape(TOKENS, MODEL_WIDTH), grad_q, grad_v)
```

```python
import jax
import jax.numpy as jnp
from jax import lax
from jax.sharding import PartitionSpec as P

HEAD_DIM = 64
ADAPTER_RANK = 8
ADAPTER_NUMER = 16
SEQ = 512
EPSILON = 1e-05
NEG_FILL = -1e30
WIDE = jnp.float32
NARROW = jnp.bfloat16


def layer_norm(rows, gain, shift):
    mean = jnp.mean(rows, axis=-1, keepdims=True)
    centered = rows - mean
    variance = jnp.mean(centered * centered, axis=-1, keepdims=True)
    inverse = lax.rsqrt(variance + EPSILON)
    normed = centered * inverse
    return normed * gain + shift, normed, inverse


def norm_back(grad, normed, inverse, gain):
    scaled = grad * gain
    centered = scaled - jnp.mean(scaled, axis=-1, keepdims=True)
    return inverse * (centered - normed * jnp.mean(scaled * normed, axis=-1, keepdims=True))


def mm(left, right):
    return jnp.dot(left, right, preferred_element_type=WIDE)


def mm_nt(left, right):
    return lax.dot_general(left, right, (((1,), (1,)), ((), ())), preferred_element_type=WIDE)


def mm_tn(left, right):
    return lax.dot_general(left, right, (((0,), (0,)), ((), ())), preferred_element_type=WIDE)


def body(
    layer_input_rows,
    output_gradient,
    query_weight,
    key_weight,
    value_weight,
    output_weight,
    up_weight,
    down_weight,
    query_bias_vector,
    value_bias_vector,
    output_bias_vector,
    up_bias_vector,
    down_bias_vector,
    query_down_frozen,
    value_down_frozen,
    query_up_trained,
    value_up_trained,
    first_norm_gain,
    first_norm_bias,
    second_norm_gain,
    second_norm_bias,
    segments,
    sentence_row_mask,
):
    adapter_scale = ADAPTER_NUMER / ADAPTER_RANK
    everyone = ("tensor", "dp")

    def spread(block):
        return lax.all_gather(block, everyone, axis=0, tiled=True)

    width = layer_input_rows.shape[1]
    rows = layer_input_rows.shape[0]

    def columns(block):
        full = spread(block)
        groups = full.shape[0] // width
        return full.reshape(groups, width, block.shape[1]).transpose(1, 0, 2).reshape(width, -1)

    full_query = columns(query_weight)
    full_key = columns(key_weight)
    full_value = columns(value_weight)
    full_out_t = columns(output_weight.T)
    full_up = columns(up_weight)
    full_down_t = columns(down_weight.T)
    query_bias = lax.all_gather(query_bias_vector, "tensor", axis=0, tiled=True)
    value_bias = lax.all_gather(value_bias_vector, "tensor", axis=0, tiled=True)
    up_bias = lax.all_gather(up_bias_vector, "tensor", axis=0, tiled=True)
    query_up = lax.all_gather(query_up_trained, "tensor", axis=1, tiled=True)
    value_up = lax.all_gather(value_up_trained, "tensor", axis=1, tiled=True)

    place = lax.axis_index("tensor")
    segment_ids = lax.dynamic_slice_in_dim(segments, place * rows, rows).reshape(-1, SEQ)
    live = lax.dynamic_slice_in_dim(sentence_row_mask, place * rows, rows).reshape(-1, SEQ)
    seqs = rows // SEQ
    heads = width // HEAD_DIM

    x = layer_input_rows
    u_q = mm(x, query_down_frozen).astype(NARROW)
    u_v = mm(x, value_down_frozen).astype(NARROW)
    q = (mm(x, full_query) + query_bias + adapter_scale * mm(u_q, query_up)).astype(NARROW)
    k = mm(x, full_key).astype(NARROW)
    v = (mm(x, full_value) + value_bias + adapter_scale * mm(u_v, value_up)).astype(NARROW)

    def by_heads(block):
        return block.reshape(seqs, SEQ, heads, HEAD_DIM)

    scale = HEAD_DIM**-0.5
    qh, kh, vh = by_heads(q), by_heads(k), by_heads(v)
    places = jnp.arange(SEQ)
    allowed = (segment_ids[:, :, None] == segment_ids[:, None, :]) & (live[:, None, :] == 1)
    allowed = allowed | (places[:, None] == places[None, :])[None]
    scores = jnp.einsum("sqhd,skhd->shqk", qh, kh, preferred_element_type=WIDE) * scale
    scores = jnp.where(allowed[:, None], scores, NEG_FILL)
    highest = jnp.max(scores, axis=-1, keepdims=True)
    powers = jnp.exp(scores - highest)
    probs = (powers / jnp.sum(powers, axis=-1, keepdims=True)).astype(NARROW)
    context = (
        jnp.einsum("shqk,skhd->sqhd", probs, vh, preferred_element_type=WIDE)
        .astype(NARROW)
        .reshape(rows, width)
    )
    attn = mm_nt(context, full_out_t) + output_bias_vector
    first, n1, s1 = layer_norm(x.astype(WIDE) + attn, first_norm_gain, first_norm_bias)
    middle = first.astype(NARROW)
    inner = mm(middle, full_up) + up_bias
    active, slope = jax.vjp(lambda value: jax.nn.gelu(value, approximate=False), inner)
    ffn = mm_nt(active.astype(NARROW), full_down_t) + down_bias_vector
    output, n2, s2 = layer_norm(first + ffn, second_norm_gain, second_norm_bias)

    grad_second = norm_back(output_gradient.astype(WIDE), n2, s2, second_norm_gain)
    grad_active = mm(grad_second.astype(NARROW), full_down_t)
    grad_inner = slope(grad_active)[0].astype(NARROW)
    grad_first = norm_back(grad_second + mm_nt(grad_inner, full_up), n1, s1, first_norm_gain)
    grad_context = by_heads(mm(grad_first.astype(NARROW), full_out_t).astype(NARROW))
    grad_probs = jnp.einsum("sqhd,skhd->shqk", grad_context, vh, preferred_element_type=WIDE)
    probs_wide = probs.astype(WIDE)
    inside = jnp.sum(probs_wide * grad_probs, axis=-1, keepdims=True)
    grad_scores = (probs_wide * (grad_probs - inside)).astype(NARROW)
    gq = jnp.einsum("shqk,skhd->sqhd", grad_scores, kh, preferred_element_type=WIDE) * scale
    gk = jnp.einsum("shqk,sqhd->skhd", grad_scores, qh, preferred_element_type=WIDE) * scale
    gv = jnp.einsum("shqk,sqhd->skhd", probs, grad_context, preferred_element_type=WIDE)
    gq, gk, gv = (item.astype(NARROW).reshape(rows, width) for item in (gq, gk, gv))
    back_q = adapter_scale * mm_nt(gq, query_up)
    back_v = adapter_scale * mm_nt(gv, value_up)
    grad_input = (
        grad_first
        + mm_nt(gq, full_query)
        + mm_nt(gk, full_key)
        + mm_nt(gv, full_value)
        + mm_nt(back_q, query_down_frozen.astype(WIDE))
        + mm_nt(back_v, value_down_frozen.astype(WIDE))
    )
    grads = jnp.concatenate([mm_tn(u_q, gq), mm_tn(u_v, gv)], axis=0) * adapter_scale
    grads = lax.psum(grads, everyone)
    mine = query_up_trained.shape[1]
    grads = lax.dynamic_slice_in_dim(grads, place * mine, mine, axis=1)
    return (
        output.astype(NARROW),
        grad_input.astype(NARROW),
        grads[:ADAPTER_RANK],
        grads[ADAPTER_RANK:],
    )


IN_SPECS = (
    P(("dp", "tensor"), None),
    P(("dp", "tensor"), None),
    P("dp", "tensor"),
    P("dp", "tensor"),
    P("dp", "tensor"),
    P("tensor", "dp"),
    P("dp", "tensor"),
    P("tensor", "dp"),
    P("tensor"),
    P("tensor"),
    P(),
    P("tensor"),
    P(),
    P(),
    P(),
    P(None, "tensor"),
    P(None, "tensor"),
    P(),
    P(),
    P(),
    P(),
    P("dp"),
    P("dp"),
)
OUT_SPECS = (
    P(("dp", "tensor"), None),
    P(("dp", "tensor"), None),
    P(None, "tensor"),
    P(None, "tensor"),
)


def solution(mesh):
    return jax.shard_map(body, mesh=mesh, in_specs=IN_SPECS, out_specs=OUT_SPECS, check_vma=False)
```

```python
import functools

import jax
import jax.numpy as jnp
from jax import lax
from jax.experimental import pallas as pl
from jax.experimental.pallas import tpu as pltpu
from jax.sharding import PartitionSpec as P

HEAD_DIM = 64
ADAPTER_RANK = 8
ADAPTER_NUMER = 16
SEQ = 512
LANES = 128
EPSILON = 1e-05
NEG_FILL = -1e30
WIDE = jnp.float32
NARROW = jnp.bfloat16
ADAPTER_SCALE = ADAPTER_NUMER / ADAPTER_RANK
SCORE_SCALE = HEAD_DIM**-0.5

KEY_SPANS = ((0, 128), (128, 384), (128, 512), (256, 512))
SPAN_STARTS = (0, 128, 384, 768)
SPAN_TOTAL = 1024


def mm(left, right):
    return jnp.dot(left, right, preferred_element_type=WIDE)


def mm_nt(left, right):
    return lax.dot_general(left, right, (((1,), (1,)), ((), ())), preferred_element_type=WIDE)


def row_mean(block):
    return jnp.sum(block, axis=-1, keepdims=True) * (1.0 / block.shape[-1])


def gelu_parts(value):
    size = jnp.abs(value)
    bell = jnp.exp(value * value * -0.5)
    t = 1.0 / (1.0 + size * (0.3275911 * 0.7071067811865476))
    series = t * (
        0.5 * 0.254829592
        + t
        * (
            0.5 * -0.284496736
            + t * (0.5 * 1.421413741 + t * (0.5 * -1.453152027 + t * (0.5 * 1.061405429)))
        )
    )
    tail = series * bell
    below = jnp.where(value < 0.0, tail, 1.0 - tail)
    return value * below, below + value * bell * 0.3989422804014327


def pair_select(low, high):
    lane = lax.broadcasted_iota(jnp.int32, low.shape, 1)
    return jnp.where(lane < HEAD_DIM, low, pltpu.roll(high, HEAD_DIM, 1))


def kernel(
    x_ref,
    gout_ref,
    a_ref,
    b_ref,
    c_ref,
    vec_ref,
    upb_ref,
    down_t_ref,
    seg_ref,
    live_ref,
    out_ref,
    gin_ref,
    gl_ref,
    wq,
    wk,
    wv,
    wo,
    q,
    k,
    v,
    probs,
    ctx,
    n1,
    s1,
    act,
    slope,
    acc,
    mask,
    u_t,
):
    rows, width = x_ref.shape
    seqs = rows // SEQ
    pairs = width // LANES
    groups = a_ref.shape[0]

    for group in range(groups):
        at = slice(group * LANES, (group + 1) * LANES)
        wq[:, at] = a_ref[group, :, 0:128]
        wk[:, at] = a_ref[group, :, 128:256]
        wv[:, at] = a_ref[group, :, 256:384]
        wo[:, at] = a_ref[group, :, 640:768]
    for half in range(groups // 2):
        at = slice((groups + half) * LANES, (groups + half + 1) * LANES)
        first = a_ref[2 * half, :, 384:512].astype(WIDE)
        second = a_ref[2 * half + 1, :, 384:512].astype(WIDE)
        wq[:, at] = pair_select(first, second).astype(NARROW)
        wk[:, at] = pair_select(pltpu.roll(first, HEAD_DIM, 1), pltpu.roll(second, HEAD_DIM, 1)).astype(NARROW)
        first = a_ref[2 * half, :, 512:640].astype(WIDE)
        second = a_ref[2 * half + 1, :, 512:640].astype(WIDE)
        wv[:, at] = pair_select(first, second).astype(NARROW)
        wo[:, at] = pair_select(pltpu.roll(first, HEAD_DIM, 1), pltpu.roll(second, HEAD_DIM, 1)).astype(NARROW)

    place = lax.broadcasted_iota(jnp.int32, (LANES, LANES), 0) == lax.broadcasted_iota(
        jnp.int32, (LANES, LANES), 1
    )
    for seq in range(seqs):
        wide_ids = []
        key_ids = []
        for block in range(4):
            row = seq * 4 + block
            ids = seg_ref[row : row + 1, :].astype(WIDE)
            live = live_ref[row : row + 1, :]
            key = jnp.where(live == 1, ids, -1.0)
            wide_ids.append(ids)
            key_ids.append(jnp.transpose(jnp.broadcast_to(key, (LANES, LANES))))
        for block in range(1, 4):
            start, stop = KEY_SPANS[block]
            for j in range((stop - start) // LANES):
                kb = start // LANES + j
                seen = key_ids[kb] == wide_ids[block]
                if kb == block:
                    seen = seen | place
                at = SPAN_STARTS[block] + j * LANES
                mask[seq, at : at + LANES, :] = jnp.where(seen, 0.0, NEG_FILL)

    u_t[...] = mm_nt(down_t_ref[...], x_ref[...]).astype(NARROW)

    def project(step, carry):
        at = pl.ds(pl.multiple_of(step * 256, 256), 256)
        xs = x_ref[...]
        q[:, at] = (mm(xs, wq[:, at]) + vec_ref[0:1, at]).astype(NARROW)
        k[:, at] = mm(xs, wk[:, at]).astype(NARROW)
        v[:, at] = (mm(xs, wv[:, at]) + vec_ref[1:2, at]).astype(NARROW)
        return carry

    lax.fori_loop(0, width // 256, project, 0)

    lane = lax.broadcasted_iota(jnp.int32, (LANES, LANES), 1)

    def stacked(tile):
        none = jnp.zeros_like(tile)
        return jnp.concatenate(
            [jnp.where(lane < HEAD_DIM, tile, none), jnp.where(lane < HEAD_DIM, none, tile)], axis=0
        )

    def turned(tile):
        own = jnp.concatenate([tile[:HEAD_DIM, :LANES], tile[HEAD_DIM:, LANES:]], axis=0)
        return jnp.transpose(own)

    def attend(step, carry):
        seq = step // pairs
        pair = step - seq * pairs
        at = pl.ds(pl.multiple_of(pair * LANES, LANES), LANES)
        base = pl.multiple_of(seq * SEQ, SEQ)
        everything = pl.ds(base, SEQ)
        keys = k[everything, at]
        values_t = jnp.transpose(v[everything, at].astype(WIDE)).astype(NARROW)
        for block, (start, stop) in enumerate(KEY_SPANS):
            here = pl.ds(base + block * LANES, LANES)
            scores = mm_nt(keys[start:stop], stacked(q[here, at]))
            span = pl.ds(SPAN_STARTS[block], stop - start)
            if block:
                shade = mask[seq, span, :]
                scores = scores + jnp.concatenate([shade, shade], axis=1)
            top = jnp.max(scores, axis=0, keepdims=True)
            powers = jnp.exp(scores - top)
            total = jnp.sum(powers, axis=0, keepdims=True)
            weights = (powers * (1.0 / total)).astype(NARROW)
            probs[step, span, :] = weights
            ctx[here, at] = turned(mm(values_t[:, start:stop], weights)).astype(NARROW)
        return carry

    lax.fori_loop(0, seqs * pairs, attend, 0)

    def first_norm(step, carry):
        at = pl.ds(pl.multiple_of(step * 256, 256), 256)
        r = x_ref[at, :].astype(WIDE) + (mm_nt(ctx[at, :], wo[...]) + vec_ref[2:3, :])
        centered = r - row_mean(r)
        inverse = lax.rsqrt(row_mean(centered * centered) + EPSILON)
        normed = centered * inverse
        n1[at, :] = normed
        s1[at, :] = inverse
        out_ref[at, :] = (normed * vec_ref[4:5, :] + vec_ref[5:6, :]).astype(NARROW)
        return carry

    lax.fori_loop(0, rows // 256, first_norm, 0)

    def up(group, carry):
        for j in range(width // 256):
            cols = slice(j * 256, (j + 1) * 256)
            at = pl.ds(pl.multiple_of(group * width + j * 256, 256), 256)
            inner = mm(out_ref[...], b_ref[group, :, cols]) + upb_ref[0:1, at]
            value, grad = gelu_parts(inner)
            act[:, at] = value.astype(NARROW)
            slope[:, at] = grad.astype(NARROW)
        return carry

    lax.fori_loop(0, groups, up, 0)

    def second_norm(step, carry):
        at = pl.ds(pl.multiple_of(step * 256, 256), 256)
        r = n1[at, :] * vec_ref[4:5, :] + vec_ref[5:6, :] + vec_ref[3:4, :]
        for group in range(groups):
            r = r + mm_nt(act[at, group * width : (group + 1) * width], c_ref[group])
        centered = r - row_mean(r)
        inverse = lax.rsqrt(row_mean(centered * centered) + EPSILON)
        normed = centered * inverse
        out_ref[at, :] = (normed * vec_ref[6:7, :] + vec_ref[7:8, :]).astype(NARROW)
        e = gout_ref[at, :].astype(WIDE) * vec_ref[6:7, :]
        acc[at, :] = inverse * (e - row_mean(e) - normed * row_mean(e * normed))
        return carry

    lax.fori_loop(0, rows // 256, second_norm, 0)

    def down_back(step, carry):
        at = pl.ds(pl.multiple_of(step * 256, 256), 256)
        second = acc[at, :]
        low = second.astype(NARROW)
        total = second
        for group in range(groups):
            cols = slice(group * width, (group + 1) * width)
            grad = (mm(low, c_ref[group]) * slope[at, cols].astype(WIDE)).astype(NARROW)
            total = total + mm_nt(grad, b_ref[group])
        normed = n1[at, :]
        e = total * vec_ref[4:5, :]
        first = s1[at, :] * (e - row_mean(e) - normed * row_mean(e * normed))
        acc[at, :] = first
        ctx[at, :] = mm(first.astype(NARROW), wo[...]).astype(NARROW)
        return carry

    lax.fori_loop(0, rows // 256, down_back, 0)

    def attend_back(step, carry):
        seq = step // pairs
        pair = step - seq * pairs
        at = pl.ds(pl.multiple_of(pair * LANES, LANES), LANES)
        base = pl.multiple_of(seq * SEQ, SEQ)
        everything = pl.ds(base, SEQ)
        keys = k[everything, at]
        values = v[everything, at]
        keys_t = jnp.transpose(keys.astype(WIDE)).astype(NARROW)
        grad_k = [None] * 4
        grad_v = [None] * 4
        for block, (start, stop) in enumerate(KEY_SPANS):
            here = pl.ds(base + block * LANES, LANES)
            grads = stacked(ctx[here, at])
            span = pl.ds(SPAN_STARTS[block], stop - start)
            weights = probs[step, span, :]
            part = weights.astype(WIDE) * mm_nt(values[start:stop], grads)
            inside = jnp.sum(part, axis=0, keepdims=True)
            grad_scores = (part - weights.astype(WIDE) * inside).astype(NARROW)
            for_keys = mm(grad_scores, stacked(q[here, at]))
            for_values = mm(weights, grads)
            q[here, at] = turned(mm(keys_t[:, start:stop], grad_scores)).astype(NARROW)
            for j in range((stop - start) // LANES):
                kb = start // LANES + j
                rows_here = slice(j * LANES, (j + 1) * LANES)
                grad_k[kb] = for_keys[rows_here] if grad_k[kb] is None else grad_k[kb] + for_keys[rows_here]
                grad_v[kb] = (
                    for_values[rows_here] if grad_v[kb] is None else grad_v[kb] + for_values[rows_here]
                )
        for kb in range(4):
            here = pl.ds(base + kb * LANES, LANES)
            k[here, at] = grad_k[kb].astype(NARROW)
            v[here, at] = grad_v[kb].astype(NARROW)
        return carry

    lax.fori_loop(0, seqs * pairs, attend_back, 0)

    def input_back(step, carry):
        at = pl.ds(pl.multiple_of(step * 256, 256), 256)
        total = acc[at, :] + mm_nt(q[at, :], wq[...])
        total = total + mm_nt(k[at, :], wk[...])
        total = total + mm_nt(v[at, :], wv[...])
        gin_ref[at, :] = total.astype(NARROW)
        return carry

    lax.fori_loop(0, rows // 256, input_back, 0)

    gl_ref[0:8, :] = mm(u_t[0:8, :], q[...]) * (ADAPTER_SCALE * SCORE_SCALE)
    gl_ref[8:16, :] = mm(u_t[8:16, :], v[...]) * ADAPTER_SCALE


def run_layer(x, gout, a, b, c, vectors, up_bias, down_t, seg, live):
    rows, width = x.shape
    hidden = up_bias.shape[1]
    pairs = width // LANES
    seqs = rows // SEQ
    shape = jax.ShapeDtypeStruct
    square = pltpu.VMEM((width, width), NARROW)
    plane = pltpu.VMEM((rows, width), NARROW)
    return pl.pallas_call(
        kernel,
        out_shape=(
            shape((rows, width), NARROW),
            shape((rows, width), NARROW),
            shape((2 * ADAPTER_RANK, width), WIDE),
        ),
        in_specs=[pl.BlockSpec(memory_space=pltpu.VMEM)] * 10,
        out_specs=[pl.BlockSpec(memory_space=pltpu.VMEM)] * 3,
        scratch_shapes=[
            square,
            square,
            square,
            square,
            plane,
            plane,
            plane,
            pltpu.VMEM((seqs * pairs, SPAN_TOTAL, 2 * LANES), NARROW),
            plane,
            pltpu.VMEM((rows, width), WIDE),
            pltpu.VMEM((rows, 1), WIDE),
            pltpu.VMEM((rows, hidden), NARROW),
            pltpu.VMEM((rows, hidden), NARROW),
            pltpu.VMEM((rows, width), WIDE),
            pltpu.VMEM((seqs, SPAN_TOTAL, LANES), WIDE),
            pltpu.VMEM((2 * ADAPTER_RANK, rows), NARROW),
        ],
        compiler_params=pltpu.CompilerParams(vmem_limit_bytes=63 << 20),
    )(x, gout, a, b, c, vectors, up_bias, down_t, seg, live)


def in_pairs(block, groups):
    parts = block.reshape(block.shape[0], groups, 3, HEAD_DIM)
    front = parts[:, :, :2].reshape(block.shape[0], -1)
    return jnp.concatenate([front, parts[:, :, 2].reshape(block.shape[0], -1)], axis=1)


def from_pairs(block, groups):
    front = block[:, : groups * LANES].reshape(block.shape[0], groups, 2, HEAD_DIM)
    back = block[:, groups * LANES :].reshape(block.shape[0], groups, 1, HEAD_DIM)
    return jnp.concatenate([front, back], axis=2).reshape(block.shape[0], -1)


def body(
    layer_input_rows,
    output_gradient,
    query_weight,
    key_weight,
    value_weight,
    output_weight,
    up_weight,
    down_weight,
    query_bias_vector,
    value_bias_vector,
    output_bias_vector,
    up_bias_vector,
    down_bias_vector,
    query_down_frozen,
    value_down_frozen,
    query_up_trained,
    value_up_trained,
    first_norm_gain,
    first_norm_bias,
    second_norm_gain,
    second_norm_bias,
    segments,
    sentence_row_mask,
):
    everyone = ("tensor", "dp")
    rows, width = layer_input_rows.shape
    groups = width // query_weight.shape[1]
    depth = query_weight.shape[0]
    place = lax.axis_index("tensor")
    which = lax.axis_index("dp")

    def folded(weight, down, up):
        own = lax.dynamic_slice_in_dim(down, which * depth, depth, axis=0)
        return weight.astype(WIDE) + ADAPTER_SCALE * mm(own, up)

    wq = (folded(query_weight, query_down_frozen, query_up_trained) * SCORE_SCALE).astype(NARROW)
    wv = folded(value_weight, value_down_frozen, value_up_trained).astype(NARROW)
    wk = key_weight
    wo = output_weight.T
    block_a = jnp.concatenate(
        [wq[:, :128], wk[:, :128], wv[:, :128], wq[:, 128:], wk[:, 128:], wv[:, 128:], wo[:, 128:], wo[:, :128]],
        axis=1,
    )

    def spread(block):
        return lax.all_gather(block, everyone, axis=0, tiled=True).reshape(groups, width, width)

    a, b, c = spread(block_a), spread(up_weight), spread(down_weight.T)
    query_bias = lax.all_gather(query_bias_vector * SCORE_SCALE, "tensor", axis=0, tiled=True)
    value_bias = lax.all_gather(value_bias_vector, "tensor", axis=0, tiled=True)
    up_bias = lax.all_gather(up_bias_vector, "tensor", axis=0, tiled=True)
    vectors = jnp.concatenate(
        [
            in_pairs(query_bias[None], groups),
            in_pairs(value_bias[None], groups),
            output_bias_vector[None],
            down_bias_vector[None],
            first_norm_gain[None],
            first_norm_bias[None],
            second_norm_gain[None],
            second_norm_bias[None],
        ],
        axis=0,
    )
    down_t = jnp.concatenate([query_down_frozen, value_down_frozen], axis=1).T
    seg = lax.dynamic_slice_in_dim(segments, place * rows, rows).reshape(-1, LANES)
    live = lax.dynamic_slice_in_dim(sentence_row_mask, place * rows, rows).reshape(-1, LANES)
    output, grad_input, grads = run_layer(
        layer_input_rows, output_gradient, a, b, c, vectors, up_bias[None], down_t, seg, live
    )
    grads = from_pairs(lax.psum(grads, everyone), groups)
    mine = query_up_trained.shape[1]
    grads = lax.dynamic_slice_in_dim(grads, place * mine, mine, axis=1)
    return output, grad_input, grads[:ADAPTER_RANK], grads[ADAPTER_RANK:]


IN_SPECS = (
    P(("dp", "tensor"), None),
    P(("dp", "tensor"), None),
    P("dp", "tensor"),
    P("dp", "tensor"),
    P("dp", "tensor"),
    P("tensor", "dp"),
    P("dp", "tensor"),
    P("tensor", "dp"),
    P("tensor"),
    P("tensor"),
    P(),
    P("tensor"),
    P(),
    P(),
    P(),
    P(None, "tensor"),
    P(None, "tensor"),
    P(),
    P(),
    P(),
    P(),
    P("dp"),
    P("dp"),
)
OUT_SPECS = (
    P(("dp", "tensor"), None),
    P(("dp", "tensor"), None),
    P(None, "tensor"),
    P(None, "tensor"),
)


def solution(mesh):
    return jax.shard_map(body, mesh=mesh, in_specs=IN_SPECS, out_specs=OUT_SPECS, check_vma=False)
```

```python
import functools

import jax
import jax.numpy as jnp
from jax import lax
from jax.experimental import pallas as pl
from jax.experimental.pallas import tpu as pltpu
from jax.sharding import PartitionSpec as P

HEAD_DIM = 64
ADAPTER_RANK = 8
ADAPTER_NUMER = 16
SEQ = 512
LANES = 128
EPSILON = 1e-05
NEG_FILL = -1e30
WIDE = jnp.float32
NARROW = jnp.bfloat16
ADAPTER_SCALE = ADAPTER_NUMER / ADAPTER_RANK
SCORE_SCALE = HEAD_DIM**-0.5

KEY_SPANS = ((0, 128), (128, 384), (128, 512), (256, 512))
SPAN_STARTS = (0, 128, 384, 768)
SPAN_TOTAL = 1024
BY_MESH = pl.DeviceIdType.MESH

ARRIVALS = (
    ("Z1", "Z2", "Z3", "X0", "X1", "X2", "X3", "Y0", "Y1", "Y2", "Y3")
    + ("D0a", "D0b", "D1", "D2a", "D2b", "D3", "C")
    + tuple("C" + kind + str(k) for kind in "ZXYD" for k in range(4) if kind + str(k) != "Z0")
)
SIGNALS = {name: i for i, name in enumerate(ARRIVALS + ("Z2down",))}
PASS_ON = {
    "own": (("X0", "x", ""), ("Y0", "y", ""), ("Z1", "up", ""), ("Z3", "down", ""), ("C", "core", "")),
    "X0": (("X1", "up", ""), ("D0b", "y", "b"), ("CX0", "core", "")),
    "Y0": (("Y3", "down", ""), ("D0a", "x", "a"), ("CY0", "core", "")),
    "Z1": (("Y1", "y", ""), ("CZ1", "core", "")),
    "Z3": (("X3", "x", ""), ("CZ3", "core", "")),
    "X1": (("CX1", "core", ""),),
    "Y3": (("CY3", "core", ""),),
    "Z2": (("X2", "x", ""), ("Y2", "y", ""), ("CZ2", "core", "")),
    "Y1": (("D1", "x", ""), ("CY1", "core", "")),
    "X3": (("D3", "y", ""), ("CX3", "core", "")),
    "X2": (("D2b", "y", "b"), ("CX2", "core", "")),
    "Y2": (("D2a", "x", "a"), ("CY2", "core", "")),
    "D0b": (("CD0", "core", ""),),
    "D1": (("CD1", "core", ""),),
    "D2b": (("CD2", "core", ""),),
    "D3": (("CD3", "core", ""),),
}
ROUNDS = (
    ("own",),
    ("X0", "Y0", "Z1", "Z3"),
    ("X1", "Y3", "Z2", "Y1", "X3"),
    ("X2", "Y2", "D0a", "D0b", "D1", "D3"),
    ("D2a", "D2b"),
    tuple(name for name in ARRIVALS if name[0] == "C"),
)


def in_rounds(*rounds):
    return [(group, name) for number, group in rounds for name in ROUNDS[number]]


PLAN = {
    "start": {0: in_rounds((0, 1), (0, 2))},
    "masked": {0: in_rounds(*((number, group) for number in range(1, 6) for group in range(3)))},
}


class Gather:
    def __init__(self, blocks, send, recv):
        self.blocks, self.send, self.recv = blocks, send, recv
        self.d, self.t = lax.axis_index("dp"), lax.axis_index("tensor")
        self.depth = blocks[0].shape[1] // 8
        self.z, self.y = self.d // 2, lax.rem(self.d, 2)
        self.tx = lax.rem(self.t + 2, 4)
        self.tc = self.t + 1 - 2 * lax.rem(self.t, 2)
        self.txc = lax.rem(self.tc + 2, 4)
        self.middle = (self.z == 1) | (self.z == 2)

    def peer(self, kind):
        return {
            "x": (self.d, self.tx),
            "y": (self.z * 2 + 1 - self.y, self.t),
            "core": (self.d, self.tc),
            "up": (lax.rem(self.z + 1, 4) * 2 + self.y, self.t),
            "down": (lax.rem(self.z + 3, 4) * 2 + self.y, self.t),
        }[kind]

    def part(self, group, name, half=""):
        if name == "own":
            dp, t = self.d, self.t
        elif name == "C":
            dp, t = self.d, self.tc
        else:
            kind = name[-2] if name[-1].isdigit() else name[-3]
            k = int(name[-1] if name[-1].isdigit() else name[-2])
            half = half or (name[-1] if not name[-1].isdigit() else "")
            near, far = (self.tc, self.txc) if name[0] == "C" else (self.t, self.tx)
            dp = lax.rem(self.z - k + 4, 4) * 2 + (self.y if kind in "ZX" else 1 - self.y)
            t = near if kind in "ZY" else far
        size = self.depth // 2 if half else self.depth
        first = dp * self.depth + (size if half == "b" else 0)
        return self.blocks[group].at[t, pl.ds(pl.multiple_of(first, 16), size), :]

    def copy(self, group, part, name, to, sender=None):
        return pltpu.make_async_remote_copy(
            src_ref=part,
            dst_ref=part,
            send_sem=self.send.at[group, SIGNALS[sender or name]],
            recv_sem=self.recv.at[group, SIGNALS[name]],
            device_id=self.peer(to),
            device_id_type=BY_MESH,
        )

    def outgoing(self, group, name):
        whole = name[:2] if name[0] == "D" else name
        return [
            self.copy(group, self.part(group, whole, half), out, to)
            for out, to, half in PASS_ON.get(name, ())
        ]

    def relayed(self, group, name):
        to, sender = ("up", "Z2") if name == "Z1" else ("down", "Z2down")
        return self.copy(group, self.part(group, name), "Z2", to, sender)

    def step(self, group, name):
        if name != "own":
            self.copy(group, self.part(group, name), name, "x").wait_recv()
        for copy in self.outgoing(group, name):
            copy.start()
        if name in ("Z1", "Z3"):

            @pl.when(self.middle)
            def _():
                self.relayed(group, name).start()

    def finish(self, group):
        for name in PASS_ON:
            for copy in self.outgoing(group, name):
                copy.wait_send()

        @pl.when(self.middle)
        def _():
            self.relayed(group, "Z1").wait_send()
            self.relayed(group, "Z3").wait_send()


def mm(left, right):
    return jnp.dot(left, right, preferred_element_type=WIDE)


def mm_nt(left, right):
    return lax.dot_general(left, right, (((1,), (1,)), ((), ())), preferred_element_type=WIDE)


def row_mean(block):
    return jnp.sum(block, axis=-1, keepdims=True) * (1.0 / block.shape[-1])


def gelu_parts(value):
    size = jnp.abs(value)
    bell = jnp.exp(value * value * -0.5)
    t = 1.0 / (1.0 + size * (0.3275911 * 0.7071067811865476))
    series = t * (
        0.5 * 0.254829592
        + t
        * (
            0.5 * -0.284496736
            + t * (0.5 * 1.421413741 + t * (0.5 * -1.453152027 + t * (0.5 * 1.061405429)))
        )
    )
    tail = series * bell
    below = jnp.where(value < 0.0, tail, 1.0 - tail)
    return value * below, below + value * bell * 0.3989422804014327


def pair_select(low, high):
    lane = lax.broadcasted_iota(jnp.int32, low.shape, 1)
    return jnp.where(lane < HEAD_DIM, low, pltpu.roll(high, HEAD_DIM, 1))


def kernel(plan, *refs):
    if plan is not None:
        (x_ref, gout_ref, wq_ref, wk_ref, wv_ref, wo_ref, up_ref, down_ref, dq_ref, dv_ref, uq_ref, uv_ref) = refs[:12]
        (bq_ref, bv_ref, bup_ref, vec_ref, down_t_ref, seg_ref, live_ref) = refs[12:19]
        (out_ref, gin_ref, glq_ref, glv_ref) = refs[19:23]
        (wq, wk, wv, wo, q, k, v, probs, ctx, n1, s1, act, slope, acc, mask, u_t) = refs[23:39]
        (a_ref, b_ref, c_ref, bias, biases, part, near, far) = refs[39:47]
        (send, recv, bias_send, bias_recv, near_send, near_recv, far_send, far_recv) = refs[47:]
    else:
        (x_ref, gout_ref, a_ref, b_ref, c_ref, biases_ref, vec_ref, down_t_ref, seg_ref, live_ref) = refs[:10]
        (out_ref, gin_ref, gl_ref) = refs[10:13]
        (wq, wk, wv, wo, q, k, v, probs, ctx, n1, s1, act, slope, acc, mask, u_t, biases) = refs[13:]
    rows, width = x_ref.shape
    seqs = rows // SEQ
    pairs = width // LANES
    groups = a_ref.shape[0]

    if plan is not None:
        gather = Gather((a_ref, b_ref, c_ref), send, recv)
        me_d, me_t = gather.d, gather.t
        dps = width // wq_ref.shape[0]
        depth = wq_ref.shape[0]
        others_t = [lax.rem(me_t + i, groups) for i in range(1, groups)]
        others_d = [lax.rem(me_d + i, dps) for i in range(1, dps)]
        seg_rows = pl.ds(pl.multiple_of(me_t * (rows // LANES), rows // LANES), rows // LANES)
        barrier = pltpu.get_barrier_semaphore()
        for other in others_t:
            pl.semaphore_signal(barrier, inc=1, device_id=(me_d, other), device_id_type=BY_MESH)
        for other in others_d:
            pl.semaphore_signal(barrier, inc=1, device_id=(other, me_t), device_id_type=BY_MESH)

        mine = pl.ds(pl.multiple_of(me_d * depth, depth), depth)
        query = wq_ref[...].astype(WIDE) + ADAPTER_SCALE * mm(dq_ref[mine, :], uq_ref[...])
        query = query * SCORE_SCALE
        value = wv_ref[...].astype(WIDE) + ADAPTER_SCALE * mm(dv_ref[mine, :], uv_ref[...])
        key = wk_ref[...].astype(WIDE)
        out_t = jnp.transpose(wo_ref[...].astype(WIDE))
        a_ref[me_t, mine, 0:128] = query[:, 0:128].astype(NARROW)
        a_ref[me_t, mine, 128:256] = key[:, 0:128].astype(NARROW)
        a_ref[me_t, mine, 256:384] = value[:, 0:128].astype(NARROW)
        a_ref[me_t, mine, 384:512] = jnp.concatenate([query[:, 128:], key[:, 128:]], axis=1).astype(NARROW)
        a_ref[me_t, mine, 512:640] = jnp.concatenate([value[:, 128:], out_t[:, 128:]], axis=1).astype(NARROW)
        a_ref[me_t, mine, 640:768] = out_t[:, 0:128].astype(NARROW)
        bias[me_t, 0:1, :] = bup_ref[...]
        bias[me_t, 1:2, 0:192] = bq_ref[...] * SCORE_SCALE
        bias[me_t, 1:2, 256:448] = bv_ref[...]
        pl.semaphore_wait(barrier, len(others_t) + len(others_d))

        def bias_copy(i):
            return pltpu.make_async_remote_copy(
                src_ref=bias.at[me_t],
                dst_ref=bias.at[me_t],
                send_sem=bias_send.at[i],
                recv_sem=bias_recv.at[i],
                device_id=(me_d, others_t[i]),
                device_id_type=BY_MESH,
            )

        for name in ("own",):
            gather.step(0, name)
        b_ref[me_t, mine, :] = up_ref[...]
        c_ref[me_t, mine, :] = jnp.transpose(down_ref[...].astype(WIDE)).astype(NARROW)
        for i in range(len(others_t)):
            bias_copy(i).start()
    else:
        seg_rows = pl.ds(0, rows // LANES)
        biases[...] = biases_ref[...]

    def ticks(place, step=None):
        if plan is None:
            return
        for at, names in plan.get(place, {}).items():
            if step is None:
                for group, name in names:
                    gather.step(group, name)
            else:

                @pl.when(step == at)
                def _():
                    for group, name in names:
                        gather.step(group, name)

    segment_ids = seg_ref[seg_rows, :]
    live_flags = live_ref[seg_rows, :]
    ticks("start")
    place = lax.broadcasted_iota(jnp.int32, (LANES, LANES), 0) == lax.broadcasted_iota(
        jnp.int32, (LANES, LANES), 1
    )
    for seq in range(seqs):
        wide_ids = []
        key_ids = []
        for block in range(4):
            row = seq * 4 + block
            ids = segment_ids[row : row + 1, :].astype(WIDE)
            live = live_flags[row : row + 1, :]
            key = jnp.where(live == 1, ids, -1.0)
            wide_ids.append(ids)
            key_ids.append(jnp.transpose(jnp.broadcast_to(key, (LANES, LANES))))
        for block in range(1, 4):
            start, stop = KEY_SPANS[block]
            for j in range((stop - start) // LANES):
                kb = start // LANES + j
                seen = key_ids[kb] == wide_ids[block]
                if kb == block:
                    seen = seen | place
                at = SPAN_STARTS[block] + j * LANES
                mask[seq, at : at + LANES, :] = jnp.where(seen, 0.0, NEG_FILL)

    u_t[...] = mm_nt(down_t_ref[...], x_ref[...]).astype(NARROW)

    ticks("masked")

    for group in range(groups):
        at = slice(group * LANES, (group + 1) * LANES)
        wq[:, at] = a_ref[group, :, 0:128]
        wk[:, at] = a_ref[group, :, 128:256]
        wv[:, at] = a_ref[group, :, 256:384]
        wo[:, at] = a_ref[group, :, 640:768]
    for half in range(groups // 2):
        at = slice((groups + half) * LANES, (groups + half + 1) * LANES)
        first = a_ref[2 * half, :, 384:512].astype(WIDE)
        second = a_ref[2 * half + 1, :, 384:512].astype(WIDE)
        wq[:, at] = pair_select(first, second).astype(NARROW)
        wk[:, at] = pair_select(pltpu.roll(first, HEAD_DIM, 1), pltpu.roll(second, HEAD_DIM, 1)).astype(NARROW)
        first = a_ref[2 * half, :, 512:640].astype(WIDE)
        second = a_ref[2 * half + 1, :, 512:640].astype(WIDE)
        wv[:, at] = pair_select(first, second).astype(NARROW)
        wo[:, at] = pair_select(pltpu.roll(first, HEAD_DIM, 1), pltpu.roll(second, HEAD_DIM, 1)).astype(NARROW)

    if plan is not None:
        for i in range(len(others_t)):
            pltpu.make_async_remote_copy(
                src_ref=bias.at[me_t],
                dst_ref=bias.at[lax.rem(me_t + groups - 1 - i, groups)],
                send_sem=bias_send.at[i],
                recv_sem=bias_recv.at[i],
                device_id=(me_d, others_t[i]),
                device_id_type=BY_MESH,
            ).wait_recv()
        for group in range(groups):
            biases[2 + group : 3 + group, :] = bias[group, 0:1, :]
            biases[0:1, group * LANES : (group + 1) * LANES] = bias[group, 1:2, 0:128]
            biases[1:2, group * LANES : (group + 1) * LANES] = bias[group, 1:2, 256:384]
        for half in range(groups // 2):
            at = slice((groups + half) * LANES, (groups + half + 1) * LANES)
            for row, first in ((0, 128), (1, 384)):
                low = jnp.broadcast_to(bias[2 * half, 1:2, first : first + 128], (8, LANES))
                high = jnp.broadcast_to(bias[2 * half + 1, 1:2, first : first + 128], (8, LANES))
                biases[row : row + 1, at] = pair_select(low, high)[0:1]

    def project(step, carry):
        ticks("project", step)
        at = pl.ds(pl.multiple_of(step * 256, 256), 256)
        xs = x_ref[...]
        q[:, at] = (mm(xs, wq[:, at]) + biases[0:1, at]).astype(NARROW)
        k[:, at] = mm(xs, wk[:, at]).astype(NARROW)
        v[:, at] = (mm(xs, wv[:, at]) + biases[1:2, at]).astype(NARROW)
        return carry

    lax.fori_loop(0, width // 256, project, 0)

    lane = lax.broadcasted_iota(jnp.int32, (LANES, LANES), 1)

    def stacked(tile):
        none = jnp.zeros_like(tile)
        return jnp.concatenate(
            [jnp.where(lane < HEAD_DIM, tile, none), jnp.where(lane < HEAD_DIM, none, tile)], axis=0
        )

    def turned(tile):
        own = jnp.concatenate([tile[:HEAD_DIM, :LANES], tile[HEAD_DIM:, LANES:]], axis=0)
        return jnp.transpose(own)

    def attend(step, carry):
        ticks("attend", step)
        seq = step // pairs
        pair = step - seq * pairs
        at = pl.ds(pl.multiple_of(pair * LANES, LANES), LANES)
        base = pl.multiple_of(seq * SEQ, SEQ)
        everything = pl.ds(base, SEQ)
        keys = k[everything, at]
        values_t = jnp.transpose(v[everything, at].astype(WIDE)).astype(NARROW)
        for block, (start, stop) in enumerate(KEY_SPANS):
            here = pl.ds(base + block * LANES, LANES)
            scores = mm_nt(keys[start:stop], stacked(q[here, at]))
            span = pl.ds(SPAN_STARTS[block], stop - start)
            if block:
                shade = mask[seq, span, :]
                scores = scores + jnp.concatenate([shade, shade], axis=1)
            top = jnp.max(scores, axis=0, keepdims=True)
            powers = jnp.exp(scores - top)
            total = jnp.sum(powers, axis=0, keepdims=True)
            weights = (powers * (1.0 / total)).astype(NARROW)
            probs[step, span, :] = weights
            ctx[here, at] = turned(mm(values_t[:, start:stop], weights)).astype(NARROW)
        return carry

    lax.fori_loop(0, seqs * pairs, attend, 0)

    def first_norm(step, carry):
        ticks("first_norm", step)
        at = pl.ds(pl.multiple_of(step * 256, 256), 256)
        r = x_ref[at, :].astype(WIDE) + (mm_nt(ctx[at, :], wo[...]) + vec_ref[0:1, :])
        centered = r - row_mean(r)
        inverse = lax.rsqrt(row_mean(centered * centered) + EPSILON)
        normed = centered * inverse
        n1[at, :] = normed
        s1[at, :] = inverse
        out_ref[at, :] = (normed * vec_ref[2:3, :] + vec_ref[3:4, :]).astype(NARROW)
        return carry

    lax.fori_loop(0, rows // 256, first_norm, 0)

    def up(group, carry):
        ticks("up", group)
        for j in range(width // 256):
            cols = slice(j * 256, (j + 1) * 256)
            at = pl.ds(pl.multiple_of(group * width + j * 256, 256), 256)
            inner = mm(out_ref[...], b_ref[group, :, cols]) + biases[pl.ds(2 + group, 1), cols]
            value, grad = gelu_parts(inner)
            act[:, at] = value.astype(NARROW)
            slope[:, at] = grad.astype(NARROW)
        return carry

    ticks("before up")
    lax.fori_loop(0, groups, up, 0)
    ticks("before down")

    def second_norm(step, carry):
        at = pl.ds(pl.multiple_of(step * 256, 256), 256)
        r = n1[at, :] * vec_ref[2:3, :] + vec_ref[3:4, :] + vec_ref[1:2, :]
        for group in range(groups):
            r = r + mm_nt(act[at, group * width : (group + 1) * width], c_ref[group])
        centered = r - row_mean(r)
        inverse = lax.rsqrt(row_mean(centered * centered) + EPSILON)
        normed = centered * inverse
        out_ref[at, :] = (normed * vec_ref[4:5, :] + vec_ref[5:6, :]).astype(NARROW)
        e = gout_ref[at, :].astype(WIDE) * vec_ref[4:5, :]
        acc[at, :] = inverse * (e - row_mean(e) - normed * row_mean(e * normed))
        return carry

    lax.fori_loop(0, rows // 256, second_norm, 0)

    def down_back(step, carry):
        at = pl.ds(pl.multiple_of(step * 256, 256), 256)
        second = acc[at, :]
        low = second.astype(NARROW)
        total = second
        for group in range(groups):
            cols = slice(group * width, (group + 1) * width)
            grad = (mm(low, c_ref[group]) * slope[at, cols].astype(WIDE)).astype(NARROW)
            total = total + mm_nt(grad, b_ref[group])
        normed = n1[at, :]
        e = total * vec_ref[2:3, :]
        first = s1[at, :] * (e - row_mean(e) - normed * row_mean(e * normed))
        acc[at, :] = first
        ctx[at, :] = mm(first.astype(NARROW), wo[...]).astype(NARROW)
        return carry

    lax.fori_loop(0, rows // 256, down_back, 0)

    def attend_back(step, carry):
        seq = step // pairs
        pair = step - seq * pairs
        at = pl.ds(pl.multiple_of(pair * LANES, LANES), LANES)
        base = pl.multiple_of(seq * SEQ, SEQ)
        everything = pl.ds(base, SEQ)
        keys = k[everything, at]
        values = v[everything, at]
        keys_t = jnp.transpose(keys.astype(WIDE)).astype(NARROW)
        grad_k = [None] * 4
        grad_v = [None] * 4
        for block, (start, stop) in enumerate(KEY_SPANS):
            here = pl.ds(base + block * LANES, LANES)
            grads = stacked(ctx[here, at])
            span = pl.ds(SPAN_STARTS[block], stop - start)
            weights = probs[step, span, :]
            part = weights.astype(WIDE) * mm_nt(values[start:stop], grads)
            inside = jnp.sum(part, axis=0, keepdims=True)
            grad_scores = (part - weights.astype(WIDE) * inside).astype(NARROW)
            for_keys = mm(grad_scores, stacked(q[here, at]))
            for_values = mm(weights, grads)
            q[here, at] = turned(mm(keys_t[:, start:stop], grad_scores)).astype(NARROW)
            for j in range((stop - start) // LANES):
                kb = start // LANES + j
                rows_here = slice(j * LANES, (j + 1) * LANES)
                grad_k[kb] = for_keys[rows_here] if grad_k[kb] is None else grad_k[kb] + for_keys[rows_here]
                grad_v[kb] = (
                    for_values[rows_here] if grad_v[kb] is None else grad_v[kb] + for_values[rows_here]
                )
        for kb in range(4):
            here = pl.ds(base + kb * LANES, LANES)
            k[here, at] = grad_k[kb].astype(NARROW)
            v[here, at] = grad_v[kb].astype(NARROW)
        return carry

    lax.fori_loop(0, seqs * pairs, attend_back, 0)

    grad_q = mm(u_t[0:8, :], q[...]) * (ADAPTER_SCALE * SCORE_SCALE)
    grad_v = mm(u_t[8:16, :], v[...]) * ADAPTER_SCALE

    def input_back(step, carry):
        at = pl.ds(pl.multiple_of(step * 256, 256), 256)
        total = acc[at, :] + mm_nt(q[at, :], wq[...])
        total = total + mm_nt(k[at, :], wk[...])
        total = total + mm_nt(v[at, :], wv[...])
        gin_ref[at, :] = total.astype(NARROW)
        return carry

    if plan is None:
        gl_ref[0:8, :] = grad_q
        gl_ref[8:16, :] = grad_v
        lax.fori_loop(0, rows // 256, input_back, 0)
        return

    for group in range(groups):
        for row, grad in ((0, grad_q), (8, grad_v)):
            part[group, row : row + 8, 0:128] = grad[:, group * LANES : (group + 1) * LANES]
            other = groups + group // 2
            part[group, row : row + 8, 128:256] = grad[:, other * LANES : (other + 1) * LANES]

    def near_copy(i, slot):
        return pltpu.make_async_remote_copy(
            src_ref=part.at[others_t[i]],
            dst_ref=near.at[slot],
            send_sem=near_send.at[i],
            recv_sem=near_recv.at[i],
            device_id=(me_d, others_t[i]),
            device_id_type=BY_MESH,
        )

    def far_copy(i, slot):
        return pltpu.make_async_remote_copy(
            src_ref=far.at[me_d],
            dst_ref=far.at[slot],
            send_sem=far_send.at[i],
            recv_sem=far_recv.at[i],
            device_id=(others_d[i], me_t),
            device_id_type=BY_MESH,
        )

    for i in range(len(others_t)):
        near_copy(i, i).start()
    lax.fori_loop(0, rows // 512, input_back, 0)
    total = part[me_t]
    for i in range(len(others_t)):
        near_copy(i, i).wait_recv()
        total = total + near[i]
    far[me_d] = total
    for i in range(len(others_d)):
        far_copy(i, me_d).start()
    lax.fori_loop(rows // 512, rows // 256, input_back, 0)
    for group in range(3):
        gather.finish(group)
    for i in range(len(others_t)):
        bias_copy(i).wait_send()
        near_copy(i, i).wait_send()
    for i in range(len(others_d)):
        far_copy(i, lax.rem(me_d + dps - 1 - i, dps)).wait_recv()
    total = far[0]
    for i in range(1, dps):
        total = total + far[i]
    last = jnp.where(lax.rem(me_t, 2) == 0, total[:, 128:], pltpu.roll(total[:, 128:], HEAD_DIM, 1))
    glq_ref[:, 0:128] = total[0:8, 0:128]
    glv_ref[:, 0:128] = total[8:16, 0:128]
    glq_ref[:, 128:192] = last[0:8, 0:HEAD_DIM]
    glv_ref[:, 128:192] = last[8:16, 0:HEAD_DIM]
    for i in range(len(others_d)):
        far_copy(i, me_d).wait_send()


def scratch(rows, width, hidden):
    pairs = width // LANES
    seqs = rows // SEQ
    square = pltpu.VMEM((width, width), NARROW)
    plane = pltpu.VMEM((rows, width), NARROW)
    return [
        square,
        square,
        square,
        square,
        plane,
        plane,
        plane,
        pltpu.VMEM((seqs * pairs, SPAN_TOTAL, 2 * LANES), NARROW),
        plane,
        pltpu.VMEM((rows, width), WIDE),
        pltpu.VMEM((rows, 1), WIDE),
        pltpu.VMEM((rows, hidden), NARROW),
        pltpu.VMEM((rows, hidden), NARROW),
        pltpu.VMEM((rows, width), WIDE),
        pltpu.VMEM((seqs, SPAN_TOTAL, LANES), WIDE),
        pltpu.VMEM((2 * ADAPTER_RANK, rows), NARROW),
    ]


def run_layer(x, gout, a, b, c, biases, vectors, down_t, seg, live):
    rows, width = x.shape
    shape = jax.ShapeDtypeStruct
    hidden = b.shape[0] * b.shape[2]
    return pl.pallas_call(
        functools.partial(kernel, None),
        out_shape=(
            shape((rows, width), NARROW),
            shape((rows, width), NARROW),
            shape((2 * ADAPTER_RANK, width), WIDE),
        ),
        in_specs=[pl.BlockSpec(memory_space=pltpu.VMEM)] * 10,
        out_specs=[pl.BlockSpec(memory_space=pltpu.VMEM)] * 3,
        scratch_shapes=scratch(rows, width, hidden) + [pltpu.VMEM((8, width), WIDE)],
        compiler_params=pltpu.CompilerParams(vmem_limit_bytes=63 << 20),
    )(x, gout, a, b, c, biases, vectors, down_t, seg, live)


def run_layer_and_gather(x, gout, blocks, adapters, biases, vectors, down_t, seg, live):
    rows, width = x.shape
    groups = width // blocks[0].shape[1]
    dps = width // blocks[0].shape[0]
    shape = jax.ShapeDtypeStruct
    gathered = pltpu.VMEM((groups, width, width), NARROW)
    signals = pltpu.SemaphoreType.DMA
    operands = (x, gout, *blocks, *adapters, *biases, vectors, down_t, seg, live)
    return pl.pallas_call(
        functools.partial(kernel, PLAN),
        out_shape=(
            shape((rows, width), NARROW),
            shape((rows, width), NARROW),
            shape((ADAPTER_RANK, width // groups), WIDE),
            shape((ADAPTER_RANK, width // groups), WIDE),
        ),
        in_specs=[pl.BlockSpec(memory_space=pltpu.VMEM)] * len(operands),
        out_specs=[pl.BlockSpec(memory_space=pltpu.VMEM)] * 4,
        scratch_shapes=scratch(rows, width, groups * width)
        + [
            gathered,
            gathered,
            gathered,
            pltpu.VMEM((groups, 8, width), WIDE),
            pltpu.VMEM((8, width), WIDE),
            pltpu.VMEM((groups, 2 * ADAPTER_RANK, 2 * LANES), WIDE),
            pltpu.VMEM((groups - 1, 2 * ADAPTER_RANK, 2 * LANES), WIDE),
            pltpu.VMEM((dps, 2 * ADAPTER_RANK, 2 * LANES), WIDE),
            signals((3, len(SIGNALS))),
            signals((3, len(SIGNALS))),
            signals((groups - 1,)),
            signals((groups - 1,)),
            signals((groups - 1,)),
            signals((groups - 1,)),
            signals((dps - 1,)),
            signals((dps - 1,)),
        ],
        compiler_params=pltpu.CompilerParams(
            collective_id=0, has_side_effects=True, vmem_limit_bytes=63 << 20
        ),
    )(*operands)


def in_pairs(block, groups):
    parts = block.reshape(block.shape[0], groups, 3, HEAD_DIM)
    front = parts[:, :, :2].reshape(block.shape[0], -1)
    return jnp.concatenate([front, parts[:, :, 2].reshape(block.shape[0], -1)], axis=1)


def from_pairs(block, groups):
    front = block[:, : groups * LANES].reshape(block.shape[0], groups, 2, HEAD_DIM)
    back = block[:, groups * LANES :].reshape(block.shape[0], groups, 1, HEAD_DIM)
    return jnp.concatenate([front, back], axis=2).reshape(block.shape[0], -1)


def body(
    grid,
    layer_input_rows,
    output_gradient,
    query_weight,
    key_weight,
    value_weight,
    output_weight,
    up_weight,
    down_weight,
    query_bias_vector,
    value_bias_vector,
    output_bias_vector,
    up_bias_vector,
    down_bias_vector,
    query_down_frozen,
    value_down_frozen,
    query_up_trained,
    value_up_trained,
    first_norm_gain,
    first_norm_bias,
    second_norm_gain,
    second_norm_bias,
    segments,
    sentence_row_mask,
):
    everyone = ("tensor", "dp")
    rows, width = layer_input_rows.shape
    depth, across = query_weight.shape
    groups = width // across
    vectors = jnp.stack(
        [
            output_bias_vector,
            down_bias_vector,
            first_norm_gain,
            first_norm_bias,
            second_norm_gain,
            second_norm_bias,
        ]
    )
    down_t = jnp.concatenate([query_down_frozen, value_down_frozen], axis=1).T
    segment_rows = segments.reshape(-1, LANES)
    live_rows = sentence_row_mask.reshape(-1, LANES)
    if grid == (8, 4):
        return run_layer_and_gather(
            layer_input_rows,
            output_gradient,
            (query_weight, key_weight, value_weight, output_weight, up_weight, down_weight),
            (query_down_frozen, value_down_frozen, query_up_trained, value_up_trained),
            (query_bias_vector[None], value_bias_vector[None], up_bias_vector[None]),
            vectors,
            down_t,
            segment_rows,
            live_rows,
        )

    place = lax.axis_index("tensor")
    which = lax.axis_index("dp")

    def folded(weight, down, up):
        own = lax.dynamic_slice_in_dim(down, which * depth, depth, axis=0)
        return weight.astype(WIDE) + ADAPTER_SCALE * mm(own, up)

    wq = (folded(query_weight, query_down_frozen, query_up_trained) * SCORE_SCALE).astype(NARROW)
    wv = folded(value_weight, value_down_frozen, value_up_trained).astype(NARROW)
    wk = key_weight
    wo = output_weight.T
    block_a = jnp.concatenate(
        [wq[:, :128], wk[:, :128], wv[:, :128], wq[:, 128:], wk[:, 128:], wv[:, 128:], wo[:, 128:], wo[:, :128]],
        axis=1,
    )

    def spread(block):
        return lax.all_gather(block, everyone, axis=0, tiled=True).reshape(groups, width, width)

    a, b, c = spread(block_a), spread(up_weight), spread(down_weight.T)
    query_bias = lax.all_gather(query_bias_vector * SCORE_SCALE, "tensor", axis=0, tiled=True)
    value_bias = lax.all_gather(value_bias_vector, "tensor", axis=0, tiled=True)
    up_bias = lax.all_gather(up_bias_vector, "tensor", axis=0, tiled=True)
    biases = jnp.concatenate(
        [
            in_pairs(query_bias[None], groups),
            in_pairs(value_bias[None], groups),
            up_bias.reshape(groups, width),
            jnp.zeros((6 - groups, width), WIDE),
        ],
        axis=0,
    )
    blocks = rows // LANES
    seg = lax.dynamic_slice_in_dim(segment_rows, place * blocks, blocks)
    live = lax.dynamic_slice_in_dim(live_rows, place * blocks, blocks)
    output, grad_input, grads = run_layer(
        layer_input_rows, output_gradient, a, b, c, biases, vectors, down_t, seg, live
    )
    grads = from_pairs(lax.psum(grads, everyone), groups)
    grads = lax.dynamic_slice_in_dim(grads, place * across, across, axis=1)
    return output, grad_input, grads[:ADAPTER_RANK], grads[ADAPTER_RANK:]


IN_SPECS = (
    P(("dp", "tensor"), None),
    P(("dp", "tensor"), None),
    P("dp", "tensor"),
    P("dp", "tensor"),
    P("dp", "tensor"),
    P("tensor", "dp"),
    P("dp", "tensor"),
    P("tensor", "dp"),
    P("tensor"),
    P("tensor"),
    P(),
    P("tensor"),
    P(),
    P(),
    P(),
    P(None, "tensor"),
    P(None, "tensor"),
    P(),
    P(),
    P(),
    P(),
    P("dp"),
    P("dp"),
)
OUT_SPECS = (
    P(("dp", "tensor"), None),
    P(("dp", "tensor"), None),
    P(None, "tensor"),
    P(None, "tensor"),
)


def solution(mesh):
    grid = (mesh.shape["dp"], mesh.shape["tensor"])
    layer = functools.partial(body, grid)
    return jax.shard_map(layer, mesh=mesh, in_specs=IN_SPECS, out_specs=OUT_SPECS, check_vma=False)
```

```python
import functools

import jax
import jax.numpy as jnp
from jax import lax
from jax.experimental import pallas as pl
from jax.experimental.pallas import tpu as pltpu
from jax.sharding import PartitionSpec as P

HEAD_DIM = 64
ADAPTER_RANK = 8
ADAPTER_NUMER = 16
SEQ = 512
LANES = 128
EPSILON = 1e-05
NEG_FILL = -1e30
WIDE = jnp.float32
NARROW = jnp.bfloat16
ADAPTER_SCALE = ADAPTER_NUMER / ADAPTER_RANK
SCORE_SCALE = HEAD_DIM**-0.5

KEY_SPANS = ((0, 128), (128, 384), (128, 512), (256, 512))
SPAN_STARTS = (0, 128, 384, 768)
SPAN_TOTAL = 1024
BY_MESH = pl.DeviceIdType.MESH

ARRIVALS = (
    ("Z1", "Z2", "Z3", "X0", "X1", "X2", "X3", "Y0", "Y1", "Y2", "Y3")
    + ("D0a", "D0b", "D1", "D2a", "D2b", "D3", "C")
    + tuple("C" + kind + str(k) for kind in "ZXYD" for k in range(4) if kind + str(k) != "Z0")
)
SIGNALS = {name: i for i, name in enumerate(ARRIVALS + ("Z2down",))}
PASS_ON = {
    "own": (("X0", "x", ""), ("Y0", "y", ""), ("Z1", "up", ""), ("Z3", "down", ""), ("C", "core", "")),
    "X0": (("X1", "up", ""), ("D0b", "y", "b"), ("CX0", "core", "")),
    "Y0": (("Y3", "down", ""), ("D0a", "x", "a"), ("CY0", "core", "")),
    "Z1": (("Y1", "y", ""), ("CZ1", "core", "")),
    "Z3": (("X3", "x", ""), ("CZ3", "core", "")),
    "X1": (("CX1", "core", ""),),
    "Y3": (("CY3", "core", ""),),
    "Z2": (("X2", "x", ""), ("Y2", "y", ""), ("CZ2", "core", "")),
    "Y1": (("D1", "x", ""), ("CY1", "core", "")),
    "X3": (("D3", "y", ""), ("CX3", "core", "")),
    "X2": (("D2b", "y", "b"), ("CX2", "core", "")),
    "Y2": (("D2a", "x", "a"), ("CY2", "core", "")),
    "D0b": (("CD0", "core", ""),),
    "D1": (("CD1", "core", ""),),
    "D2b": (("CD2", "core", ""),),
    "D3": (("CD3", "core", ""),),
}
ROUNDS = (
    ("own",),
    ("X0", "Y0", "Z1", "Z3"),
    ("X1", "Y3", "Z2", "Y1", "X3"),
    ("X2", "Y2", "D0a", "D0b", "D1", "D3"),
    ("D2a", "D2b"),
    tuple(name for name in ARRIVALS if name[0] == "C"),
)


def in_rounds(*rounds):
    return [(group, name) for number, group in rounds for name in ROUNDS[number]]


PLAN = {
    "start": {0: in_rounds((1, 0), (0, 1), (2, 0), (1, 1), (3, 0), (0, 2), (4, 0), (5, 0))},
    "project": {0: in_rounds((2, 1)), 1: in_rounds((1, 2)), 2: in_rounds((3, 1))},
    "attend": {0: in_rounds((2, 2)), 1: in_rounds((4, 1), (3, 2)), 2: in_rounds((4, 2))},
    "before up": {0: in_rounds((5, 1))},
    "before down": {0: in_rounds((5, 2))},
}


class Gather:
    def __init__(self, blocks, send, recv):
        self.blocks, self.send, self.recv = blocks, send, recv
        self.d, self.t = lax.axis_index("dp"), lax.axis_index("tensor")
        self.depth = blocks[0].shape[1] // 8
        self.z, self.y = self.d // 2, lax.rem(self.d, 2)
        self.tx = lax.rem(self.t + 2, 4)
        self.tc = self.t + 1 - 2 * lax.rem(self.t, 2)
        self.txc = lax.rem(self.tc + 2, 4)
        self.middle = (self.z == 1) | (self.z == 2)

    def peer(self, kind):
        return {
            "x": (self.d, self.tx),
            "y": (self.z * 2 + 1 - self.y, self.t),
            "core": (self.d, self.tc),
            "up": (lax.rem(self.z + 1, 4) * 2 + self.y, self.t),
            "down": (lax.rem(self.z + 3, 4) * 2 + self.y, self.t),
        }[kind]

    def part(self, group, name, half=""):
        if name == "own":
            dp, t = self.d, self.t
        elif name == "C":
            dp, t = self.d, self.tc
        else:
            kind = name[-2] if name[-1].isdigit() else name[-3]
            k = int(name[-1] if name[-1].isdigit() else name[-2])
            half = half or (name[-1] if not name[-1].isdigit() else "")
            near, far = (self.tc, self.txc) if name[0] == "C" else (self.t, self.tx)
            dp = lax.rem(self.z - k + 4, 4) * 2 + (self.y if kind in "ZX" else 1 - self.y)
            t = near if kind in "ZY" else far
        size = self.depth // 2 if half else self.depth
        first = dp * self.depth + (size if half == "b" else 0)
        return self.blocks[group].at[t, pl.ds(pl.multiple_of(first, 16), size), :]

    def copy(self, group, part, name, to, sender=None):
        return pltpu.make_async_remote_copy(
            src_ref=part,
            dst_ref=part,
            send_sem=self.send.at[group, SIGNALS[sender or name]],
            recv_sem=self.recv.at[group, SIGNALS[name]],
            device_id=self.peer(to),
            device_id_type=BY_MESH,
        )

    def outgoing(self, group, name):
        whole = name[:2] if name[0] == "D" else name
        return [
            self.copy(group, self.part(group, whole, half), out, to)
            for out, to, half in PASS_ON.get(name, ())
        ]

    def relayed(self, group, name):
        to, sender = ("up", "Z2") if name == "Z1" else ("down", "Z2down")
        return self.copy(group, self.part(group, name), "Z2", to, sender)

    def step(self, group, name):
        if name != "own":
            self.copy(group, self.part(group, name), name, "x").wait_recv()
        for copy in self.outgoing(group, name):
            copy.start()
        if name in ("Z1", "Z3"):

            @pl.when(self.middle)
            def _():
                self.relayed(group, name).start()

    def finish(self, group):
        for name in PASS_ON:
            for copy in self.outgoing(group, name):
                copy.wait_send()

        @pl.when(self.middle)
        def _():
            self.relayed(group, "Z1").wait_send()
            self.relayed(group, "Z3").wait_send()


def mm(left, right):
    return jnp.dot(left, right, preferred_element_type=WIDE)


def mm_nt(left, right):
    return lax.dot_general(left, right, (((1,), (1,)), ((), ())), preferred_element_type=WIDE)


def mm_tn(left, right):
    return lax.dot_general(left, right, (((0,), (0,)), ((), ())), preferred_element_type=WIDE)


def row_mean(block):
    return jnp.sum(block, axis=-1, keepdims=True) * (1.0 / block.shape[-1])


def gelu_parts(value):
    below = 0.5 + 0.5 * lax.erf(value * 0.7071067811865476)
    bell = jnp.exp(value * value * -0.5) * 0.3989422804014327
    return value * below, below + value * bell


def pair_select(low, high):
    lane = lax.broadcasted_iota(jnp.int32, low.shape, 1)
    return jnp.where(lane < HEAD_DIM, low, pltpu.roll(high, HEAD_DIM, 1))


def kernel(plan, *refs):
    if plan is not None:
        (x_ref, gout_ref, wq_ref, wk_ref, wv_ref, wo_ref, up_ref, down_ref, dq_ref, dv_ref, uq_ref, uv_ref) = refs[:12]
        (bq_ref, bv_ref, bup_ref) = refs[12:15]
        vector_refs, (seg_ref, live_ref) = refs[15:21], refs[21:23]
        (out_ref, gin_ref, glq_ref, glv_ref) = refs[23:27]
        (wq, wk, wv, wo, q, k, v, probs, ctx, n1, s1, act, slope, acc, mask, u_t) = refs[27:43]
        (a_ref, b_ref, c_ref, bias, biases, part, near, far) = refs[43:51]
        (send, recv, bias_send, bias_recv, near_send, near_recv, far_send, far_recv) = refs[51:]
    else:
        (x_ref, gout_ref, a_ref, b_ref, c_ref, biases_ref, dq_ref, dv_ref) = refs[:8]
        vector_refs, (seg_ref, live_ref) = refs[8:14], refs[14:16]
        (out_ref, gin_ref, gl_ref) = refs[16:19]
        (wq, wk, wv, wo, q, k, v, probs, ctx, n1, s1, act, slope, acc, mask, u_t, biases) = refs[19:]
    rows, width = x_ref.shape
    seqs = rows // SEQ
    pairs = width // LANES
    groups = a_ref.shape[0]
    out_bias, down_bias, gain1, shift1, gain2, shift2 = (
        jnp.reshape(ref[...], (1, width)) for ref in vector_refs
    )

    if plan is not None:
        gather = Gather((a_ref, b_ref, c_ref), send, recv)
        me_d, me_t = gather.d, gather.t
        dps = width // wq_ref.shape[0]
        depth = wq_ref.shape[0]
        others_t = [lax.rem(me_t + i, groups) for i in range(1, groups)]
        others_d = [lax.rem(me_d + i, dps) for i in range(1, dps)]
        seg_rows = pl.ds(pl.multiple_of(me_t * (rows // LANES), rows // LANES), rows // LANES)
        barrier = pltpu.get_barrier_semaphore()
        for other in others_t:
            pl.semaphore_signal(barrier, inc=1, device_id=(me_d, other), device_id_type=BY_MESH)
        for other in others_d:
            pl.semaphore_signal(barrier, inc=1, device_id=(other, me_t), device_id_type=BY_MESH)

        mine = pl.ds(pl.multiple_of(me_d * depth, depth), depth)
        across = wq_ref.shape[1]
        acc[0:width, 0:across] = mm_tn(dq_ref[...], uq_ref[...])
        acc[0:width, 256 : 256 + across] = mm_tn(dv_ref[...], uv_ref[...])
        query = (wq_ref[...].astype(WIDE) + ADAPTER_SCALE * acc[mine, 0:across]) * SCORE_SCALE
        value = wv_ref[...].astype(WIDE) + ADAPTER_SCALE * acc[mine, 256 : 256 + across]
        key = wk_ref[...].astype(WIDE)
        out_t = jnp.transpose(wo_ref[...].astype(WIDE))
        a_ref[me_t, mine, 0:128] = query[:, 0:128].astype(NARROW)
        a_ref[me_t, mine, 128:256] = key[:, 0:128].astype(NARROW)
        a_ref[me_t, mine, 256:384] = value[:, 0:128].astype(NARROW)
        a_ref[me_t, mine, 384:512] = jnp.concatenate([query[:, 128:], key[:, 128:]], axis=1).astype(NARROW)
        a_ref[me_t, mine, 512:640] = jnp.concatenate([value[:, 128:], out_t[:, 128:]], axis=1).astype(NARROW)
        a_ref[me_t, mine, 640:768] = out_t[:, 0:128].astype(NARROW)
        bias[me_t, 0:1, :] = jnp.reshape(bup_ref[...], (1, width))
        bias[me_t, 1:2, 0:across] = jnp.reshape(bq_ref[...], (1, across)) * SCORE_SCALE
        bias[me_t, 1:2, 256 : 256 + across] = jnp.reshape(bv_ref[...], (1, across))
        pl.semaphore_wait(barrier, len(others_t) + len(others_d))

        def bias_copy(i):
            return pltpu.make_async_remote_copy(
                src_ref=bias.at[me_t],
                dst_ref=bias.at[me_t],
                send_sem=bias_send.at[i],
                recv_sem=bias_recv.at[i],
                device_id=(me_d, others_t[i]),
                device_id_type=BY_MESH,
            )

        for name in ("own",):
            gather.step(0, name)
        b_ref[me_t, mine, :] = up_ref[...]
        c_ref[me_t, mine, :] = down_ref[...]
        for i in range(len(others_t)):
            bias_copy(i).start()
    else:
        seg_rows = pl.ds(0, rows // LANES)
        biases[...] = biases_ref[...]

    def ticks(place, step=None):
        if plan is None:
            return
        for at, names in plan.get(place, {}).items():
            if step is None:
                for group, name in names:
                    gather.step(group, name)
            else:

                @pl.when(step == at)
                def _():
                    for group, name in names:
                        gather.step(group, name)

    segment_ids = seg_ref[seg_rows, :]
    live_flags = live_ref[seg_rows, :]
    ticks("start")
    place = lax.broadcasted_iota(jnp.int32, (LANES, LANES), 0) == lax.broadcasted_iota(
        jnp.int32, (LANES, LANES), 1
    )
    for seq in range(seqs):
        wide_ids = []
        key_ids = []
        for block in range(4):
            row = seq * 4 + block
            ids = segment_ids[row : row + 1, :].astype(WIDE)
            live = live_flags[row : row + 1, :]
            key = jnp.where(live == 1, ids, -1.0)
            wide_ids.append(ids)
            key_ids.append(jnp.transpose(jnp.broadcast_to(key, (LANES, LANES))))
        for block in range(1, 4):
            start, stop = KEY_SPANS[block]
            for j in range((stop - start) // LANES):
                kb = start // LANES + j
                seen = key_ids[kb] == wide_ids[block]
                if kb == block:
                    seen = seen | place
                at = SPAN_STARTS[block] + j * LANES
                mask[seq, at : at + LANES, :] = jnp.where(seen, 0.0, NEG_FILL)

    adapters_down = jnp.concatenate([dq_ref[...].astype(WIDE), dv_ref[...].astype(WIDE)], axis=0)
    u_t[...] = mm_nt(adapters_down.astype(NARROW), x_ref[...]).astype(NARROW)

    ticks("masked")

    for group in range(groups):
        at = slice(group * LANES, (group + 1) * LANES)
        wq[:, at] = a_ref[group, :, 0:128]
        wk[:, at] = a_ref[group, :, 128:256]
        wv[:, at] = a_ref[group, :, 256:384]
        wo[:, at] = a_ref[group, :, 640:768]
    for half in range(groups // 2):
        at = slice((groups + half) * LANES, (groups + half + 1) * LANES)
        first = a_ref[2 * half, :, 384:512].astype(WIDE)
        second = a_ref[2 * half + 1, :, 384:512].astype(WIDE)
        wq[:, at] = pair_select(first, second).astype(NARROW)
        wk[:, at] = pair_select(pltpu.roll(first, HEAD_DIM, 1), pltpu.roll(second, HEAD_DIM, 1)).astype(NARROW)
        first = a_ref[2 * half, :, 512:640].astype(WIDE)
        second = a_ref[2 * half + 1, :, 512:640].astype(WIDE)
        wv[:, at] = pair_select(first, second).astype(NARROW)
        wo[:, at] = pair_select(pltpu.roll(first, HEAD_DIM, 1), pltpu.roll(second, HEAD_DIM, 1)).astype(NARROW)

    if plan is not None:
        for i in range(len(others_t)):
            pltpu.make_async_remote_copy(
                src_ref=bias.at[me_t],
                dst_ref=bias.at[lax.rem(me_t + groups - 1 - i, groups)],
                send_sem=bias_send.at[i],
                recv_sem=bias_recv.at[i],
                device_id=(me_d, others_t[i]),
                device_id_type=BY_MESH,
            ).wait_recv()
        for group in range(groups):
            biases[2 + group : 3 + group, :] = bias[group, 0:1, :]
            biases[0:1, group * LANES : (group + 1) * LANES] = bias[group, 1:2, 0:128]
            biases[1:2, group * LANES : (group + 1) * LANES] = bias[group, 1:2, 256:384]
        for half in range(groups // 2):
            at = slice((groups + half) * LANES, (groups + half + 1) * LANES)
            for row, first in ((0, 128), (1, 384)):
                low = jnp.broadcast_to(bias[2 * half, 1:2, first : first + 128], (8, LANES))
                high = jnp.broadcast_to(bias[2 * half + 1, 1:2, first : first + 128], (8, LANES))
                biases[row : row + 1, at] = pair_select(low, high)[0:1]

    def project(step, carry):
        ticks("project", step)
        at = pl.ds(pl.multiple_of(step * 256, 256), 256)
        xs = x_ref[...]
        q[:, at] = (mm(xs, wq[:, at]) + biases[0:1, at]).astype(NARROW)
        k[:, at] = mm(xs, wk[:, at]).astype(NARROW)
        v[:, at] = (mm(xs, wv[:, at]) + biases[1:2, at]).astype(NARROW)
        return carry

    lax.fori_loop(0, width // 256, project, 0)

    lane = lax.broadcasted_iota(jnp.int32, (LANES, LANES), 1)
    together = 3
    steps = seqs * pairs // together

    def stacked(tile):
        none = jnp.zeros_like(tile)
        return jnp.concatenate(
            [jnp.where(lane < HEAD_DIM, tile, none), jnp.where(lane < HEAD_DIM, none, tile)], axis=0
        )

    def merged(tile):
        return jnp.where(lane < HEAD_DIM, tile[:LANES], tile[LANES:]).astype(NARROW)

    def work_of(step):
        items = []
        for one in range(together):
            index = step * together + one
            seq = index // pairs
            base = pl.multiple_of(seq * SEQ, SEQ)
            at = pl.ds(pl.multiple_of((index - seq * pairs) * LANES, LANES), LANES)
            for block, (start, stop) in enumerate(KEY_SPANS):
                here = pl.ds(base + block * LANES, LANES)
                there = pl.ds(base + start, stop - start)
                span = pl.ds(SPAN_STARTS[block], stop - start)
                items.append((index, seq, here, there, at, span, block))
        return items

    def attend(step, carry):
        ticks("attend", step)
        items = work_of(step)
        scores = [mm_nt(k[there, at], stacked(q[here, at])) for _, _, here, there, at, _, _ in items]
        weights = []
        for (index, seq, _, _, _, span, block), score in zip(items, scores):
            if block:
                shade = mask[seq, span, :]
                score = score + jnp.concatenate([shade, shade], axis=1)
            powers = jnp.exp(score - jnp.max(score, axis=0, keepdims=True))
            total = jnp.sum(powers, axis=0, keepdims=True)
            weights.append((powers * (1.0 / total)).astype(NARROW))
            probs[index, span, :] = weights[-1]
        for (_, _, here, there, at, _, _), weight in zip(items, weights):
            ctx[here, at] = merged(mm_tn(weight, v[there, at]))
        return carry

    lax.fori_loop(0, steps, attend, 0)

    def first_norm(step, carry):
        ticks("first_norm", step)
        at = pl.ds(pl.multiple_of(step * 256, 256), 256)
        r = x_ref[at, :].astype(WIDE) + (mm_nt(ctx[at, :], wo[...]) + out_bias)
        centered = r - row_mean(r)
        inverse = lax.rsqrt(row_mean(centered * centered) + EPSILON)
        normed = centered * inverse
        n1[at, :] = normed
        s1[at, :] = inverse
        out_ref[at, :] = (normed * gain1 + shift1).astype(NARROW)
        return carry

    lax.fori_loop(0, rows // 256, first_norm, 0)

    def up(group, carry):
        ticks("up", group)
        for j in range(width // 256):
            cols = slice(j * 256, (j + 1) * 256)
            at = pl.ds(pl.multiple_of(group * width + j * 256, 256), 256)
            inner = mm(out_ref[...], b_ref[group, :, cols]) + biases[pl.ds(2 + group, 1), cols]
            value, grad = gelu_parts(inner)
            act[:, at] = value.astype(NARROW)
            slope[:, at] = grad.astype(NARROW)
        return carry

    ticks("before up")
    lax.fori_loop(0, groups, up, 0)
    ticks("before down")

    def second_norm(step, carry):
        at = pl.ds(pl.multiple_of(step * 256, 256), 256)
        r = n1[at, :] * gain1 + shift1 + down_bias
        for group in range(groups):
            r = r + mm_nt(act[at, group * width : (group + 1) * width], c_ref[group])
        centered = r - row_mean(r)
        inverse = lax.rsqrt(row_mean(centered * centered) + EPSILON)
        normed = centered * inverse
        out_ref[at, :] = (normed * gain2 + shift2).astype(NARROW)
        e = gout_ref[at, :].astype(WIDE) * gain2
        acc[at, :] = inverse * (e - row_mean(e) - normed * row_mean(e * normed))
        return carry

    lax.fori_loop(0, rows // 256, second_norm, 0)

    def down_back(step, carry):
        at = pl.ds(pl.multiple_of(step * 256, 256), 256)
        second = acc[at, :]
        low = second.astype(NARROW)
        total = second
        for group in range(groups):
            cols = slice(group * width, (group + 1) * width)
            grad = (mm(low, c_ref[group]) * slope[at, cols].astype(WIDE)).astype(NARROW)
            total = total + mm_nt(grad, b_ref[group])
        normed = n1[at, :]
        e = total * gain1
        first = s1[at, :] * (e - row_mean(e) - normed * row_mean(e * normed))
        acc[at, :] = first
        ctx[at, :] = mm(first.astype(NARROW), wo[...]).astype(NARROW)
        return carry

    lax.fori_loop(0, rows // 256, down_back, 0)

    def attend_back(step, carry):
        items = work_of(step)
        grad_q, grad_k, grad_v = [], {}, {}
        for index, seq, here, there, at, span, block in items:
            grads = stacked(ctx[here, at])
            weights = probs[index, span, :]
            part = weights.astype(WIDE) * mm_nt(v[there, at], grads)
            inside = jnp.sum(part, axis=0, keepdims=True)
            grad_scores = (part - weights.astype(WIDE) * inside).astype(NARROW)
            grad_q.append(merged(mm_tn(grad_scores, k[there, at])))
            for_keys = mm(grad_scores, stacked(q[here, at]))
            for_values = mm(weights, grads)
            start, stop = KEY_SPANS[block]
            for j in range((stop - start) // LANES):
                rows_here = slice(j * LANES, (j + 1) * LANES)
                key = (len(grad_q) - 1) // 4, start // LANES + j
                for grad, more in ((grad_k, for_keys), (grad_v, for_values)):
                    grad[key] = grad[key] + more[rows_here] if key in grad else more[rows_here]
        for (_, _, here, _, at, _, _), grad in zip(items, grad_q):
            q[here, at] = grad
        for one, kb in grad_k:
            _, _, here, _, at, _, _ = items[4 * one + kb]
            k[here, at] = grad_k[one, kb].astype(NARROW)
            v[here, at] = grad_v[one, kb].astype(NARROW)
        return carry

    lax.fori_loop(0, steps, attend_back, 0)

    grad_q = mm(u_t[0:8, :], q[...]) * (ADAPTER_SCALE * SCORE_SCALE)
    grad_v = mm(u_t[8:16, :], v[...]) * ADAPTER_SCALE

    def input_back(step, carry):
        at = pl.ds(pl.multiple_of(step * 256, 256), 256)
        total = acc[at, :] + mm_nt(q[at, :], wq[...])
        total = total + mm_nt(k[at, :], wk[...])
        total = total + mm_nt(v[at, :], wv[...])
        gin_ref[at, :] = total.astype(NARROW)
        return carry

    if plan is None:
        gl_ref[0:8, :] = grad_q
        gl_ref[8:16, :] = grad_v
        lax.fori_loop(0, rows // 256, input_back, 0)
        return

    for group in range(groups):
        for row, grad in ((0, grad_q), (8, grad_v)):
            part[group, row : row + 8, 0:128] = grad[:, group * LANES : (group + 1) * LANES]
            other = groups + group // 2
            part[group, row : row + 8, 128:256] = grad[:, other * LANES : (other + 1) * LANES]

    def near_copy(i, slot):
        return pltpu.make_async_remote_copy(
            src_ref=part.at[others_t[i]],
            dst_ref=near.at[slot],
            send_sem=near_send.at[i],
            recv_sem=near_recv.at[i],
            device_id=(me_d, others_t[i]),
            device_id_type=BY_MESH,
        )

    def far_copy(i, slot):
        return pltpu.make_async_remote_copy(
            src_ref=far.at[me_d],
            dst_ref=far.at[slot],
            send_sem=far_send.at[i],
            recv_sem=far_recv.at[i],
            device_id=(others_d[i], me_t),
            device_id_type=BY_MESH,
        )

    for i in range(len(others_t)):
        near_copy(i, i).start()
    lax.fori_loop(0, rows // 512, input_back, 0)
    total = part[me_t]
    for i in range(len(others_t)):
        near_copy(i, i).wait_recv()
        total = total + near[i]
    far[me_d] = total
    for i in range(len(others_d)):
        far_copy(i, me_d).start()
    lax.fori_loop(rows // 512, rows // 256, input_back, 0)
    for group in range(3):
        gather.finish(group)
    for i in range(len(others_t)):
        bias_copy(i).wait_send()
        near_copy(i, i).wait_send()
    for i in range(len(others_d)):
        far_copy(i, lax.rem(me_d + dps - 1 - i, dps)).wait_recv()
    total = far[0]
    for i in range(1, dps):
        total = total + far[i]
    last = jnp.where(lax.rem(me_t, 2) == 0, total[:, 128:], pltpu.roll(total[:, 128:], HEAD_DIM, 1))
    glq_ref[:, 0:128] = total[0:8, 0:128]
    glv_ref[:, 0:128] = total[8:16, 0:128]
    glq_ref[:, 128:192] = last[0:8, 0:HEAD_DIM]
    glv_ref[:, 128:192] = last[8:16, 0:HEAD_DIM]
    for i in range(len(others_d)):
        far_copy(i, me_d).wait_send()


def scratch(rows, width, hidden):
    pairs = width // LANES
    seqs = rows // SEQ
    square = pltpu.VMEM((width, width), NARROW)
    plane = pltpu.VMEM((rows, width), NARROW)
    return [
        square,
        square,
        square,
        square,
        plane,
        plane,
        plane,
        pltpu.VMEM((seqs * pairs, SPAN_TOTAL, 2 * LANES), NARROW),
        plane,
        pltpu.VMEM((rows, width), WIDE),
        pltpu.VMEM((rows, 1), WIDE),
        pltpu.VMEM((rows, hidden), NARROW),
        pltpu.VMEM((rows, hidden), NARROW),
        pltpu.VMEM((rows, width), WIDE),
        pltpu.VMEM((seqs, SPAN_TOTAL, LANES), WIDE),
        pltpu.VMEM((2 * ADAPTER_RANK, rows), NARROW),
    ]


def run_layer(x, gout, a, b, c, biases, downs, vectors, seg, live):
    rows, width = x.shape
    shape = jax.ShapeDtypeStruct
    hidden = b.shape[0] * b.shape[2]
    return pl.pallas_call(
        functools.partial(kernel, None),
        out_shape=(
            shape((rows, width), NARROW),
            shape((rows, width), NARROW),
            shape((2 * ADAPTER_RANK, width), WIDE),
        ),
        in_specs=[pl.BlockSpec(memory_space=pltpu.VMEM)] * 16,
        out_specs=[pl.BlockSpec(memory_space=pltpu.VMEM)] * 3,
        scratch_shapes=scratch(rows, width, hidden) + [pltpu.VMEM((8, width), WIDE)],
        compiler_params=pltpu.CompilerParams(vmem_limit_bytes=63 << 20),
    )(x, gout, a, b, c, biases, *downs, *vectors, seg, live)


def run_layer_and_gather(x, gout, blocks, adapters, biases, vectors, seg, live):
    rows, width = x.shape
    groups = width // blocks[0].shape[1]
    dps = width // blocks[0].shape[0]
    shape = jax.ShapeDtypeStruct
    gathered = pltpu.VMEM((groups, width, width), NARROW)
    signals = pltpu.SemaphoreType.DMA
    operands = (x, gout, *blocks, *adapters, *biases, *vectors, seg, live)
    return pl.pallas_call(
        functools.partial(kernel, PLAN),
        out_shape=(
            shape((rows, width), NARROW),
            shape((rows, width), NARROW),
            shape((ADAPTER_RANK, width // groups), WIDE),
            shape((ADAPTER_RANK, width // groups), WIDE),
        ),
        in_specs=[pl.BlockSpec(memory_space=pltpu.VMEM)] * len(operands),
        out_specs=[pl.BlockSpec(memory_space=pltpu.VMEM)] * 4,
        scratch_shapes=scratch(rows, width, groups * width)
        + [
            gathered,
            gathered,
            gathered,
            pltpu.VMEM((groups, 8, width), WIDE),
            pltpu.VMEM((8, width), WIDE),
            pltpu.VMEM((groups, 2 * ADAPTER_RANK, 2 * LANES), WIDE),
            pltpu.VMEM((groups - 1, 2 * ADAPTER_RANK, 2 * LANES), WIDE),
            pltpu.VMEM((dps, 2 * ADAPTER_RANK, 2 * LANES), WIDE),
            signals((3, len(SIGNALS))),
            signals((3, len(SIGNALS))),
            signals((groups - 1,)),
            signals((groups - 1,)),
            signals((groups - 1,)),
            signals((groups - 1,)),
            signals((dps - 1,)),
            signals((dps - 1,)),
        ],
        compiler_params=pltpu.CompilerParams(
            collective_id=0, has_side_effects=True, vmem_limit_bytes=63 << 20
        ),
    )(*operands)


def in_pairs(block, groups):
    parts = block.reshape(block.shape[0], groups, 3, HEAD_DIM)
    front = parts[:, :, :2].reshape(block.shape[0], -1)
    return jnp.concatenate([front, parts[:, :, 2].reshape(block.shape[0], -1)], axis=1)


def from_pairs(block, groups):
    front = block[:, : groups * LANES].reshape(block.shape[0], groups, 2, HEAD_DIM)
    back = block[:, groups * LANES :].reshape(block.shape[0], groups, 1, HEAD_DIM)
    return jnp.concatenate([front, back], axis=2).reshape(block.shape[0], -1)


def body(
    grid,
    layer_input_rows,
    output_gradient,
    query_weight,
    key_weight,
    value_weight,
    output_weight,
    up_weight,
    down_weight,
    query_bias_vector,
    value_bias_vector,
    output_bias_vector,
    up_bias_vector,
    down_bias_vector,
    query_down_frozen,
    value_down_frozen,
    query_up_trained,
    value_up_trained,
    first_norm_gain,
    first_norm_bias,
    second_norm_gain,
    second_norm_bias,
    segments,
    sentence_row_mask,
):
    everyone = ("tensor", "dp")
    rows, width = layer_input_rows.shape
    depth, across = query_weight.shape
    groups = width // across
    vectors = (
        output_bias_vector,
        down_bias_vector,
        first_norm_gain,
        first_norm_bias,
        second_norm_gain,
        second_norm_bias,
    )
    downs = (query_down_frozen.T, value_down_frozen.T)
    segment_rows = segments.reshape(-1, LANES)
    live_rows = sentence_row_mask.reshape(-1, LANES)
    if grid == (8, 4):
        return run_layer_and_gather(
            layer_input_rows,
            output_gradient,
            (query_weight, key_weight, value_weight, output_weight, up_weight, down_weight.T),
            (*downs, query_up_trained, value_up_trained),
            (query_bias_vector, value_bias_vector, up_bias_vector),
            vectors,
            segment_rows,
            live_rows,
        )

    place = lax.axis_index("tensor")
    which = lax.axis_index("dp")

    def folded(weight, down, up):
        own = lax.dynamic_slice_in_dim(down, which * depth, depth, axis=0)
        return weight.astype(WIDE) + ADAPTER_SCALE * mm(own, up)

    wq = (folded(query_weight, query_down_frozen, query_up_trained) * SCORE_SCALE).astype(NARROW)
    wv = folded(value_weight, value_down_frozen, value_up_trained).astype(NARROW)
    wk = key_weight
    wo = output_weight.T
    block_a = jnp.concatenate(
        [wq[:, :128], wk[:, :128], wv[:, :128], wq[:, 128:], wk[:, 128:], wv[:, 128:], wo[:, 128:], wo[:, :128]],
        axis=1,
    )

    def spread(block):
        return lax.all_gather(block, everyone, axis=0, tiled=True).reshape(groups, width, width)

    a, b, c = spread(block_a), spread(up_weight), spread(down_weight.T)
    query_bias = lax.all_gather(query_bias_vector * SCORE_SCALE, "tensor", axis=0, tiled=True)
    value_bias = lax.all_gather(value_bias_vector, "tensor", axis=0, tiled=True)
    up_bias = lax.all_gather(up_bias_vector, "tensor", axis=0, tiled=True)
    biases = jnp.concatenate(
        [
            in_pairs(query_bias[None], groups),
            in_pairs(value_bias[None], groups),
            up_bias.reshape(groups, width),
            jnp.zeros((6 - groups, width), WIDE),
        ],
        axis=0,
    )
    blocks = rows // LANES
    seg = lax.dynamic_slice_in_dim(segment_rows, place * blocks, blocks)
    live = lax.dynamic_slice_in_dim(live_rows, place * blocks, blocks)
    output, grad_input, grads = run_layer(
        layer_input_rows, output_gradient, a, b, c, biases, downs, vectors, seg, live
    )
    grads = from_pairs(lax.psum(grads, everyone), groups)
    grads = lax.dynamic_slice_in_dim(grads, place * across, across, axis=1)
    return output, grad_input, grads[:ADAPTER_RANK], grads[ADAPTER_RANK:]


IN_SPECS = (
    P(("dp", "tensor"), None),
    P(("dp", "tensor"), None),
    P("dp", "tensor"),
    P("dp", "tensor"),
    P("dp", "tensor"),
    P("tensor", "dp"),
    P("dp", "tensor"),
    P("tensor", "dp"),
    P("tensor"),
    P("tensor"),
    P(),
    P("tensor"),
    P(),
    P(),
    P(),
    P(None, "tensor"),
    P(None, "tensor"),
    P(),
    P(),
    P(),
    P(),
    P("dp"),
    P("dp"),
)
OUT_SPECS = (
    P(("dp", "tensor"), None),
    P(("dp", "tensor"), None),
    P(None, "tensor"),
    P(None, "tensor"),
)


def solution(mesh):
    grid = (mesh.shape["dp"], mesh.shape["tensor"])
    layer = functools.partial(body, grid)
    return jax.shard_map(layer, mesh=mesh, in_specs=IN_SPECS, out_specs=OUT_SPECS, check_vma=False)
```

```python
import functools

import jax
import jax.numpy as jnp
from jax import lax
from jax.experimental import pallas as pl
from jax.experimental.pallas import tpu as pltpu
from jax.sharding import PartitionSpec as P

HEAD_DIM = 64
ADAPTER_RANK = 8
ADAPTER_NUMER = 16
SEQ = 512
LANES = 128
EPSILON = 1e-05
NEG_FILL = -1e30
WIDE = jnp.float32
NARROW = jnp.bfloat16
ADAPTER_SCALE = ADAPTER_NUMER / ADAPTER_RANK
SCORE_SCALE = HEAD_DIM**-0.5

KEY_SPANS = ((0, 128), (128, 384), (128, 512), (256, 512))
SPAN_STARTS = (0, 128, 384, 768)
SPAN_TOTAL = 1024
BY_MESH = pl.DeviceIdType.MESH

AWAY = {"u1": 3, "u2": 2, "u3": 1, "d1": 1, "d2": 2, "d3": 3}
ARRIVALS = (
    ("X0", "Y0", "D0a", "D0b", "C", "CX0", "CY0", "CD0")
    + tuple(kind + str(k) for kind in ("Z", "X", "Y", "CZ", "CX", "CY", "CD") for k in (1, 2, 3))
    + tuple("D" + str(k) + half for k in (1, 2, 3) for half in "ab")
)
SIGNALS = {name: i for i, name in enumerate(ARRIVALS)}
for name in tuple(kind + str(k) for kind in "ZXY" for k in (1, 2, 3)):
    SIGNALS[name + "-"] = len(SIGNALS)
FROM_CORE = tuple(name for name in ARRIVALS if name[0] == "C")
PASS_ON = {
    "own": [("X0", "x", ""), ("Y0", "y", ""), ("C", "core", "")],
    "ownz": [("Zd1", "+", ""), ("Zu1", "-", "")],
    "X0": [("D0b", "y", "b"), ("CX0", "core", "")],
    "X0z": [("Xd1", "+", ""), ("Xu1", "-", "")],
    "Y0": [("D0a", "x", "a"), ("CY0", "core", "")],
    "Y0z": [("Yd1", "+", ""), ("Yu1", "-", "")],
    "D0a": [],
    "D0b": [("CD0", "core", "")],
}
for away in AWAY:
    onward = "Z" + away[0] + str(int(away[1]) + 1)
    spread_z = [(onward, "+" if away[0] == "d" else "-", "")] if away[1] < "3" else []
    spread_xy = [("X" + away, "x", ""), ("Y" + away, "y", "")] if away[1] > "1" else []
    PASS_ON["Z" + away] = spread_z + spread_xy + [("CZ" + away, "core", "")]
    PASS_ON["X" + away] = [("D" + away + "b", "y", "b"), ("CX" + away, "core", "")]
    PASS_ON["Y" + away] = [("D" + away + "a", "x", "a"), ("CY" + away, "core", "")]
    PASS_ON["D" + away + "a"] = []
    PASS_ON["D" + away + "b"] = [("CD" + away, "core", "")]


STEPS = tuple(PASS_ON)


def steps_of(*codes):
    return [(code // 100, STEPS[code % 100]) for code in codes]


PLAN = {
    "first": {
        0: steps_of(
            1, 0,
        ),
    },
    "start": {
        0: steps_of(
            100, 101, 8, 4, 2, 200, 23, 5, 6, 102, 13, 28, 25, 204, 3, 29, 18, 14, 33, 10, 30,
            108, 15, 19, 20, 123, 24, 7, 11, 9, 201, 113, 34, 35, 16, 17, 202,
        ),
    },
    "masked": {
        0: steps_of(
            128, 26, 12, 21, 22, 36, 37, 27, 104, 31, 32, 206,
        ) + [(0, name) for name in FROM_CORE],
    },
    "project": {
        0: steps_of(
            208, 130, 133, 118, 223, 103,
        ),
        1: steps_of(
            105,
        ),
        2: steps_of(
            228, 114,
        ),
    },
    "attend": {
        0: steps_of(
            213, 119, 129,
        ),
        2: steps_of(
            115, 230, 203, 205, 120, 134,
        ),
        3: steps_of(
            125, 109, 135, 110, 124,
        ),
    },
    "first_norm": {
        2: steps_of(
            126, 231, 116, 117, 121, 106, 107, 229, 218, 127,
        ),
        3: steps_of(
            122, 136, 137, 214, 111, 112, 233, 215, 131, 132,
        ),
    },
    "before up": {
        0: steps_of(

        ) + [(1, name) for name in FROM_CORE],
    },
    "up": {
        1: steps_of(
            219, 235, 234, 207, 220, 225, 216, 209, 217, 210, 224, 232,
        ),
        3: steps_of(
            221, 222, 211, 212, 226, 227, 236, 237,
        ),
    },
    "before down": {
        0: steps_of(

        ) + [(2, name) for name in FROM_CORE],
    },
}


class Gather:
    def __init__(self, blocks, send, recv):
        self.blocks, self.send, self.recv = blocks, send, recv
        self.d, self.t = lax.axis_index("dp"), lax.axis_index("tensor")
        self.depth = blocks[0].shape[1] // 8
        self.z, self.y = self.d // 2, lax.rem(self.d, 2)
        self.tx = lax.rem(self.t + 2, 4)
        self.tc = self.t + 1 - 2 * lax.rem(self.t, 2)
        self.txc = lax.rem(self.tc + 2, 4)

    def peer(self, kind):
        return {
            "x": (self.d, self.tx),
            "y": (self.z * 2 + 1 - self.y, self.t),
            "core": (self.d, self.tc),
            "+": (self.d + 2, self.t),
            "-": (self.d - 2, self.t),
        }[kind]

    def there_is(self, kind):
        if kind[0] in "+u":
            return self.z <= 3 - int(kind[1:] or 1)
        if kind[0] in "-d":
            return self.z >= int(kind[1:] or 1)
        return None

    @staticmethod
    def away(name):
        for away, k in AWAY.items():
            if away in name:
                return away, name.replace(away, str(k))
        return None, name

    def part(self, group, name, half=""):
        away, signal = self.away(name)
        if name.startswith("own"):
            dp, t = self.d, self.t
        elif name == "C":
            dp, t = self.d, self.tc
        else:
            bare = signal.rstrip("abz")
            half = half or signal[len(bare) :].strip("z")
            kind, k = bare[-2], int(bare[-1])
            if away:
                plane = self.z + int(away[1]) if away[0] == "u" else self.z - int(away[1])
            else:
                plane = lax.rem(self.z - k + 4, 4) if k else self.z
            near, far = (self.tc, self.txc) if name[0] == "C" else (self.t, self.tx)
            dp = plane * 2 + (self.y if kind in "ZX" else 1 - self.y)
            t = near if kind in "ZY" else far
        size = self.depth // 2 if half else self.depth
        first = dp * self.depth + (size if half == "b" else 0)
        return self.blocks[group].at[t, pl.ds(pl.multiple_of(first, 16), size), :]

    def copy(self, group, part, name, to):
        signal = self.away(name)[1]
        return pltpu.make_async_remote_copy(
            src_ref=part,
            dst_ref=part,
            send_sem=self.send.at[group, SIGNALS[signal + "-" if to == "-" else signal]],
            recv_sem=self.recv.at[group, SIGNALS[signal]],
            device_id=self.peer(to),
            device_id_type=BY_MESH,
        )

    def when(self, kind, body):
        there = self.there_is(kind) if kind else None
        if there is None:
            body()
        else:
            pl.when(there)(body)

    def each_copy(self, group, name, act):
        for out, to, half in PASS_ON.get(name, ()):
            source = name[:-1] if name[0] == "D" else name

            def one(out=out, to=to, half=half, source=source):
                act(self.copy(group, self.part(group, source, half), out, to))

            self.when(to, one)

    def step(self, group, name):
        def body():
            if not name.startswith("own") and not name.endswith("z"):
                self.copy(group, self.part(group, name), name, "x").wait_recv()
            self.each_copy(group, name, lambda copy: copy.start())

        self.when(self.away(name)[0], body)

    def finish(self, group):
        for name in PASS_ON:
            self.when(
                self.away(name)[0],
                lambda name=name: self.each_copy(group, name, lambda copy: copy.wait_send()),
            )


def mm(left, right):
    return jnp.dot(left, right, preferred_element_type=WIDE)


def mm_nt(left, right):
    return lax.dot_general(left, right, (((1,), (1,)), ((), ())), preferred_element_type=WIDE)


def mm_tn(left, right):
    return lax.dot_general(left, right, (((0,), (0,)), ((), ())), preferred_element_type=WIDE)


def row_mean(block):
    return jnp.sum(block, axis=-1, keepdims=True) * (1.0 / block.shape[-1])


def gelu_parts(value):
    below = 0.5 + 0.5 * lax.erf(value * 0.7071067811865476)
    bell = jnp.exp(value * value * -0.5) * 0.3989422804014327
    return value * below, below + value * bell


def pair_select(low, high):
    lane = lax.broadcasted_iota(jnp.int32, low.shape, 1)
    return jnp.where(lane < HEAD_DIM, low, pltpu.roll(high, HEAD_DIM, 1))


def kernel(plan, *refs):
    if plan is not None:
        (x_ref, gout_ref, wq_ref, wk_ref, wv_ref, wo_ref, up_ref, down_ref, dq_ref, dv_ref, uq_ref, uv_ref) = refs[:12]
        (bq_ref, bv_ref, bup_ref) = refs[12:15]
        vector_refs, (seg_ref, live_ref) = refs[15:21], refs[21:23]
        (out_ref, gin_ref, glq_ref, glv_ref) = refs[23:27]
        (wq, wk, wv, wo, q, k, v, probs, ctx, n1, s1, act, slope, acc, mask, u_t) = refs[27:43]
        (a_ref, b_ref, c_ref, bias, biases, part, near, far) = refs[43:51]
        (send, recv, bias_send, bias_recv, near_send, near_recv, far_send, far_recv) = refs[51:]
    else:
        (x_ref, gout_ref, a_ref, b_ref, c_ref, biases_ref, dq_ref, dv_ref) = refs[:8]
        vector_refs, (seg_ref, live_ref) = refs[8:14], refs[14:16]
        (out_ref, gin_ref, gl_ref) = refs[16:19]
        (wq, wk, wv, wo, q, k, v, probs, ctx, n1, s1, act, slope, acc, mask, u_t, biases) = refs[19:]
    rows, width = x_ref.shape
    seqs = rows // SEQ
    pairs = width // LANES
    groups = a_ref.shape[0]
    out_bias, down_bias, gain1, shift1, gain2, shift2 = (
        jnp.reshape(ref[...], (1, width)) for ref in vector_refs
    )

    if plan is not None:
        gather = Gather((a_ref, b_ref, c_ref), send, recv)
        me_d, me_t = gather.d, gather.t
        dps = width // wq_ref.shape[0]
        depth = wq_ref.shape[0]
        others_t = [lax.rem(me_t + i, groups) for i in range(1, groups)]
        others_d = [lax.rem(me_d + i, dps) for i in range(1, dps)]
        seg_rows = pl.ds(pl.multiple_of(me_t * (rows // LANES), rows // LANES), rows // LANES)
        barrier = pltpu.get_barrier_semaphore()
        for other in others_t:
            pl.semaphore_signal(barrier, inc=1, device_id=(me_d, other), device_id_type=BY_MESH)
        for other in others_d:
            pl.semaphore_signal(barrier, inc=1, device_id=(other, me_t), device_id_type=BY_MESH)

        mine = pl.ds(pl.multiple_of(me_d * depth, depth), depth)
        across = wq_ref.shape[1]
        acc[0:width, 0:across] = mm_tn(dq_ref[...], uq_ref[...])
        acc[0:width, 256 : 256 + across] = mm_tn(dv_ref[...], uv_ref[...])
        query = (wq_ref[...].astype(WIDE) + ADAPTER_SCALE * acc[mine, 0:across]) * SCORE_SCALE
        value = wv_ref[...].astype(WIDE) + ADAPTER_SCALE * acc[mine, 256 : 256 + across]
        key = wk_ref[...].astype(WIDE)
        out_t = jnp.transpose(wo_ref[...].astype(WIDE))
        a_ref[me_t, mine, 0:128] = query[:, 0:128].astype(NARROW)
        a_ref[me_t, mine, 128:256] = key[:, 0:128].astype(NARROW)
        a_ref[me_t, mine, 256:384] = value[:, 0:128].astype(NARROW)
        a_ref[me_t, mine, 384:512] = jnp.concatenate([query[:, 128:], key[:, 128:]], axis=1).astype(NARROW)
        a_ref[me_t, mine, 512:640] = jnp.concatenate([value[:, 128:], out_t[:, 128:]], axis=1).astype(NARROW)
        a_ref[me_t, mine, 640:768] = out_t[:, 0:128].astype(NARROW)
        bias[me_t, 0:1, :] = jnp.reshape(bup_ref[...], (1, width))
        bias[me_t, 1:2, 0:across] = jnp.reshape(bq_ref[...], (1, across)) * SCORE_SCALE
        bias[me_t, 1:2, 256 : 256 + across] = jnp.reshape(bv_ref[...], (1, across))
        pl.semaphore_wait(barrier, len(others_t) + len(others_d))

        def bias_copy(i):
            return pltpu.make_async_remote_copy(
                src_ref=bias.at[me_t],
                dst_ref=bias.at[me_t],
                send_sem=bias_send.at[i],
                recv_sem=bias_recv.at[i],
                device_id=(me_d, others_t[i]),
                device_id_type=BY_MESH,
            )

        for group, name in plan.get("first", {0: ()})[0]:
            gather.step(group, name)
        b_ref[me_t, mine, :] = up_ref[...]
        c_ref[me_t, mine, :] = down_ref[...]
        for i in range(len(others_t)):
            bias_copy(i).start()
    else:
        seg_rows = pl.ds(0, rows // LANES)
        biases[...] = biases_ref[...]

    def ticks(place, step=None):
        if plan is None:
            return
        for at, names in plan.get(place, {}).items():
            if step is None:
                for group, name in names:
                    gather.step(group, name)
            else:

                @pl.when(step == at)
                def _():
                    for group, name in names:
                        gather.step(group, name)

    segment_ids = seg_ref[seg_rows, :]
    live_flags = live_ref[seg_rows, :]
    ticks("start")
    place = lax.broadcasted_iota(jnp.int32, (LANES, LANES), 0) == lax.broadcasted_iota(
        jnp.int32, (LANES, LANES), 1
    )
    for seq in range(seqs):
        wide_ids = []
        key_ids = []
        for block in range(4):
            row = seq * 4 + block
            ids = segment_ids[row : row + 1, :].astype(WIDE)
            live = live_flags[row : row + 1, :]
            key = jnp.where(live == 1, ids, -1.0)
            wide_ids.append(ids)
            key_ids.append(jnp.transpose(jnp.broadcast_to(key, (LANES, LANES))))
        for block in range(1, 4):
            start, stop = KEY_SPANS[block]
            for j in range((stop - start) // LANES):
                kb = start // LANES + j
                seen = key_ids[kb] == wide_ids[block]
                if kb == block:
                    seen = seen | place
                at = SPAN_STARTS[block] + j * LANES
                mask[seq, at : at + LANES, :] = jnp.where(seen, 0.0, NEG_FILL)

    adapters_down = jnp.concatenate([dq_ref[...].astype(WIDE), dv_ref[...].astype(WIDE)], axis=0)
    u_t[...] = mm_nt(adapters_down.astype(NARROW), x_ref[...]).astype(NARROW)

    ticks("masked")

    for group in range(groups):
        at = slice(group * LANES, (group + 1) * LANES)
        wq[:, at] = a_ref[group, :, 0:128]
        wk[:, at] = a_ref[group, :, 128:256]
        wv[:, at] = a_ref[group, :, 256:384]
        wo[:, at] = a_ref[group, :, 640:768]
    for half in range(groups // 2):
        at = slice((groups + half) * LANES, (groups + half + 1) * LANES)
        first = a_ref[2 * half, :, 384:512].astype(WIDE)
        second = a_ref[2 * half + 1, :, 384:512].astype(WIDE)
        wq[:, at] = pair_select(first, second).astype(NARROW)
        wk[:, at] = pair_select(pltpu.roll(first, HEAD_DIM, 1), pltpu.roll(second, HEAD_DIM, 1)).astype(NARROW)
        first = a_ref[2 * half, :, 512:640].astype(WIDE)
        second = a_ref[2 * half + 1, :, 512:640].astype(WIDE)
        wv[:, at] = pair_select(first, second).astype(NARROW)
        wo[:, at] = pair_select(pltpu.roll(first, HEAD_DIM, 1), pltpu.roll(second, HEAD_DIM, 1)).astype(NARROW)

    if plan is not None:
        for i in range(len(others_t)):
            pltpu.make_async_remote_copy(
                src_ref=bias.at[me_t],
                dst_ref=bias.at[lax.rem(me_t + groups - 1 - i, groups)],
                send_sem=bias_send.at[i],
                recv_sem=bias_recv.at[i],
                device_id=(me_d, others_t[i]),
                device_id_type=BY_MESH,
            ).wait_recv()
        for group in range(groups):
            biases[2 + group : 3 + group, :] = bias[group, 0:1, :]
            biases[0:1, group * LANES : (group + 1) * LANES] = bias[group, 1:2, 0:128]
            biases[1:2, group * LANES : (group + 1) * LANES] = bias[group, 1:2, 256:384]
        for half in range(groups // 2):
            at = slice((groups + half) * LANES, (groups + half + 1) * LANES)
            for row, first in ((0, 128), (1, 384)):
                low = jnp.broadcast_to(bias[2 * half, 1:2, first : first + 128], (8, LANES))
                high = jnp.broadcast_to(bias[2 * half + 1, 1:2, first : first + 128], (8, LANES))
                biases[row : row + 1, at] = pair_select(low, high)[0:1]

    def project(step, carry):
        ticks("project", step)
        at = pl.ds(pl.multiple_of(step * 256, 256), 256)
        xs = x_ref[...]
        q[:, at] = (mm(xs, wq[:, at]) + biases[0:1, at]).astype(NARROW)
        k[:, at] = mm(xs, wk[:, at]).astype(NARROW)
        v[:, at] = (mm(xs, wv[:, at]) + biases[1:2, at]).astype(NARROW)
        return carry

    lax.fori_loop(0, width // 256, project, 0)

    lane = lax.broadcasted_iota(jnp.int32, (LANES, LANES), 1)
    together = 3
    steps = seqs * pairs // together

    def stacked(tile):
        none = jnp.zeros_like(tile)
        return jnp.concatenate(
            [jnp.where(lane < HEAD_DIM, tile, none), jnp.where(lane < HEAD_DIM, none, tile)], axis=0
        )

    def merged(tile):
        return jnp.where(lane < HEAD_DIM, tile[:LANES], tile[LANES:]).astype(NARROW)

    def work_of(step):
        items = []
        for one in range(together):
            index = step * together + one
            seq = index // pairs
            base = pl.multiple_of(seq * SEQ, SEQ)
            at = pl.ds(pl.multiple_of((index - seq * pairs) * LANES, LANES), LANES)
            for block, (start, stop) in enumerate(KEY_SPANS):
                here = pl.ds(base + block * LANES, LANES)
                there = pl.ds(base + start, stop - start)
                span = pl.ds(SPAN_STARTS[block], stop - start)
                items.append((index, seq, here, there, at, span, block))
        return items

    def attend(step, carry):
        ticks("attend", step)
        items = work_of(step)
        scores = [mm_nt(k[there, at], stacked(q[here, at])) for _, _, here, there, at, _, _ in items]
        weights = []
        for (index, seq, _, _, _, span, block), score in zip(items, scores):
            if block:
                shade = mask[seq, span, :]
                score = score + jnp.concatenate([shade, shade], axis=1)
            powers = jnp.exp(score - jnp.max(score, axis=0, keepdims=True))
            total = jnp.sum(powers, axis=0, keepdims=True)
            weights.append((powers * (1.0 / total)).astype(NARROW))
            probs[index, span, :] = weights[-1]
        for (_, _, here, there, at, _, _), weight in zip(items, weights):
            ctx[here, at] = merged(mm_tn(weight, v[there, at]))
        return carry

    lax.fori_loop(0, steps, attend, 0)

    def first_norm(step, carry):
        ticks("first_norm", step)
        at = pl.ds(pl.multiple_of(step * 256, 256), 256)
        r = x_ref[at, :].astype(WIDE) + (mm_nt(ctx[at, :], wo[...]) + out_bias)
        centered = r - row_mean(r)
        inverse = lax.rsqrt(row_mean(centered * centered) + EPSILON)
        normed = centered * inverse
        n1[at, :] = normed
        s1[at, :] = inverse
        out_ref[at, :] = (normed * gain1 + shift1).astype(NARROW)
        return carry

    lax.fori_loop(0, rows // 256, first_norm, 0)

    def up(group, carry):
        ticks("up", group)
        for j in range(width // 256):
            cols = slice(j * 256, (j + 1) * 256)
            at = pl.ds(pl.multiple_of(group * width + j * 256, 256), 256)
            inner = mm(out_ref[...], b_ref[group, :, cols]) + biases[pl.ds(2 + group, 1), cols]
            value, grad = gelu_parts(inner)
            act[:, at] = value.astype(NARROW)
            slope[:, at] = grad.astype(NARROW)
        return carry

    ticks("before up")
    lax.fori_loop(0, groups, up, 0)
    ticks("before down")

    def second_norm(step, carry):
        at = pl.ds(pl.multiple_of(step * 256, 256), 256)
        r = n1[at, :] * gain1 + shift1 + down_bias
        for group in range(groups):
            r = r + mm_nt(act[at, group * width : (group + 1) * width], c_ref[group])
        centered = r - row_mean(r)
        inverse = lax.rsqrt(row_mean(centered * centered) + EPSILON)
        normed = centered * inverse
        out_ref[at, :] = (normed * gain2 + shift2).astype(NARROW)
        e = gout_ref[at, :].astype(WIDE) * gain2
        acc[at, :] = inverse * (e - row_mean(e) - normed * row_mean(e * normed))
        return carry

    lax.fori_loop(0, rows // 256, second_norm, 0)

    def down_back(step, carry):
        at = pl.ds(pl.multiple_of(step * 256, 256), 256)
        second = acc[at, :]
        low = second.astype(NARROW)
        total = second
        for group in range(groups):
            cols = slice(group * width, (group + 1) * width)
            grad = (mm(low, c_ref[group]) * slope[at, cols].astype(WIDE)).astype(NARROW)
            total = total + mm_nt(grad, b_ref[group])
        normed = n1[at, :]
        e = total * gain1
        first = s1[at, :] * (e - row_mean(e) - normed * row_mean(e * normed))
        acc[at, :] = first
        ctx[at, :] = mm(first.astype(NARROW), wo[...]).astype(NARROW)
        return carry

    lax.fori_loop(0, rows // 256, down_back, 0)

    def attend_back(step, carry):
        items = work_of(step)
        grad_q, grad_k, grad_v = [], {}, {}
        for index, seq, here, there, at, span, block in items:
            grads = stacked(ctx[here, at])
            weights = probs[index, span, :]
            part = weights.astype(WIDE) * mm_nt(v[there, at], grads)
            inside = jnp.sum(part, axis=0, keepdims=True)
            grad_scores = (part - weights.astype(WIDE) * inside).astype(NARROW)
            grad_q.append(merged(mm_tn(grad_scores, k[there, at])))
            for_keys = mm(grad_scores, stacked(q[here, at]))
            for_values = mm(weights, grads)
            start, stop = KEY_SPANS[block]
            for j in range((stop - start) // LANES):
                rows_here = slice(j * LANES, (j + 1) * LANES)
                key = (len(grad_q) - 1) // 4, start // LANES + j
                for grad, more in ((grad_k, for_keys), (grad_v, for_values)):
                    grad[key] = grad[key] + more[rows_here] if key in grad else more[rows_here]
        for (_, _, here, _, at, _, _), grad in zip(items, grad_q):
            q[here, at] = grad
        for one, kb in grad_k:
            _, _, here, _, at, _, _ = items[4 * one + kb]
            k[here, at] = grad_k[one, kb].astype(NARROW)
            v[here, at] = grad_v[one, kb].astype(NARROW)
        return carry

    lax.fori_loop(0, steps, attend_back, 0)

    grad_q = mm(u_t[0:8, :], q[...]) * (ADAPTER_SCALE * SCORE_SCALE)
    grad_v = mm(u_t[8:16, :], v[...]) * ADAPTER_SCALE

    def input_back(step, carry):
        at = pl.ds(pl.multiple_of(step * 256, 256), 256)
        total = acc[at, :] + mm_nt(q[at, :], wq[...])
        total = total + mm_nt(k[at, :], wk[...])
        total = total + mm_nt(v[at, :], wv[...])
        gin_ref[at, :] = total.astype(NARROW)
        return carry

    if plan is None:
        gl_ref[0:8, :] = grad_q
        gl_ref[8:16, :] = grad_v
        lax.fori_loop(0, rows // 256, input_back, 0)
        return

    for group in range(groups):
        for row, grad in ((0, grad_q), (8, grad_v)):
            part[group, row : row + 8, 0:128] = grad[:, group * LANES : (group + 1) * LANES]
            other = groups + group // 2
            part[group, row : row + 8, 128:256] = grad[:, other * LANES : (other + 1) * LANES]

    def near_copy(i, slot):
        return pltpu.make_async_remote_copy(
            src_ref=part.at[others_t[i]],
            dst_ref=near.at[slot],
            send_sem=near_send.at[i],
            recv_sem=near_recv.at[i],
            device_id=(me_d, others_t[i]),
            device_id_type=BY_MESH,
        )

    def far_copy(i, slot):
        return pltpu.make_async_remote_copy(
            src_ref=far.at[me_d],
            dst_ref=far.at[slot],
            send_sem=far_send.at[i],
            recv_sem=far_recv.at[i],
            device_id=(others_d[i], me_t),
            device_id_type=BY_MESH,
        )

    for i in range(len(others_t)):
        near_copy(i, i).start()
    lax.fori_loop(0, rows // 512, input_back, 0)
    total = part[me_t]
    for i in range(len(others_t)):
        near_copy(i, i).wait_recv()
        total = total + near[i]
    far[me_d] = total
    for i in range(len(others_d)):
        far_copy(i, me_d).start()
    lax.fori_loop(rows // 512, rows // 256, input_back, 0)
    for group in range(3):
        gather.finish(group)
    for i in range(len(others_t)):
        bias_copy(i).wait_send()
        near_copy(i, i).wait_send()
    for i in range(len(others_d)):
        far_copy(i, lax.rem(me_d + dps - 1 - i, dps)).wait_recv()
    total = far[0]
    for i in range(1, dps):
        total = total + far[i]
    last = jnp.where(lax.rem(me_t, 2) == 0, total[:, 128:], pltpu.roll(total[:, 128:], HEAD_DIM, 1))
    glq_ref[:, 0:128] = total[0:8, 0:128]
    glv_ref[:, 0:128] = total[8:16, 0:128]
    glq_ref[:, 128:192] = last[0:8, 0:HEAD_DIM]
    glv_ref[:, 128:192] = last[8:16, 0:HEAD_DIM]
    for i in range(len(others_d)):
        far_copy(i, me_d).wait_send()


def scratch(rows, width, hidden):
    pairs = width // LANES
    seqs = rows // SEQ
    square = pltpu.VMEM((width, width), NARROW)
    plane = pltpu.VMEM((rows, width), NARROW)
    return [
        square,
        square,
        square,
        square,
        plane,
        plane,
        plane,
        pltpu.VMEM((seqs * pairs, SPAN_TOTAL, 2 * LANES), NARROW),
        plane,
        pltpu.VMEM((rows, width), WIDE),
        pltpu.VMEM((rows, 1), WIDE),
        pltpu.VMEM((rows, hidden), NARROW),
        pltpu.VMEM((rows, hidden), NARROW),
        pltpu.VMEM((rows, width), WIDE),
        pltpu.VMEM((seqs, SPAN_TOTAL, LANES), WIDE),
        pltpu.VMEM((2 * ADAPTER_RANK, rows), NARROW),
    ]


def run_layer(x, gout, a, b, c, biases, downs, vectors, seg, live):
    rows, width = x.shape
    shape = jax.ShapeDtypeStruct
    hidden = b.shape[0] * b.shape[2]
    return pl.pallas_call(
        functools.partial(kernel, None),
        out_shape=(
            shape((rows, width), NARROW),
            shape((rows, width), NARROW),
            shape((2 * ADAPTER_RANK, width), WIDE),
        ),
        in_specs=[pl.BlockSpec(memory_space=pltpu.VMEM)] * 16,
        out_specs=[pl.BlockSpec(memory_space=pltpu.VMEM)] * 3,
        scratch_shapes=scratch(rows, width, hidden) + [pltpu.VMEM((8, width), WIDE)],
        compiler_params=pltpu.CompilerParams(vmem_limit_bytes=63 << 20),
    )(x, gout, a, b, c, biases, *downs, *vectors, seg, live)


def run_layer_and_gather(x, gout, blocks, adapters, biases, vectors, seg, live):
    rows, width = x.shape
    groups = width // blocks[0].shape[1]
    dps = width // blocks[0].shape[0]
    gathered = pltpu.VMEM((groups, width, width), NARROW)
    signals = pltpu.SemaphoreType.DMA
    operands = (x, gout, *blocks, *adapters, *biases, *vectors, seg, live)
    return pl.pallas_call(
        functools.partial(kernel, PLAN),
        out_shape=(
            pltpu.VMEM((rows, width), NARROW),
            pltpu.VMEM((rows, width), NARROW),
            pltpu.VMEM((ADAPTER_RANK, width // groups), WIDE),
            pltpu.VMEM((ADAPTER_RANK, width // groups), WIDE),
        ),
        in_specs=[pl.BlockSpec(memory_space=pltpu.VMEM)] * len(operands),
        out_specs=[pl.BlockSpec(memory_space=pltpu.VMEM)] * 4,
        scratch_shapes=scratch(rows, width, groups * width)
        + [
            gathered,
            gathered,
            gathered,
            pltpu.VMEM((groups, 8, width), WIDE),
            pltpu.VMEM((8, width), WIDE),
            pltpu.VMEM((groups, 2 * ADAPTER_RANK, 2 * LANES), WIDE),
            pltpu.VMEM((groups - 1, 2 * ADAPTER_RANK, 2 * LANES), WIDE),
            pltpu.VMEM((dps, 2 * ADAPTER_RANK, 2 * LANES), WIDE),
            signals((3, len(SIGNALS))),
            signals((3, len(SIGNALS))),
            signals((groups - 1,)),
            signals((groups - 1,)),
            signals((groups - 1,)),
            signals((groups - 1,)),
            signals((dps - 1,)),
            signals((dps - 1,)),
        ],
        compiler_params=pltpu.CompilerParams(
            collective_id=0, has_side_effects=True, vmem_limit_bytes=59 << 20
        ),
    )(*operands)


def in_pairs(block, groups):
    parts = block.reshape(block.shape[0], groups, 3, HEAD_DIM)
    front = parts[:, :, :2].reshape(block.shape[0], -1)
    return jnp.concatenate([front, parts[:, :, 2].reshape(block.shape[0], -1)], axis=1)


def from_pairs(block, groups):
    front = block[:, : groups * LANES].reshape(block.shape[0], groups, 2, HEAD_DIM)
    back = block[:, groups * LANES :].reshape(block.shape[0], groups, 1, HEAD_DIM)
    return jnp.concatenate([front, back], axis=2).reshape(block.shape[0], -1)


def body(
    grid,
    layer_input_rows,
    output_gradient,
    query_weight,
    key_weight,
    value_weight,
    output_weight,
    up_weight,
    down_weight,
    query_bias_vector,
    value_bias_vector,
    output_bias_vector,
    up_bias_vector,
    down_bias_vector,
    query_down_frozen,
    value_down_frozen,
    query_up_trained,
    value_up_trained,
    first_norm_gain,
    first_norm_bias,
    second_norm_gain,
    second_norm_bias,
    segments,
    sentence_row_mask,
):
    everyone = ("tensor", "dp")
    rows, width = layer_input_rows.shape
    depth, across = query_weight.shape
    groups = width // across
    vectors = (
        output_bias_vector,
        down_bias_vector,
        first_norm_gain,
        first_norm_bias,
        second_norm_gain,
        second_norm_bias,
    )
    downs = (query_down_frozen.T, value_down_frozen.T)
    segment_rows = segments.reshape(-1, LANES)
    live_rows = sentence_row_mask.reshape(-1, LANES)
    if grid == (8, 4):
        return run_layer_and_gather(
            layer_input_rows,
            output_gradient,
            (query_weight, key_weight, value_weight, output_weight, up_weight, down_weight.T),
            (*downs, query_up_trained, value_up_trained),
            (query_bias_vector, value_bias_vector, up_bias_vector),
            vectors,
            segment_rows,
            live_rows,
        )

    place = lax.axis_index("tensor")
    which = lax.axis_index("dp")

    def folded(weight, down, up):
        own = lax.dynamic_slice_in_dim(down, which * depth, depth, axis=0)
        return weight.astype(WIDE) + ADAPTER_SCALE * mm(own, up)

    wq = (folded(query_weight, query_down_frozen, query_up_trained) * SCORE_SCALE).astype(NARROW)
    wv = folded(value_weight, value_down_frozen, value_up_trained).astype(NARROW)
    wk = key_weight
    wo = output_weight.T
    block_a = jnp.concatenate(
        [wq[:, :128], wk[:, :128], wv[:, :128], wq[:, 128:], wk[:, 128:], wv[:, 128:], wo[:, 128:], wo[:, :128]],
        axis=1,
    )

    def spread(block):
        return lax.all_gather(block, everyone, axis=0, tiled=True).reshape(groups, width, width)

    a, b, c = spread(block_a), spread(up_weight), spread(down_weight.T)
    query_bias = lax.all_gather(query_bias_vector * SCORE_SCALE, "tensor", axis=0, tiled=True)
    value_bias = lax.all_gather(value_bias_vector, "tensor", axis=0, tiled=True)
    up_bias = lax.all_gather(up_bias_vector, "tensor", axis=0, tiled=True)
    biases = jnp.concatenate(
        [
            in_pairs(query_bias[None], groups),
            in_pairs(value_bias[None], groups),
            up_bias.reshape(groups, width),
            jnp.zeros((6 - groups, width), WIDE),
        ],
        axis=0,
    )
    blocks = rows // LANES
    seg = lax.dynamic_slice_in_dim(segment_rows, place * blocks, blocks)
    live = lax.dynamic_slice_in_dim(live_rows, place * blocks, blocks)
    output, grad_input, grads = run_layer(
        layer_input_rows, output_gradient, a, b, c, biases, downs, vectors, seg, live
    )
    grads = from_pairs(lax.psum(grads, everyone), groups)
    grads = lax.dynamic_slice_in_dim(grads, place * across, across, axis=1)
    return output, grad_input, grads[:ADAPTER_RANK], grads[ADAPTER_RANK:]


IN_SPECS = (
    P(("dp", "tensor"), None),
    P(("dp", "tensor"), None),
    P("dp", "tensor"),
    P("dp", "tensor"),
    P("dp", "tensor"),
    P("tensor", "dp"),
    P("dp", "tensor"),
    P("tensor", "dp"),
    P("tensor"),
    P("tensor"),
    P(),
    P("tensor"),
    P(),
    P(),
    P(),
    P(None, "tensor"),
    P(None, "tensor"),
    P(),
    P(),
    P(),
    P(),
    P("dp"),
    P("dp"),
)
OUT_SPECS = (
    P(("dp", "tensor"), None),
    P(("dp", "tensor"), None),
    P(None, "tensor"),
    P(None, "tensor"),
)


def solution(mesh):
    grid = (mesh.shape["dp"], mesh.shape["tensor"])
    layer = functools.partial(body, grid)
    return jax.shard_map(layer, mesh=mesh, in_specs=IN_SPECS, out_specs=OUT_SPECS, check_vma=False)
```

```python
import functools

import jax
import jax.numpy as jnp
from jax import lax
from jax.experimental import pallas as pl
from jax.experimental.pallas import tpu as pltpu
from jax.sharding import PartitionSpec as P

HEAD_DIM = 64
ADAPTER_RANK = 8
ADAPTER_NUMER = 16
SEQ = 512
LANES = 128
EPSILON = 1e-05
NEG_FILL = -1e30
WIDE = jnp.float32
NARROW = jnp.bfloat16
ADAPTER_SCALE = ADAPTER_NUMER / ADAPTER_RANK
SCORE_SCALE = HEAD_DIM**-0.5

KEY_SPANS = ((0, 128), (128, 384), (128, 512), (256, 512))
SPAN_STARTS = (0, 128, 384, 768)
SPAN_TOTAL = 1024
BY_MESH = pl.DeviceIdType.MESH

AWAY = {"u1": 3, "u2": 2, "u3": 1, "d1": 1, "d2": 2, "d3": 3}
ARRIVALS = (
    ("X0", "Y0", "D0a", "D0b", "C", "CX0", "CY0", "CD0")
    + tuple(kind + str(k) for kind in ("Z", "X", "Y", "CZ", "CX", "CY", "CD") for k in (1, 2, 3))
    + tuple("D" + str(k) + half for k in (1, 2, 3) for half in "ab")
)
SIGNALS = {name: i for i, name in enumerate(ARRIVALS)}
for name in tuple(kind + str(k) for kind in "ZXY" for k in (1, 2, 3)):
    SIGNALS[name + "-"] = len(SIGNALS)
FROM_CORE = tuple(name for name in ARRIVALS if name[0] == "C")
PASS_ON = {
    "own": [("X0", "x", ""), ("Y0", "y", ""), ("C", "core", "")],
    "ownz": [("Zd1", "+", ""), ("Zu1", "-", "")],
    "X0": [("D0b", "y", "b"), ("CX0", "core", "")],
    "X0z": [("Xd1", "+", ""), ("Xu1", "-", "")],
    "Y0": [("D0a", "x", "a"), ("CY0", "core", "")],
    "Y0z": [("Yd1", "+", ""), ("Yu1", "-", "")],
    "D0a": [],
    "D0b": [("CD0", "core", "")],
}
for away in AWAY:
    onward = "Z" + away[0] + str(int(away[1]) + 1)
    spread_z = [(onward, "+" if away[0] == "d" else "-", "")] if away[1] < "3" else []
    spread_xy = [("X" + away, "x", ""), ("Y" + away, "y", "")] if away[1] > "1" else []
    PASS_ON["Z" + away] = spread_z + spread_xy + [("CZ" + away, "core", "")]
    PASS_ON["X" + away] = [("D" + away + "b", "y", "b"), ("CX" + away, "core", "")]
    PASS_ON["Y" + away] = [("D" + away + "a", "x", "a"), ("CY" + away, "core", "")]
    PASS_ON["D" + away + "a"] = []
    PASS_ON["D" + away + "b"] = [("CD" + away, "core", "")]


STEPS = tuple(PASS_ON)


def steps_of(*codes):
    return [(code // 100, STEPS[code % 100]) for code in codes]


PLAN = {
    "first": {
        0: steps_of(
            1, 0,
        ),
    },
    "start": {
        0: steps_of(
            100, 101, 8, 4, 2, 200, 23, 5, 6, 102, 13, 28, 25, 204, 3, 29, 18, 14, 33, 10, 30,
            108, 15, 19, 20, 123, 24, 7, 11, 9, 201, 113, 34, 35, 16, 17, 202,
        ),
    },
    "masked": {
        0: steps_of(
            128, 26, 12, 21, 22, 36, 37, 27, 104, 31, 32, 206,
        ) + [(0, name) for name in FROM_CORE],
    },
    "project": {
        0: steps_of(
            208, 130, 133, 118, 223, 103,
        ),
        1: steps_of(
            105,
        ),
        2: steps_of(
            228, 114,
        ),
    },
    "attend": {
        0: steps_of(
            213, 119, 129,
        ),
        2: steps_of(
            115, 230, 203, 205, 120, 134,
        ),
        3: steps_of(
            125, 109, 135, 110, 124,
        ),
    },
    "first_norm": {
        2: steps_of(
            126, 231, 116, 117, 121, 106, 107, 229, 218, 127,
        ),
        3: steps_of(
            122, 136, 137, 214, 111, 112, 233, 215, 131, 132,
        ),
    },
    "before up": {
        0: steps_of(

        ) + [(1, name) for name in FROM_CORE],
    },
    "up": {
        1: steps_of(
            219, 235, 234, 207, 220, 225, 216, 209, 217, 210, 224, 232,
        ),
        3: steps_of(
            221, 222, 211, 212, 226, 227, 236, 237,
        ),
    },
    "before down": {
        0: steps_of(

        ) + [(2, name) for name in FROM_CORE],
    },
}


class Gather:
    def __init__(self, blocks, send, recv):
        self.blocks, self.send, self.recv = blocks, send, recv
        self.d, self.t = lax.axis_index("dp"), lax.axis_index("tensor")
        self.depth = blocks[0].shape[1] // 8
        self.z, self.y = self.d // 2, lax.rem(self.d, 2)
        self.tx = lax.rem(self.t + 2, 4)
        self.tc = self.t + 1 - 2 * lax.rem(self.t, 2)
        self.txc = lax.rem(self.tc + 2, 4)

    def peer(self, kind):
        return {
            "x": (self.d, self.tx),
            "y": (self.z * 2 + 1 - self.y, self.t),
            "core": (self.d, self.tc),
            "+": (self.d + 2, self.t),
            "-": (self.d - 2, self.t),
        }[kind]

    def there_is(self, kind):
        if kind[0] in "+u":
            return self.z <= 3 - int(kind[1:] or 1)
        if kind[0] in "-d":
            return self.z >= int(kind[1:] or 1)
        return None

    @staticmethod
    def away(name):
        for away, k in AWAY.items():
            if away in name:
                return away, name.replace(away, str(k))
        return None, name

    def part(self, group, name, half=""):
        away, signal = self.away(name)
        if name.startswith("own"):
            dp, t = self.d, self.t
        elif name == "C":
            dp, t = self.d, self.tc
        else:
            bare = signal.rstrip("abz")
            half = half or signal[len(bare) :].strip("z")
            kind, k = bare[-2], int(bare[-1])
            if away:
                plane = self.z + int(away[1]) if away[0] == "u" else self.z - int(away[1])
            else:
                plane = lax.rem(self.z - k + 4, 4) if k else self.z
            near, far = (self.tc, self.txc) if name[0] == "C" else (self.t, self.tx)
            dp = plane * 2 + (self.y if kind in "ZX" else 1 - self.y)
            t = near if kind in "ZY" else far
        size = self.depth // 2 if half else self.depth
        first = dp * self.depth + (size if half == "b" else 0)
        return self.blocks[group].at[t, pl.ds(pl.multiple_of(first, 16), size), :]

    def copy(self, group, part, name, to):
        signal = self.away(name)[1]
        return pltpu.make_async_remote_copy(
            src_ref=part,
            dst_ref=part,
            send_sem=self.send.at[group, SIGNALS[signal + "-" if to == "-" else signal]],
            recv_sem=self.recv.at[group, SIGNALS[signal]],
            device_id=self.peer(to),
            device_id_type=BY_MESH,
        )

    def when(self, kind, body):
        there = self.there_is(kind) if kind else None
        if there is None:
            body()
        else:
            pl.when(there)(body)

    def each_copy(self, group, name, act):
        for out, to, half in PASS_ON.get(name, ()):
            source = name[:-1] if name[0] == "D" else name

            def one(out=out, to=to, half=half, source=source):
                act(self.copy(group, self.part(group, source, half), out, to))

            self.when(to, one)

    def step(self, group, name):
        def body():
            if not name.startswith("own") and not name.endswith("z"):
                self.copy(group, self.part(group, name), name, "x").wait_recv()
            self.each_copy(group, name, lambda copy: copy.start())

        self.when(self.away(name)[0], body)

    def finish(self, group):
        for name in PASS_ON:
            self.when(
                self.away(name)[0],
                lambda name=name: self.each_copy(group, name, lambda copy: copy.wait_send()),
            )


def mm(left, right):
    return jnp.dot(left, right, preferred_element_type=WIDE)


def mm_nt(left, right):
    return lax.dot_general(left, right, (((1,), (1,)), ((), ())), preferred_element_type=WIDE)


def mm_tn(left, right):
    return lax.dot_general(left, right, (((0,), (0,)), ((), ())), preferred_element_type=WIDE)


def row_mean(block):
    return jnp.sum(block, axis=-1, keepdims=True) * (1.0 / block.shape[-1])


def gelu_parts(value):
    below = 0.5 + 0.5 * lax.erf(value * 0.7071067811865476)
    bell = jnp.exp(value * value * -0.5) * 0.3989422804014327
    return value * below, below + value * bell


def pair_select(low, high):
    lane = lax.broadcasted_iota(jnp.int32, low.shape, 1)
    return jnp.where(lane < HEAD_DIM, low, pltpu.roll(high, HEAD_DIM, 1))


def kernel(plan, *refs):
    if plan is not None:
        (x_hbm, gout_hbm, wq_ref, wk_ref, wv_ref, wo_ref, up_ref, down_ref, dq_ref, dv_ref, uq_ref, uv_ref) = refs[:12]
        (bq_ref, bv_ref, bup_ref) = refs[12:15]
        vector_refs, (seg_ref, live_ref) = refs[15:21], refs[21:23]
        (out_ref, gin_ref, glq_ref, glv_ref) = refs[23:27]
        (wq, wk, wv, wo, q, k, v, probs, ctx, n1, s1, act, slope, acc, mask, u_t) = refs[27:43]
        (a_ref, b_ref, c_ref, bias, biases, part, near, far) = refs[43:51]
        (send, recv, bias_send, bias_recv, near_send, near_recv, far_send, far_recv) = refs[51:59]
        (x_ref, gout_ref, load) = refs[59:]
    else:
        (x_ref, gout_ref, a_ref, b_ref, c_ref, biases_ref, dq_ref, dv_ref) = refs[:8]
        vector_refs, (seg_ref, live_ref) = refs[8:14], refs[14:16]
        (out_ref, gin_ref, gl_ref) = refs[16:19]
        (wq, wk, wv, wo, q, k, v, probs, ctx, n1, s1, act, slope, acc, mask, u_t, biases) = refs[19:]
    rows, width = x_ref.shape
    seqs = rows // SEQ
    pairs = width // LANES
    groups = a_ref.shape[0]
    out_bias, down_bias, gain1, shift1, gain2, shift2 = (
        jnp.reshape(ref[...], (1, width)) for ref in vector_refs
    )

    if plan is not None:
        gather = Gather((a_ref, b_ref, c_ref), send, recv)
        me_d, me_t = gather.d, gather.t
        dps = width // wq_ref.shape[0]
        depth = wq_ref.shape[0]
        others_t = [lax.rem(me_t + i, groups) for i in range(1, groups)]
        others_d = [lax.rem(me_d + i, dps) for i in range(1, dps)]
        seg_rows = pl.ds(pl.multiple_of(me_t * (rows // LANES), rows // LANES), rows // LANES)
        barrier = pltpu.get_barrier_semaphore()
        neighbours = [(me_d, other) for other in others_t] + [gather.peer("y")]
        for peer in neighbours:
            pl.semaphore_signal(barrier, inc=1, device_id=peer, device_id_type=BY_MESH)
        for kind in "+-":

            @pl.when(gather.there_is(kind))
            def _(kind=kind):
                pl.semaphore_signal(barrier, inc=1, device_id=gather.peer(kind), device_id_type=BY_MESH)

        loads = [
            pltpu.make_async_copy(source, target, load.at[i])
            for i, (source, target) in enumerate(((x_hbm, x_ref), (gout_hbm, gout_ref)))
        ]
        for copy in loads:
            copy.start()

        mine = pl.ds(pl.multiple_of(me_d * depth, depth), depth)
        across = wq_ref.shape[1]
        acc[0:width, 0:across] = mm_tn(dq_ref[...], uq_ref[...])
        acc[0:width, 256 : 256 + across] = mm_tn(dv_ref[...], uv_ref[...])
        query = (wq_ref[...].astype(WIDE) + ADAPTER_SCALE * acc[mine, 0:across]) * SCORE_SCALE
        value = wv_ref[...].astype(WIDE) + ADAPTER_SCALE * acc[mine, 256 : 256 + across]
        key = wk_ref[...].astype(WIDE)
        out_t = jnp.transpose(wo_ref[...].astype(WIDE))
        a_ref[me_t, mine, 0:128] = query[:, 0:128].astype(NARROW)
        a_ref[me_t, mine, 128:256] = key[:, 0:128].astype(NARROW)
        a_ref[me_t, mine, 256:384] = value[:, 0:128].astype(NARROW)
        a_ref[me_t, mine, 384:512] = jnp.concatenate([query[:, 128:], key[:, 128:]], axis=1).astype(NARROW)
        a_ref[me_t, mine, 512:640] = jnp.concatenate([value[:, 128:], out_t[:, 128:]], axis=1).astype(NARROW)
        a_ref[me_t, mine, 640:768] = out_t[:, 0:128].astype(NARROW)
        bias[me_t, 0:1, :] = jnp.reshape(bup_ref[...], (1, width))
        bias[me_t, 1:2, 0:across] = jnp.reshape(bq_ref[...], (1, across)) * SCORE_SCALE
        bias[me_t, 1:2, 256 : 256 + across] = jnp.reshape(bv_ref[...], (1, across))
        outer = lax.rem(gather.z, 3) == 0
        pl.semaphore_wait(barrier, len(neighbours) + jnp.where(outer, 1, 2))

        def bias_copy(i):
            return pltpu.make_async_remote_copy(
                src_ref=bias.at[me_t],
                dst_ref=bias.at[me_t],
                send_sem=bias_send.at[i],
                recv_sem=bias_recv.at[i],
                device_id=(me_d, others_t[i]),
                device_id_type=BY_MESH,
            )

        for group, name in plan.get("first", {0: ()})[0]:
            gather.step(group, name)
        b_ref[me_t, mine, :] = up_ref[...]
        c_ref[me_t, mine, :] = down_ref[...]
        for i in range(len(others_t)):
            bias_copy(i).start()
    else:
        seg_rows = pl.ds(0, rows // LANES)
        biases[...] = biases_ref[...]

    def ticks(place, step=None):
        if plan is None:
            return
        for at, names in plan.get(place, {}).items():
            if step is None:
                for group, name in names:
                    gather.step(group, name)
            else:

                @pl.when(step == at)
                def _():
                    for group, name in names:
                        gather.step(group, name)

    segment_ids = seg_ref[seg_rows, :]
    live_flags = live_ref[seg_rows, :]
    ticks("start")
    place = lax.broadcasted_iota(jnp.int32, (LANES, LANES), 0) == lax.broadcasted_iota(
        jnp.int32, (LANES, LANES), 1
    )
    for seq in range(seqs):
        wide_ids = []
        key_ids = []
        for block in range(4):
            row = seq * 4 + block
            ids = segment_ids[row : row + 1, :].astype(WIDE)
            live = live_flags[row : row + 1, :]
            key = jnp.where(live == 1, ids, -1.0)
            wide_ids.append(ids)
            key_ids.append(jnp.transpose(jnp.broadcast_to(key, (LANES, LANES))))
        for block in range(1, 4):
            start, stop = KEY_SPANS[block]
            for j in range((stop - start) // LANES):
                kb = start // LANES + j
                seen = key_ids[kb] == wide_ids[block]
                if kb == block:
                    seen = seen | place
                at = SPAN_STARTS[block] + j * LANES
                mask[seq, at : at + LANES, :] = jnp.where(seen, 0.0, NEG_FILL)

    if plan is not None:
        loads[0].wait()
    adapters_down = jnp.concatenate([dq_ref[...].astype(WIDE), dv_ref[...].astype(WIDE)], axis=0)
    u_t[...] = mm_nt(adapters_down.astype(NARROW), x_ref[...]).astype(NARROW)

    ticks("masked")

    for group in range(groups):
        at = slice(group * LANES, (group + 1) * LANES)
        wq[:, at] = a_ref[group, :, 0:128]
        wk[:, at] = a_ref[group, :, 128:256]
        wv[:, at] = a_ref[group, :, 256:384]
        wo[:, at] = a_ref[group, :, 640:768]
    for half in range(groups // 2):
        at = slice((groups + half) * LANES, (groups + half + 1) * LANES)
        first = a_ref[2 * half, :, 384:512].astype(WIDE)
        second = a_ref[2 * half + 1, :, 384:512].astype(WIDE)
        wq[:, at] = pair_select(first, second).astype(NARROW)
        wk[:, at] = pair_select(pltpu.roll(first, HEAD_DIM, 1), pltpu.roll(second, HEAD_DIM, 1)).astype(NARROW)
        first = a_ref[2 * half, :, 512:640].astype(WIDE)
        second = a_ref[2 * half + 1, :, 512:640].astype(WIDE)
        wv[:, at] = pair_select(first, second).astype(NARROW)
        wo[:, at] = pair_select(pltpu.roll(first, HEAD_DIM, 1), pltpu.roll(second, HEAD_DIM, 1)).astype(NARROW)

    if plan is not None:
        for i in range(len(others_t)):
            pltpu.make_async_remote_copy(
                src_ref=bias.at[me_t],
                dst_ref=bias.at[lax.rem(me_t + groups - 1 - i, groups)],
                send_sem=bias_send.at[i],
                recv_sem=bias_recv.at[i],
                device_id=(me_d, others_t[i]),
                device_id_type=BY_MESH,
            ).wait_recv()
        for group in range(groups):
            biases[2 + group : 3 + group, :] = bias[group, 0:1, :]
            biases[0:1, group * LANES : (group + 1) * LANES] = bias[group, 1:2, 0:128]
            biases[1:2, group * LANES : (group + 1) * LANES] = bias[group, 1:2, 256:384]
        for half in range(groups // 2):
            at = slice((groups + half) * LANES, (groups + half + 1) * LANES)
            for row, first in ((0, 128), (1, 384)):
                low = jnp.broadcast_to(bias[2 * half, 1:2, first : first + 128], (8, LANES))
                high = jnp.broadcast_to(bias[2 * half + 1, 1:2, first : first + 128], (8, LANES))
                biases[row : row + 1, at] = pair_select(low, high)[0:1]

    def project(step, carry):
        ticks("project", step)
        at = pl.ds(pl.multiple_of(step * 256, 256), 256)
        xs = x_ref[...]
        q[:, at] = (mm(xs, wq[:, at]) + biases[0:1, at]).astype(NARROW)
        k[:, at] = mm(xs, wk[:, at]).astype(NARROW)
        v[:, at] = (mm(xs, wv[:, at]) + biases[1:2, at]).astype(NARROW)
        return carry

    lax.fori_loop(0, width // 256, project, 0)

    lane = lax.broadcasted_iota(jnp.int32, (LANES, LANES), 1)
    together = 3
    steps = seqs * pairs // together

    def stacked(tile):
        none = jnp.zeros_like(tile)
        return jnp.concatenate(
            [jnp.where(lane < HEAD_DIM, tile, none), jnp.where(lane < HEAD_DIM, none, tile)], axis=0
        )

    def merged(tile):
        return jnp.where(lane < HEAD_DIM, tile[:LANES], tile[LANES:]).astype(NARROW)

    def work_of(step):
        items = []
        for one in range(together):
            index = step * together + one
            seq = index // pairs
            base = pl.multiple_of(seq * SEQ, SEQ)
            at = pl.ds(pl.multiple_of((index - seq * pairs) * LANES, LANES), LANES)
            for block, (start, stop) in enumerate(KEY_SPANS):
                here = pl.ds(base + block * LANES, LANES)
                there = pl.ds(base + start, stop - start)
                span = pl.ds(SPAN_STARTS[block], stop - start)
                items.append((index, seq, here, there, at, span, block))
        return items

    def attend(step, carry):
        ticks("attend", step)
        items = work_of(step)
        scores = [mm_nt(k[there, at], stacked(q[here, at])) for _, _, here, there, at, _, _ in items]
        weights = []
        for (index, seq, _, _, _, span, block), score in zip(items, scores):
            if block:
                shade = mask[seq, span, :]
                score = score + jnp.concatenate([shade, shade], axis=1)
            powers = jnp.exp(score - jnp.max(score, axis=0, keepdims=True))
            total = jnp.sum(powers, axis=0, keepdims=True)
            weights.append((powers * (1.0 / total)).astype(NARROW))
            probs[index, span, :] = weights[-1]
        for (_, _, here, there, at, _, _), weight in zip(items, weights):
            ctx[here, at] = merged(mm_tn(weight, v[there, at]))
        return carry

    lax.fori_loop(0, steps, attend, 0)

    def first_norm(step, carry):
        ticks("first_norm", step)
        at = pl.ds(pl.multiple_of(step * 256, 256), 256)
        r = x_ref[at, :].astype(WIDE) + (mm_nt(ctx[at, :], wo[...]) + out_bias)
        centered = r - row_mean(r)
        inverse = lax.rsqrt(row_mean(centered * centered) + EPSILON)
        normed = centered * inverse
        n1[at, :] = normed
        s1[at, :] = inverse
        out_ref[at, :] = (normed * gain1 + shift1).astype(NARROW)
        return carry

    lax.fori_loop(0, rows // 256, first_norm, 0, unroll=2)

    def up(group, carry):
        ticks("up", group)
        for j in range(width // 256):
            cols = slice(j * 256, (j + 1) * 256)
            at = pl.ds(pl.multiple_of(group * width + j * 256, 256), 256)
            inner = mm(out_ref[...], b_ref[group, :, cols]) + biases[pl.ds(2 + group, 1), cols]
            value, grad = gelu_parts(inner)
            act[:, at] = value.astype(NARROW)
            slope[:, at] = grad.astype(NARROW)
        return carry

    ticks("before up")
    lax.fori_loop(0, groups, up, 0)
    ticks("before down")
    if plan is not None:
        loads[1].wait()

    def second_norm(step, carry):
        at = pl.ds(pl.multiple_of(step * 256, 256), 256)
        r = n1[at, :] * gain1 + shift1 + down_bias
        for group in range(groups):
            r = r + mm_nt(act[at, group * width : (group + 1) * width], c_ref[group])
        centered = r - row_mean(r)
        inverse = lax.rsqrt(row_mean(centered * centered) + EPSILON)
        normed = centered * inverse
        out_ref[at, :] = (normed * gain2 + shift2).astype(NARROW)
        e = gout_ref[at, :].astype(WIDE) * gain2
        acc[at, :] = inverse * (e - row_mean(e) - normed * row_mean(e * normed))
        return carry

    lax.fori_loop(0, rows // 256, second_norm, 0, unroll=2)

    def down_back(step, carry):
        at = pl.ds(pl.multiple_of(step * 256, 256), 256)
        second = acc[at, :]
        low = second.astype(NARROW)
        total = second
        for group in range(groups):
            cols = slice(group * width, (group + 1) * width)
            grad = (mm(low, c_ref[group]) * slope[at, cols].astype(WIDE)).astype(NARROW)
            total = total + mm_nt(grad, b_ref[group])
        normed = n1[at, :]
        e = total * gain1
        first = s1[at, :] * (e - row_mean(e) - normed * row_mean(e * normed))
        acc[at, :] = first
        ctx[at, :] = mm(first.astype(NARROW), wo[...]).astype(NARROW)
        return carry

    lax.fori_loop(0, rows // 256, down_back, 0, unroll=2)

    def attend_back(step, carry):
        items = work_of(step)
        grads = [stacked(ctx[here, at]) for _, _, here, _, at, _, _ in items]
        rows_q = [stacked(q[here, at]) for _, _, here, _, at, _, _ in items]
        grad_q, grad_k, grad_v = [], {}, {}
        for n, (index, seq, here, there, at, span, block) in enumerate(items):
            weights = probs[index, span, :]
            part = weights.astype(WIDE) * mm_nt(v[there, at], grads[n])
            inside = jnp.sum(part, axis=0, keepdims=True)
            grad_scores = (part - weights.astype(WIDE) * inside).astype(NARROW)
            for_keys = mm(grad_scores, rows_q[n])
            for_values = mm(weights, grads[n])
            grad_q.append(merged(mm_tn(grad_scores, k[there, at])))
            start, stop = KEY_SPANS[block]
            for j in range((stop - start) // LANES):
                rows_here = slice(j * LANES, (j + 1) * LANES)
                key = n // 4, start // LANES + j
                for grad, more in ((grad_k, for_keys), (grad_v, for_values)):
                    grad[key] = grad[key] + more[rows_here] if key in grad else more[rows_here]
        for (_, _, here, _, at, _, _), grad in zip(items, grad_q):
            q[here, at] = grad
        for one, kb in grad_k:
            _, _, here, _, at, _, _ = items[4 * one + kb]
            k[here, at] = grad_k[one, kb].astype(NARROW)
            v[here, at] = grad_v[one, kb].astype(NARROW)
        return carry

    lax.fori_loop(0, steps, attend_back, 0)

    grad_q = mm(u_t[0:8, :], q[...]) * (ADAPTER_SCALE * SCORE_SCALE)
    grad_v = mm(u_t[8:16, :], v[...]) * ADAPTER_SCALE

    def input_back(step, carry):
        at = pl.ds(pl.multiple_of(step * 256, 256), 256)
        total = acc[at, :] + mm_nt(q[at, :], wq[...])
        total = total + mm_nt(k[at, :], wk[...])
        total = total + mm_nt(v[at, :], wv[...])
        gin_ref[at, :] = total.astype(NARROW)
        return carry

    if plan is None:
        gl_ref[0:8, :] = grad_q
        gl_ref[8:16, :] = grad_v
        lax.fori_loop(0, rows // 256, input_back, 0)
        return

    for group in range(groups):
        for row, grad in ((0, grad_q), (8, grad_v)):
            part[group, row : row + 8, 0:128] = grad[:, group * LANES : (group + 1) * LANES]
            other = groups + group // 2
            part[group, row : row + 8, 128:256] = grad[:, other * LANES : (other + 1) * LANES]

    def near_copy(i, slot):
        return pltpu.make_async_remote_copy(
            src_ref=part.at[others_t[i]],
            dst_ref=near.at[slot],
            send_sem=near_send.at[i],
            recv_sem=near_recv.at[i],
            device_id=(me_d, others_t[i]),
            device_id_type=BY_MESH,
        )

    def far_copy(i, slot):
        return pltpu.make_async_remote_copy(
            src_ref=far.at[me_d],
            dst_ref=far.at[slot],
            send_sem=far_send.at[i],
            recv_sem=far_recv.at[i],
            device_id=(others_d[i], me_t),
            device_id_type=BY_MESH,
        )

    for i in range(len(others_t)):
        near_copy(i, i).start()
    lax.fori_loop(0, rows // 512, input_back, 0)
    total = part[me_t]
    for i in range(len(others_t)):
        near_copy(i, i).wait_recv()
        total = total + near[i]
    far[me_d] = total
    for i in range(len(others_d)):
        far_copy(i, me_d).start()
    lax.fori_loop(rows // 512, rows // 256, input_back, 0)
    for group in range(3):
        gather.finish(group)
    for i in range(len(others_t)):
        bias_copy(i).wait_send()
        near_copy(i, i).wait_send()
    for i in range(len(others_d)):
        far_copy(i, lax.rem(me_d + dps - 1 - i, dps)).wait_recv()
    total = far[0]
    for i in range(1, dps):
        total = total + far[i]
    last = jnp.where(lax.rem(me_t, 2) == 0, total[:, 128:], pltpu.roll(total[:, 128:], HEAD_DIM, 1))
    glq_ref[:, 0:128] = total[0:8, 0:128]
    glv_ref[:, 0:128] = total[8:16, 0:128]
    glq_ref[:, 128:192] = last[0:8, 0:HEAD_DIM]
    glv_ref[:, 128:192] = last[8:16, 0:HEAD_DIM]
    for i in range(len(others_d)):
        far_copy(i, me_d).wait_send()


def scratch(rows, width, hidden):
    pairs = width // LANES
    seqs = rows // SEQ
    square = pltpu.VMEM((width, width), NARROW)
    plane = pltpu.VMEM((rows, width), NARROW)
    return [
        square,
        square,
        square,
        square,
        plane,
        plane,
        plane,
        pltpu.VMEM((seqs * pairs, SPAN_TOTAL, 2 * LANES), NARROW),
        plane,
        pltpu.VMEM((rows, width), WIDE),
        pltpu.VMEM((rows, 1), WIDE),
        pltpu.VMEM((rows, hidden), NARROW),
        pltpu.VMEM((rows, hidden), NARROW),
        pltpu.VMEM((rows, width), WIDE),
        pltpu.VMEM((seqs, SPAN_TOTAL, LANES), WIDE),
        pltpu.VMEM((2 * ADAPTER_RANK, rows), NARROW),
    ]


def run_layer(x, gout, a, b, c, biases, downs, vectors, seg, live):
    rows, width = x.shape
    shape = jax.ShapeDtypeStruct
    hidden = b.shape[0] * b.shape[2]
    return pl.pallas_call(
        functools.partial(kernel, None),
        out_shape=(
            shape((rows, width), NARROW),
            shape((rows, width), NARROW),
            shape((2 * ADAPTER_RANK, width), WIDE),
        ),
        in_specs=[pl.BlockSpec(memory_space=pltpu.VMEM)] * 16,
        out_specs=[pl.BlockSpec(memory_space=pltpu.VMEM)] * 3,
        scratch_shapes=scratch(rows, width, hidden) + [pltpu.VMEM((8, width), WIDE)],
        compiler_params=pltpu.CompilerParams(vmem_limit_bytes=63 << 20),
    )(x, gout, a, b, c, biases, *downs, *vectors, seg, live)


def run_layer_and_gather(x, gout, blocks, adapters, biases, vectors, seg, live):
    rows, width = x.shape
    groups = width // blocks[0].shape[1]
    dps = width // blocks[0].shape[0]
    gathered = pltpu.VMEM((groups, width, width), NARROW)
    signals = pltpu.SemaphoreType.DMA
    operands = (x, gout, *blocks, *adapters, *biases, *vectors, seg, live)
    return pl.pallas_call(
        functools.partial(kernel, PLAN),
        out_shape=(
            pltpu.VMEM((rows, width), NARROW),
            pltpu.VMEM((rows, width), NARROW),
            pltpu.VMEM((ADAPTER_RANK, width // groups), WIDE),
            pltpu.VMEM((ADAPTER_RANK, width // groups), WIDE),
        ),
        in_specs=[pl.BlockSpec(memory_space=pl.ANY)] * 2
        + [pl.BlockSpec(memory_space=pltpu.VMEM)] * (len(operands) - 2),
        out_specs=[pl.BlockSpec(memory_space=pltpu.VMEM)] * 4,
        scratch_shapes=scratch(rows, width, groups * width)
        + [
            gathered,
            gathered,
            gathered,
            pltpu.VMEM((groups, 8, width), WIDE),
            pltpu.VMEM((8, width), WIDE),
            pltpu.VMEM((groups, 2 * ADAPTER_RANK, 2 * LANES), WIDE),
            pltpu.VMEM((groups - 1, 2 * ADAPTER_RANK, 2 * LANES), WIDE),
            pltpu.VMEM((dps, 2 * ADAPTER_RANK, 2 * LANES), WIDE),
            signals((3, len(SIGNALS))),
            signals((3, len(SIGNALS))),
            signals((groups - 1,)),
            signals((groups - 1,)),
            signals((groups - 1,)),
            signals((groups - 1,)),
            signals((dps - 1,)),
            signals((dps - 1,)),
            pltpu.VMEM((rows, width), NARROW),
            pltpu.VMEM((rows, width), NARROW),
            signals((2,)),
        ],
        compiler_params=pltpu.CompilerParams(
            collective_id=0, has_side_effects=True, vmem_limit_bytes=59 << 20
        ),
    )(*operands)


def in_pairs(block, groups):
    parts = block.reshape(block.shape[0], groups, 3, HEAD_DIM)
    front = parts[:, :, :2].reshape(block.shape[0], -1)
    return jnp.concatenate([front, parts[:, :, 2].reshape(block.shape[0], -1)], axis=1)


def from_pairs(block, groups):
    front = block[:, : groups * LANES].reshape(block.shape[0], groups, 2, HEAD_DIM)
    back = block[:, groups * LANES :].reshape(block.shape[0], groups, 1, HEAD_DIM)
    return jnp.concatenate([front, back], axis=2).reshape(block.shape[0], -1)


def body(
    grid,
    layer_input_rows,
    output_gradient,
    query_weight,
    key_weight,
    value_weight,
    output_weight,
    up_weight,
    down_weight,
    query_bias_vector,
    value_bias_vector,
    output_bias_vector,
    up_bias_vector,
    down_bias_vector,
    query_down_frozen,
    value_down_frozen,
    query_up_trained,
    value_up_trained,
    first_norm_gain,
    first_norm_bias,
    second_norm_gain,
    second_norm_bias,
    segments,
    sentence_row_mask,
):
    everyone = ("tensor", "dp")
    rows, width = layer_input_rows.shape
    depth, across = query_weight.shape
    groups = width // across
    vectors = (
        output_bias_vector,
        down_bias_vector,
        first_norm_gain,
        first_norm_bias,
        second_norm_gain,
        second_norm_bias,
    )
    downs = (query_down_frozen.T, value_down_frozen.T)
    segment_rows = segments.reshape(-1, LANES)
    live_rows = sentence_row_mask.reshape(-1, LANES)
    if grid == (8, 4):
        return run_layer_and_gather(
            layer_input_rows,
            output_gradient,
            (query_weight, key_weight, value_weight, output_weight, up_weight, down_weight.T),
            (*downs, query_up_trained, value_up_trained),
            (query_bias_vector, value_bias_vector, up_bias_vector),
            vectors,
            segment_rows,
            live_rows,
        )

    place = lax.axis_index("tensor")
    which = lax.axis_index("dp")

    def folded(weight, down, up):
        own = lax.dynamic_slice_in_dim(down, which * depth, depth, axis=0)
        return weight.astype(WIDE) + ADAPTER_SCALE * mm(own, up)

    wq = (folded(query_weight, query_down_frozen, query_up_trained) * SCORE_SCALE).astype(NARROW)
    wv = folded(value_weight, value_down_frozen, value_up_trained).astype(NARROW)
    wk = key_weight
    wo = output_weight.T
    block_a = jnp.concatenate(
        [wq[:, :128], wk[:, :128], wv[:, :128], wq[:, 128:], wk[:, 128:], wv[:, 128:], wo[:, 128:], wo[:, :128]],
        axis=1,
    )

    def spread(block):
        return lax.all_gather(block, everyone, axis=0, tiled=True).reshape(groups, width, width)

    a, b, c = spread(block_a), spread(up_weight), spread(down_weight.T)
    query_bias = lax.all_gather(query_bias_vector * SCORE_SCALE, "tensor", axis=0, tiled=True)
    value_bias = lax.all_gather(value_bias_vector, "tensor", axis=0, tiled=True)
    up_bias = lax.all_gather(up_bias_vector, "tensor", axis=0, tiled=True)
    biases = jnp.concatenate(
        [
            in_pairs(query_bias[None], groups),
            in_pairs(value_bias[None], groups),
            up_bias.reshape(groups, width),
            jnp.zeros((6 - groups, width), WIDE),
        ],
        axis=0,
    )
    blocks = rows // LANES
    seg = lax.dynamic_slice_in_dim(segment_rows, place * blocks, blocks)
    live = lax.dynamic_slice_in_dim(live_rows, place * blocks, blocks)
    output, grad_input, grads = run_layer(
        layer_input_rows, output_gradient, a, b, c, biases, downs, vectors, seg, live
    )
    grads = from_pairs(lax.psum(grads, everyone), groups)
    grads = lax.dynamic_slice_in_dim(grads, place * across, across, axis=1)
    return output, grad_input, grads[:ADAPTER_RANK], grads[ADAPTER_RANK:]


IN_SPECS = (
    P(("dp", "tensor"), None),
    P(("dp", "tensor"), None),
    P("dp", "tensor"),
    P("dp", "tensor"),
    P("dp", "tensor"),
    P("tensor", "dp"),
    P("dp", "tensor"),
    P("tensor", "dp"),
    P("tensor"),
    P("tensor"),
    P(),
    P("tensor"),
    P(),
    P(),
    P(),
    P(None, "tensor"),
    P(None, "tensor"),
    P(),
    P(),
    P(),
    P(),
    P("dp"),
    P("dp"),
)
OUT_SPECS = (
    P(("dp", "tensor"), None),
    P(("dp", "tensor"), None),
    P(None, "tensor"),
    P(None, "tensor"),
)


def solution(mesh):
    grid = (mesh.shape["dp"], mesh.shape["tensor"])
    layer = functools.partial(body, grid)
    return jax.shard_map(layer, mesh=mesh, in_specs=IN_SPECS, out_specs=OUT_SPECS, check_vma=False)
```

```python
import functools

import jax
import jax.numpy as jnp
from jax import lax
from jax.experimental import pallas as pl
from jax.experimental.pallas import tpu as pltpu
from jax.sharding import PartitionSpec as P

HEAD_DIM = 64
ADAPTER_RANK = 8
ADAPTER_NUMER = 16
SEQ = 512
LANES = 128
EPSILON = 1e-05
NEG_FILL = -1e30
WIDE = jnp.float32
NARROW = jnp.bfloat16
ADAPTER_SCALE = ADAPTER_NUMER / ADAPTER_RANK
SCORE_SCALE = HEAD_DIM**-0.5

KEY_SPANS = ((0, 128), (128, 384), (128, 512), (256, 512))
SPAN_STARTS = (0, 128, 384, 768)
SPAN_TOTAL = 1024
BY_MESH = pl.DeviceIdType.MESH

AWAY = {"u1": 3, "u2": 2, "u3": 1, "d1": 1, "d2": 2, "d3": 3}
ARRIVALS = (
    ("X0", "Y0", "D0a", "D0b", "C", "CX0", "CY0", "CD0")
    + tuple(kind + str(k) for kind in ("Z", "X", "Y", "CZ", "CX", "CY", "CD") for k in (1, 2, 3))
    + tuple("D" + str(k) + half for k in (1, 2, 3) for half in "ab")
)
SIGNALS = {name: i for i, name in enumerate(ARRIVALS)}
for name in tuple(kind + str(k) for kind in "ZXY" for k in (1, 2, 3)):
    SIGNALS[name + "-"] = len(SIGNALS)
FROM_CORE = tuple(name for name in ARRIVALS if name[0] == "C")
PASS_ON = {
    "own": [("X0", "x", ""), ("Y0", "y", ""), ("C", "core", "")],
    "ownz": [("Zd1", "+", ""), ("Zu1", "-", "")],
    "X0": [("D0b", "y", "b"), ("CX0", "core", "")],
    "X0z": [("Xd1", "+", ""), ("Xu1", "-", "")],
    "Y0": [("D0a", "x", "a"), ("CY0", "core", "")],
    "Y0z": [("Yd1", "+", ""), ("Yu1", "-", "")],
    "D0a": [],
    "D0b": [("CD0", "core", "")],
}
for away in AWAY:
    onward = "Z" + away[0] + str(int(away[1]) + 1)
    spread_z = [(onward, "+" if away[0] == "d" else "-", "")] if away[1] < "3" else []
    spread_xy = [("X" + away, "x", ""), ("Y" + away, "y", "")] if away[1] > "1" else []
    PASS_ON["Z" + away] = spread_z + spread_xy + [("CZ" + away, "core", "")]
    PASS_ON["X" + away] = [("D" + away + "b", "y", "b"), ("CX" + away, "core", "")]
    PASS_ON["Y" + away] = [("D" + away + "a", "x", "a"), ("CY" + away, "core", "")]
    PASS_ON["D" + away + "a"] = []
    PASS_ON["D" + away + "b"] = [("CD" + away, "core", "")]


STEPS = tuple(PASS_ON)


def steps_of(*codes):
    return [(code // 100, STEPS[code % 100]) for code in codes]


PLAN = {
    "first": {
        0: steps_of(
            1, 0,
        ),
    },
    "start": {
        0: steps_of(
            100, 101, 23, 4, 200, 8, 5, 2, 13, 28, 202, 3, 25, 104,
        ),
    },
    "masked": {
        0: steps_of(
            10, 29, 33, 201, 14, 30, 108, 18, 24, 6, 7, 9, 15, 26, 20, 35, 19, 123, 34, 106, 102,
            223, 31, 11, 204, 12, 16, 208, 21, 27, 17, 22, 32, 36, 37, 113, 128, 105, 103,
        ) + [(0, name) for name in FROM_CORE],
    },
    "project": {
        0: steps_of(
            228, 213,
        ),
        1: steps_of(
            115, 130,
        ),
    },
    "attend": {
        0: steps_of(
            203, 133, 118,
        ),
        2: steps_of(
            125, 129, 206, 107, 114, 110, 131,
        ),
        3: steps_of(
            124, 135, 116, 134, 120, 109, 205, 207, 119,
        ),
    },
    "first_norm": {
        0: steps_of(
            214, 230, 117, 215, 111, 132, 126,
        ),
        1: steps_of(
            136,
        ),
        2: steps_of(
            233, 127, 121,
        ),
        3: steps_of(
            229, 112, 137, 122, 218,
        ),
    },
    "before up": {
        0: steps_of(

        ) + [(1, name) for name in FROM_CORE],
    },
    "up": {
        0: steps_of(
            209,
        ),
        1: steps_of(
            235, 220, 234, 224, 210, 225,
        ),
        2: steps_of(
            219, 231, 216,
        ),
        3: steps_of(
            221, 211, 236, 212, 217, 237, 222, 232, 226, 227,
        ),
    },
    "before down": {
        0: steps_of(

        ) + [(2, name) for name in FROM_CORE],
    },
}


class Gather:
    def __init__(self, blocks, send, recv):
        self.blocks, self.send, self.recv = blocks, send, recv
        self.d, self.t = lax.axis_index("dp"), lax.axis_index("tensor")
        self.depth = blocks[0].shape[1] // 8
        self.z, self.y = self.d // 2, lax.rem(self.d, 2)
        self.tx = lax.rem(self.t + 2, 4)
        self.tc = self.t + 1 - 2 * lax.rem(self.t, 2)
        self.txc = lax.rem(self.tc + 2, 4)

    def peer(self, kind):
        return {
            "x": (self.d, self.tx),
            "y": (self.z * 2 + 1 - self.y, self.t),
            "core": (self.d, self.tc),
            "+": (self.d + 2, self.t),
            "-": (self.d - 2, self.t),
        }[kind]

    def there_is(self, kind):
        if kind[0] in "+u":
            return self.z <= 3 - int(kind[1:] or 1)
        if kind[0] in "-d":
            return self.z >= int(kind[1:] or 1)
        return None

    @staticmethod
    def away(name):
        for away, k in AWAY.items():
            if away in name:
                return away, name.replace(away, str(k))
        return None, name

    def part(self, group, name, half=""):
        away, signal = self.away(name)
        if name.startswith("own"):
            dp, t = self.d, self.t
        elif name == "C":
            dp, t = self.d, self.tc
        else:
            bare = signal.rstrip("abz")
            half = half or signal[len(bare) :].strip("z")
            kind, k = bare[-2], int(bare[-1])
            if away:
                plane = self.z + int(away[1]) if away[0] == "u" else self.z - int(away[1])
            else:
                plane = lax.rem(self.z - k + 4, 4) if k else self.z
            near, far = (self.tc, self.txc) if name[0] == "C" else (self.t, self.tx)
            dp = plane * 2 + (self.y if kind in "ZX" else 1 - self.y)
            t = near if kind in "ZY" else far
        size = self.depth // 2 if half else self.depth
        first = dp * self.depth + (size if half == "b" else 0)
        return self.blocks[group].at[t, pl.ds(pl.multiple_of(first, 16), size), :]

    def copy(self, group, part, name, to):
        signal = self.away(name)[1]
        return pltpu.make_async_remote_copy(
            src_ref=part,
            dst_ref=part,
            send_sem=self.send.at[group, SIGNALS[signal + "-" if to == "-" else signal]],
            recv_sem=self.recv.at[group, SIGNALS[signal]],
            device_id=self.peer(to),
            device_id_type=BY_MESH,
        )

    def when(self, kind, body):
        there = self.there_is(kind) if kind else None
        if there is None:
            body()
        else:
            pl.when(there)(body)

    def each_copy(self, group, name, act):
        for out, to, half in PASS_ON.get(name, ()):
            source = name[:-1] if name[0] == "D" else name

            def one(out=out, to=to, half=half, source=source):
                act(self.copy(group, self.part(group, source, half), out, to))

            self.when(to, one)

    def step(self, group, name):
        def body():
            if not name.startswith("own") and not name.endswith("z"):
                self.copy(group, self.part(group, name), name, "x").wait_recv()
            self.each_copy(group, name, lambda copy: copy.start())

        self.when(self.away(name)[0], body)

    def finish(self, group):
        for name in PASS_ON:
            self.when(
                self.away(name)[0],
                lambda name=name: self.each_copy(group, name, lambda copy: copy.wait_send()),
            )


def mm(left, right):
    return jnp.dot(left, right, preferred_element_type=WIDE)


def mm_nt(left, right):
    return lax.dot_general(left, right, (((1,), (1,)), ((), ())), preferred_element_type=WIDE)


def mm_tn(left, right):
    return lax.dot_general(left, right, (((0,), (0,)), ((), ())), preferred_element_type=WIDE)


def row_mean(block):
    return jnp.sum(block, axis=-1, keepdims=True) * (1.0 / block.shape[-1])


def gelu_parts(value):
    below = 0.5 + 0.5 * lax.erf(value * 0.7071067811865476)
    bell = jnp.exp(value * value * -0.5) * 0.3989422804014327
    return value * below, below + value * bell


def pair_select(low, high):
    lane = lax.broadcasted_iota(jnp.int32, low.shape, 1)
    return jnp.where(lane < HEAD_DIM, low, pltpu.roll(high, HEAD_DIM, 1))


def kernel(plan, *refs):
    if plan is not None:
        (x_hbm, gout_hbm, wq_ref, wk_ref, wv_ref, wo_ref, up_ref, down_ref, dq_ref, dv_ref, uq_ref, uv_ref) = refs[:12]
        (bq_ref, bv_ref, bup_ref) = refs[12:15]
        vector_refs, (seg_ref, live_ref) = refs[15:21], refs[21:23]
        (out_ref, gin_ref, glq_ref, glv_ref) = refs[23:27]
        (wq, wk, wv, wo, q, k, v, probs, ctx, n1, s1, act, slope, acc, mask, u_t) = refs[27:43]
        (a_ref, b_ref, c_ref, bias, biases, part, near, far) = refs[43:51]
        (send, recv, bias_send, bias_recv, near_send, near_recv, far_send, far_recv) = refs[51:59]
        (x_ref, gout_ref, load) = refs[59:]
    else:
        (x_ref, gout_ref, a_ref, b_ref, c_ref, biases_ref, dq_ref, dv_ref) = refs[:8]
        vector_refs, (seg_ref, live_ref) = refs[8:14], refs[14:16]
        (out_ref, gin_ref, gl_ref) = refs[16:19]
        (wq, wk, wv, wo, q, k, v, probs, ctx, n1, s1, act, slope, acc, mask, u_t, biases) = refs[19:]
    rows, width = x_ref.shape
    seqs = rows // SEQ
    pairs = width // LANES
    groups = a_ref.shape[0]
    out_bias, down_bias, gain1, shift1, gain2, shift2 = (
        jnp.reshape(ref[...], (1, width)) for ref in vector_refs
    )

    if plan is not None:
        gather = Gather((a_ref, b_ref, c_ref), send, recv)
        me_d, me_t = gather.d, gather.t
        dps = width // wq_ref.shape[0]
        depth = wq_ref.shape[0]
        others_t = [lax.rem(me_t + i, groups) for i in range(1, groups)]
        others_d = [lax.rem(me_d + i, dps) for i in range(1, dps)]
        seg_rows = pl.ds(pl.multiple_of(me_t * (rows // LANES), rows // LANES), rows // LANES)
        barrier = pltpu.get_barrier_semaphore()
        neighbours = [(me_d, other) for other in others_t] + [gather.peer("y")]
        for peer in neighbours:
            pl.semaphore_signal(barrier, inc=1, device_id=peer, device_id_type=BY_MESH)
        for kind in "+-":

            @pl.when(gather.there_is(kind))
            def _(kind=kind):
                pl.semaphore_signal(barrier, inc=1, device_id=gather.peer(kind), device_id_type=BY_MESH)

        loads = [
            pltpu.make_async_copy(source, target, load.at[i])
            for i, (source, target) in enumerate(((x_hbm, x_ref), (gout_hbm, gout_ref)))
        ]
        for copy in loads:
            copy.start()

        mine = pl.ds(pl.multiple_of(me_d * depth, depth), depth)
        across = wq_ref.shape[1]
        acc[0:width, 0:across] = mm_tn(dq_ref[...], uq_ref[...])
        acc[0:width, 256 : 256 + across] = mm_tn(dv_ref[...], uv_ref[...])
        query = (wq_ref[...].astype(WIDE) + ADAPTER_SCALE * acc[mine, 0:across]) * SCORE_SCALE
        value = wv_ref[...].astype(WIDE) + ADAPTER_SCALE * acc[mine, 256 : 256 + across]
        key = wk_ref[...].astype(WIDE)
        out_t = jnp.transpose(wo_ref[...].astype(WIDE))
        a_ref[me_t, mine, 0:128] = query[:, 0:128].astype(NARROW)
        a_ref[me_t, mine, 128:256] = key[:, 0:128].astype(NARROW)
        a_ref[me_t, mine, 256:384] = value[:, 0:128].astype(NARROW)
        a_ref[me_t, mine, 384:512] = jnp.concatenate([query[:, 128:], key[:, 128:]], axis=1).astype(NARROW)
        a_ref[me_t, mine, 512:640] = jnp.concatenate([value[:, 128:], out_t[:, 128:]], axis=1).astype(NARROW)
        a_ref[me_t, mine, 640:768] = out_t[:, 0:128].astype(NARROW)
        bias[me_t, 0:1, :] = jnp.reshape(bup_ref[...], (1, width))
        bias[me_t, 1:2, 0:across] = jnp.reshape(bq_ref[...], (1, across)) * SCORE_SCALE
        bias[me_t, 1:2, 256 : 256 + across] = jnp.reshape(bv_ref[...], (1, across))
        outer = lax.rem(gather.z, 3) == 0
        pl.semaphore_wait(barrier, len(neighbours) + jnp.where(outer, 1, 2))

        def bias_copy(i):
            return pltpu.make_async_remote_copy(
                src_ref=bias.at[me_t],
                dst_ref=bias.at[me_t],
                send_sem=bias_send.at[i],
                recv_sem=bias_recv.at[i],
                device_id=(me_d, others_t[i]),
                device_id_type=BY_MESH,
            )

        for group, name in plan.get("first", {0: ()})[0]:
            gather.step(group, name)
        b_ref[me_t, mine, :] = up_ref[...]
        c_ref[me_t, mine, :] = down_ref[...]
        for i in range(len(others_t)):
            bias_copy(i).start()
    else:
        seg_rows = pl.ds(0, rows // LANES)
        biases[...] = biases_ref[...]

    def ticks(place, step=None):
        if plan is None:
            return
        for at, names in plan.get(place, {}).items():
            if step is None:
                for group, name in names:
                    gather.step(group, name)
            else:

                @pl.when(step == at)
                def _():
                    for group, name in names:
                        gather.step(group, name)

    segment_ids = seg_ref[seg_rows, :]
    live_flags = live_ref[seg_rows, :]
    ticks("start")
    place = lax.broadcasted_iota(jnp.int32, (LANES, LANES), 0) == lax.broadcasted_iota(
        jnp.int32, (LANES, LANES), 1
    )
    for seq in range(seqs):
        wide_ids = []
        key_ids = []
        for block in range(4):
            row = seq * 4 + block
            ids = segment_ids[row : row + 1, :].astype(WIDE)
            live = live_flags[row : row + 1, :]
            key = jnp.where(live == 1, ids, -1.0)
            wide_ids.append(ids)
            key_ids.append(jnp.transpose(jnp.broadcast_to(key, (LANES, LANES))))
        for block in range(1, 4):
            start, stop = KEY_SPANS[block]
            for j in range((stop - start) // LANES):
                kb = start // LANES + j
                seen = key_ids[kb] == wide_ids[block]
                if kb == block:
                    seen = seen | place
                at = SPAN_STARTS[block] + j * LANES
                mask[seq, at : at + LANES, :] = jnp.where(seen, 0.0, NEG_FILL)

    if plan is not None:
        loads[0].wait()
    adapters_down = jnp.concatenate([dq_ref[...].astype(WIDE), dv_ref[...].astype(WIDE)], axis=0)
    u_t[...] = mm_nt(adapters_down.astype(NARROW), x_ref[...]).astype(NARROW)

    ticks("masked")

    for group in range(groups):
        at = slice(group * LANES, (group + 1) * LANES)
        wq[:, at] = a_ref[group, :, 0:128]
        wk[:, at] = a_ref[group, :, 128:256]
        wv[:, at] = a_ref[group, :, 256:384]
        wo[:, at] = a_ref[group, :, 640:768]
    for half in range(groups // 2):
        at = slice((groups + half) * LANES, (groups + half + 1) * LANES)
        first = a_ref[2 * half, :, 384:512].astype(WIDE)
        second = a_ref[2 * half + 1, :, 384:512].astype(WIDE)
        wq[:, at] = pair_select(first, second).astype(NARROW)
        wk[:, at] = pair_select(pltpu.roll(first, HEAD_DIM, 1), pltpu.roll(second, HEAD_DIM, 1)).astype(NARROW)
        first = a_ref[2 * half, :, 512:640].astype(WIDE)
        second = a_ref[2 * half + 1, :, 512:640].astype(WIDE)
        wv[:, at] = pair_select(first, second).astype(NARROW)
        wo[:, at] = pair_select(pltpu.roll(first, HEAD_DIM, 1), pltpu.roll(second, HEAD_DIM, 1)).astype(NARROW)

    if plan is not None:
        for i in range(len(others_t)):
            pltpu.make_async_remote_copy(
                src_ref=bias.at[me_t],
                dst_ref=bias.at[lax.rem(me_t + groups - 1 - i, groups)],
                send_sem=bias_send.at[i],
                recv_sem=bias_recv.at[i],
                device_id=(me_d, others_t[i]),
                device_id_type=BY_MESH,
            ).wait_recv()
        for group in range(groups):
            biases[2 + group : 3 + group, :] = bias[group, 0:1, :]
            biases[0:1, group * LANES : (group + 1) * LANES] = bias[group, 1:2, 0:128]
            biases[1:2, group * LANES : (group + 1) * LANES] = bias[group, 1:2, 256:384]
        for half in range(groups // 2):
            at = slice((groups + half) * LANES, (groups + half + 1) * LANES)
            for row, first in ((0, 128), (1, 384)):
                low = jnp.broadcast_to(bias[2 * half, 1:2, first : first + 128], (8, LANES))
                high = jnp.broadcast_to(bias[2 * half + 1, 1:2, first : first + 128], (8, LANES))
                biases[row : row + 1, at] = pair_select(low, high)[0:1]

    def project(step, carry):
        ticks("project", step)
        at = pl.ds(pl.multiple_of(step * 256, 256), 256)
        xs = x_ref[...]
        q[:, at] = (mm(xs, wq[:, at]) + biases[0:1, at]).astype(NARROW)
        k[:, at] = mm(xs, wk[:, at]).astype(NARROW)
        v[:, at] = (mm(xs, wv[:, at]) + biases[1:2, at]).astype(NARROW)
        return carry

    lax.fori_loop(0, width // 256, project, 0)

    lane = lax.broadcasted_iota(jnp.int32, (LANES, LANES), 1)
    together = 3
    steps = seqs * pairs // together

    def stacked(tile):
        none = jnp.zeros_like(tile)
        return jnp.concatenate(
            [jnp.where(lane < HEAD_DIM, tile, none), jnp.where(lane < HEAD_DIM, none, tile)], axis=0
        )

    def merged(tile):
        return jnp.where(lane < HEAD_DIM, tile[:LANES], tile[LANES:]).astype(NARROW)

    def work_of(step):
        items = []
        for one in range(together):
            index = step * together + one
            seq = index // pairs
            base = pl.multiple_of(seq * SEQ, SEQ)
            at = pl.ds(pl.multiple_of((index - seq * pairs) * LANES, LANES), LANES)
            for block, (start, stop) in enumerate(KEY_SPANS):
                here = pl.ds(base + block * LANES, LANES)
                there = pl.ds(base + start, stop - start)
                span = pl.ds(SPAN_STARTS[block], stop - start)
                items.append((index, seq, here, there, at, span, block))
        return items

    def attend(step, carry):
        ticks("attend", step)
        items = work_of(step)
        scores = [mm_nt(k[there, at], stacked(q[here, at])) for _, _, here, there, at, _, _ in items]
        weights = []
        for (index, seq, _, _, _, span, block), score in zip(items, scores):
            if block:
                shade = mask[seq, span, :]
                score = score + jnp.concatenate([shade, shade], axis=1)
            powers = jnp.exp(score - jnp.max(score, axis=0, keepdims=True))
            total = jnp.sum(powers, axis=0, keepdims=True)
            weights.append((powers * (1.0 / total)).astype(NARROW))
            probs[index, span, :] = weights[-1]
        for (_, _, here, there, at, _, _), weight in zip(items, weights):
            ctx[here, at] = merged(mm_tn(weight, v[there, at]))
        return carry

    lax.fori_loop(0, steps, attend, 0)

    def first_norm(step, carry):
        ticks("first_norm", step)
        at = pl.ds(pl.multiple_of(step * 256, 256), 256)
        r = x_ref[at, :].astype(WIDE) + (mm_nt(ctx[at, :], wo[...]) + out_bias)
        centered = r - row_mean(r)
        inverse = lax.rsqrt(row_mean(centered * centered) + EPSILON)
        normed = centered * inverse
        n1[at, :] = normed
        s1[at, :] = inverse
        out_ref[at, :] = (normed * gain1 + shift1).astype(NARROW)
        return carry

    lax.fori_loop(0, rows // 256, first_norm, 0, unroll=2)

    def up(group, carry):
        ticks("up", group)
        for j in range(width // 256):
            cols = slice(j * 256, (j + 1) * 256)
            at = pl.ds(pl.multiple_of(group * width + j * 256, 256), 256)
            inner = mm(out_ref[...], b_ref[group, :, cols]) + biases[pl.ds(2 + group, 1), cols]
            value, grad = gelu_parts(inner)
            act[:, at] = value.astype(NARROW)
            slope[:, at] = grad.astype(NARROW)
        return carry

    ticks("before up")
    lax.fori_loop(0, groups, up, 0)
    ticks("before down")
    if plan is not None:
        loads[1].wait()

    def second_norm(step, carry):
        at = pl.ds(pl.multiple_of(step * 256, 256), 256)
        r = n1[at, :] * gain1 + shift1 + down_bias
        for group in range(groups):
            r = r + mm_nt(act[at, group * width : (group + 1) * width], c_ref[group])
        centered = r - row_mean(r)
        inverse = lax.rsqrt(row_mean(centered * centered) + EPSILON)
        normed = centered * inverse
        out_ref[at, :] = (normed * gain2 + shift2).astype(NARROW)
        e = gout_ref[at, :].astype(WIDE) * gain2
        acc[at, :] = inverse * (e - row_mean(e) - normed * row_mean(e * normed))
        return carry

    lax.fori_loop(0, rows // 256, second_norm, 0, unroll=2)

    def down_back(step, carry):
        at = pl.ds(pl.multiple_of(step * 256, 256), 256)
        second = acc[at, :]
        low = second.astype(NARROW)
        total = second
        for group in range(groups):
            cols = slice(group * width, (group + 1) * width)
            grad = (mm(low, c_ref[group]) * slope[at, cols].astype(WIDE)).astype(NARROW)
            total = total + mm_nt(grad, b_ref[group])
        normed = n1[at, :]
        e = total * gain1
        first = s1[at, :] * (e - row_mean(e) - normed * row_mean(e * normed))
        acc[at, :] = first
        ctx[at, :] = mm(first.astype(NARROW), wo[...]).astype(NARROW)
        return carry

    lax.fori_loop(0, rows // 256, down_back, 0, unroll=2)

    def attend_back(step, carry):
        items = work_of(step)
        grads = [stacked(ctx[here, at]) for _, _, here, _, at, _, _ in items]
        rows_q = [stacked(q[here, at]) for _, _, here, _, at, _, _ in items]
        grad_q, grad_k, grad_v = [], {}, {}
        for n, (index, seq, here, there, at, span, block) in enumerate(items):
            weights = probs[index, span, :]
            part = weights.astype(WIDE) * mm_nt(v[there, at], grads[n])
            inside = jnp.sum(part, axis=0, keepdims=True)
            grad_scores = (part - weights.astype(WIDE) * inside).astype(NARROW)
            for_keys = mm(grad_scores, rows_q[n])
            for_values = mm(weights, grads[n])
            grad_q.append(merged(mm_tn(grad_scores, k[there, at])))
            start, stop = KEY_SPANS[block]
            for j in range((stop - start) // LANES):
                rows_here = slice(j * LANES, (j + 1) * LANES)
                key = n // 4, start // LANES + j
                for grad, more in ((grad_k, for_keys), (grad_v, for_values)):
                    grad[key] = grad[key] + more[rows_here] if key in grad else more[rows_here]
        for (_, _, here, _, at, _, _), grad in zip(items, grad_q):
            q[here, at] = grad
        for one, kb in grad_k:
            _, _, here, _, at, _, _ = items[4 * one + kb]
            k[here, at] = grad_k[one, kb].astype(NARROW)
            v[here, at] = grad_v[one, kb].astype(NARROW)
        return carry

    lax.fori_loop(0, steps, attend_back, 0)

    grad_q = mm(u_t[0:8, :], q[...]) * (ADAPTER_SCALE * SCORE_SCALE)
    grad_v = mm(u_t[8:16, :], v[...]) * ADAPTER_SCALE

    def input_back(step, carry):
        at = pl.ds(pl.multiple_of(step * 256, 256), 256)
        total = acc[at, :] + mm_nt(q[at, :], wq[...])
        total = total + mm_nt(k[at, :], wk[...])
        total = total + mm_nt(v[at, :], wv[...])
        gin_ref[at, :] = total.astype(NARROW)
        return carry

    if plan is None:
        gl_ref[0:8, :] = grad_q
        gl_ref[8:16, :] = grad_v
        lax.fori_loop(0, rows // 256, input_back, 0)
        return

    for group in range(groups):
        for row, grad in ((0, grad_q), (8, grad_v)):
            part[group, row : row + 8, 0:128] = grad[:, group * LANES : (group + 1) * LANES]
            other = groups + group // 2
            part[group, row : row + 8, 128:256] = grad[:, other * LANES : (other + 1) * LANES]

    def near_copy(i, slot):
        return pltpu.make_async_remote_copy(
            src_ref=part.at[others_t[i]],
            dst_ref=near.at[slot],
            send_sem=near_send.at[i],
            recv_sem=near_recv.at[i],
            device_id=(me_d, others_t[i]),
            device_id_type=BY_MESH,
        )

    def far_copy(i, slot):
        return pltpu.make_async_remote_copy(
            src_ref=far.at[me_d],
            dst_ref=far.at[slot],
            send_sem=far_send.at[i],
            recv_sem=far_recv.at[i],
            device_id=(others_d[i], me_t),
            device_id_type=BY_MESH,
        )

    for i in range(len(others_t)):
        near_copy(i, i).start()
    lax.fori_loop(0, rows // 512, input_back, 0)
    total = part[me_t]
    for i in range(len(others_t)):
        near_copy(i, i).wait_recv()
        total = total + near[i]
    far[me_d] = total
    for i in range(len(others_d)):
        far_copy(i, me_d).start()
    lax.fori_loop(rows // 512, rows // 256, input_back, 0)
    for group in range(3):
        gather.finish(group)
    for i in range(len(others_t)):
        bias_copy(i).wait_send()
        near_copy(i, i).wait_send()
    for i in range(len(others_d)):
        far_copy(i, lax.rem(me_d + dps - 1 - i, dps)).wait_recv()
    total = far[0]
    for i in range(1, dps):
        total = total + far[i]
    last = jnp.where(lax.rem(me_t, 2) == 0, total[:, 128:], pltpu.roll(total[:, 128:], HEAD_DIM, 1))
    glq_ref[:, 0:128] = total[0:8, 0:128]
    glv_ref[:, 0:128] = total[8:16, 0:128]
    glq_ref[:, 128:192] = last[0:8, 0:HEAD_DIM]
    glv_ref[:, 128:192] = last[8:16, 0:HEAD_DIM]
    for i in range(len(others_d)):
        far_copy(i, me_d).wait_send()


def scratch(rows, width, hidden):
    pairs = width // LANES
    seqs = rows // SEQ
    square = pltpu.VMEM((width, width), NARROW)
    plane = pltpu.VMEM((rows, width), NARROW)
    return [
        square,
        square,
        square,
        square,
        plane,
        plane,
        plane,
        pltpu.VMEM((seqs * pairs, SPAN_TOTAL, 2 * LANES), NARROW),
        plane,
        pltpu.VMEM((rows, width), WIDE),
        pltpu.VMEM((rows, 1), WIDE),
        pltpu.VMEM((rows, hidden), NARROW),
        pltpu.VMEM((rows, hidden), NARROW),
        pltpu.VMEM((rows, width), WIDE),
        pltpu.VMEM((seqs, SPAN_TOTAL, LANES), WIDE),
        pltpu.VMEM((2 * ADAPTER_RANK, rows), NARROW),
    ]


def run_layer(x, gout, a, b, c, biases, downs, vectors, seg, live):
    rows, width = x.shape
    shape = jax.ShapeDtypeStruct
    hidden = b.shape[0] * b.shape[2]
    return pl.pallas_call(
        functools.partial(kernel, None),
        out_shape=(
            shape((rows, width), NARROW),
            shape((rows, width), NARROW),
            shape((2 * ADAPTER_RANK, width), WIDE),
        ),
        in_specs=[pl.BlockSpec(memory_space=pltpu.VMEM)] * 16,
        out_specs=[pl.BlockSpec(memory_space=pltpu.VMEM)] * 3,
        scratch_shapes=scratch(rows, width, hidden) + [pltpu.VMEM((8, width), WIDE)],
        compiler_params=pltpu.CompilerParams(vmem_limit_bytes=63 << 20),
    )(x, gout, a, b, c, biases, *downs, *vectors, seg, live)


def run_layer_and_gather(x, gout, blocks, adapters, biases, vectors, seg, live):
    rows, width = x.shape
    groups = width // blocks[0].shape[1]
    dps = width // blocks[0].shape[0]
    gathered = pltpu.VMEM((groups, width, width), NARROW)
    signals = pltpu.SemaphoreType.DMA
    operands = (x, gout, *blocks, *adapters, *biases, *vectors, seg, live)
    return pl.pallas_call(
        functools.partial(kernel, PLAN),
        out_shape=(
            pltpu.VMEM((rows, width), NARROW),
            pltpu.VMEM((rows, width), NARROW),
            pltpu.VMEM((ADAPTER_RANK, width // groups), WIDE),
            pltpu.VMEM((ADAPTER_RANK, width // groups), WIDE),
        ),
        in_specs=[pl.BlockSpec(memory_space=pl.ANY)] * 2
        + [pl.BlockSpec(memory_space=pltpu.VMEM)] * (len(operands) - 2),
        out_specs=[pl.BlockSpec(memory_space=pltpu.VMEM)] * 4,
        scratch_shapes=scratch(rows, width, groups * width)
        + [
            gathered,
            gathered,
            gathered,
            pltpu.VMEM((groups, 8, width), WIDE),
            pltpu.VMEM((8, width), WIDE),
            pltpu.VMEM((groups, 2 * ADAPTER_RANK, 2 * LANES), WIDE),
            pltpu.VMEM((groups - 1, 2 * ADAPTER_RANK, 2 * LANES), WIDE),
            pltpu.VMEM((dps, 2 * ADAPTER_RANK, 2 * LANES), WIDE),
            signals((3, len(SIGNALS))),
            signals((3, len(SIGNALS))),
            signals((groups - 1,)),
            signals((groups - 1,)),
            signals((groups - 1,)),
            signals((groups - 1,)),
            signals((dps - 1,)),
            signals((dps - 1,)),
            pltpu.VMEM((rows, width), NARROW),
            pltpu.VMEM((rows, width), NARROW),
            signals((2,)),
        ],
        compiler_params=pltpu.CompilerParams(
            collective_id=0, has_side_effects=True, vmem_limit_bytes=59 << 20
        ),
    )(*operands)


def in_pairs(block, groups):
    parts = block.reshape(block.shape[0], groups, 3, HEAD_DIM)
    front = parts[:, :, :2].reshape(block.shape[0], -1)
    return jnp.concatenate([front, parts[:, :, 2].reshape(block.shape[0], -1)], axis=1)


def from_pairs(block, groups):
    front = block[:, : groups * LANES].reshape(block.shape[0], groups, 2, HEAD_DIM)
    back = block[:, groups * LANES :].reshape(block.shape[0], groups, 1, HEAD_DIM)
    return jnp.concatenate([front, back], axis=2).reshape(block.shape[0], -1)


def body(
    grid,
    layer_input_rows,
    output_gradient,
    query_weight,
    key_weight,
    value_weight,
    output_weight,
    up_weight,
    down_weight,
    query_bias_vector,
    value_bias_vector,
    output_bias_vector,
    up_bias_vector,
    down_bias_vector,
    query_down_frozen,
    value_down_frozen,
    query_up_trained,
    value_up_trained,
    first_norm_gain,
    first_norm_bias,
    second_norm_gain,
    second_norm_bias,
    segments,
    sentence_row_mask,
):
    everyone = ("tensor", "dp")
    rows, width = layer_input_rows.shape
    depth, across = query_weight.shape
    groups = width // across
    vectors = (
        output_bias_vector,
        down_bias_vector,
        first_norm_gain,
        first_norm_bias,
        second_norm_gain,
        second_norm_bias,
    )
    downs = (query_down_frozen.T, value_down_frozen.T)
    segment_rows = segments.reshape(-1, LANES)
    live_rows = sentence_row_mask.reshape(-1, LANES)
    if grid == (8, 4):
        return run_layer_and_gather(
            layer_input_rows,
            output_gradient,
            (query_weight, key_weight, value_weight, output_weight, up_weight, down_weight.T),
            (*downs, query_up_trained, value_up_trained),
            (query_bias_vector, value_bias_vector, up_bias_vector),
            vectors,
            segment_rows,
            live_rows,
        )

    place = lax.axis_index("tensor")
    which = lax.axis_index("dp")

    def folded(weight, down, up):
        own = lax.dynamic_slice_in_dim(down, which * depth, depth, axis=0)
        return weight.astype(WIDE) + ADAPTER_SCALE * mm(own, up)

    wq = (folded(query_weight, query_down_frozen, query_up_trained) * SCORE_SCALE).astype(NARROW)
    wv = folded(value_weight, value_down_frozen, value_up_trained).astype(NARROW)
    wk = key_weight
    wo = output_weight.T
    block_a = jnp.concatenate(
        [wq[:, :128], wk[:, :128], wv[:, :128], wq[:, 128:], wk[:, 128:], wv[:, 128:], wo[:, 128:], wo[:, :128]],
        axis=1,
    )

    def spread(block):
        return lax.all_gather(block, everyone, axis=0, tiled=True).reshape(groups, width, width)

    a, b, c = spread(block_a), spread(up_weight), spread(down_weight.T)
    query_bias = lax.all_gather(query_bias_vector * SCORE_SCALE, "tensor", axis=0, tiled=True)
    value_bias = lax.all_gather(value_bias_vector, "tensor", axis=0, tiled=True)
    up_bias = lax.all_gather(up_bias_vector, "tensor", axis=0, tiled=True)
    biases = jnp.concatenate(
        [
            in_pairs(query_bias[None], groups),
            in_pairs(value_bias[None], groups),
            up_bias.reshape(groups, width),
            jnp.zeros((6 - groups, width), WIDE),
        ],
        axis=0,
    )
    blocks = rows // LANES
    seg = lax.dynamic_slice_in_dim(segment_rows, place * blocks, blocks)
    live = lax.dynamic_slice_in_dim(live_rows, place * blocks, blocks)
    output, grad_input, grads = run_layer(
        layer_input_rows, output_gradient, a, b, c, biases, downs, vectors, seg, live
    )
    grads = from_pairs(lax.psum(grads, everyone), groups)
    grads = lax.dynamic_slice_in_dim(grads, place * across, across, axis=1)
    return output, grad_input, grads[:ADAPTER_RANK], grads[ADAPTER_RANK:]


IN_SPECS = (
    P(("dp", "tensor"), None),
    P(("dp", "tensor"), None),
    P("dp", "tensor"),
    P("dp", "tensor"),
    P("dp", "tensor"),
    P("tensor", "dp"),
    P("dp", "tensor"),
    P("tensor", "dp"),
    P("tensor"),
    P("tensor"),
    P(),
    P("tensor"),
    P(),
    P(),
    P(),
    P(None, "tensor"),
    P(None, "tensor"),
    P(),
    P(),
    P(),
    P(),
    P("dp"),
    P("dp"),
)
OUT_SPECS = (
    P(("dp", "tensor"), None),
    P(("dp", "tensor"), None),
    P(None, "tensor"),
    P(None, "tensor"),
)


def solution(mesh):
    grid = (mesh.shape["dp"], mesh.shape["tensor"])
    layer = functools.partial(body, grid)
    return jax.shard_map(layer, mesh=mesh, in_specs=IN_SPECS, out_specs=OUT_SPECS, check_vma=False)
```

```python
import functools

import jax
import jax.numpy as jnp
from jax import lax
from jax.experimental import pallas as pl
from jax.experimental.pallas import tpu as pltpu
from jax.sharding import PartitionSpec as P

HEAD_DIM = 64
ADAPTER_RANK = 8
ADAPTER_NUMER = 16
SEQ = 512
LANES = 128
EPSILON = 1e-05
NEG_FILL = -1e30
WIDE = jnp.float32
NARROW = jnp.bfloat16
ADAPTER_SCALE = ADAPTER_NUMER / ADAPTER_RANK
SCORE_SCALE = HEAD_DIM**-0.5

KEY_SPANS = ((0, 128), (128, 384), (128, 512), (256, 512))
SPAN_STARTS = (0, 128, 384, 768)
SPAN_TOTAL = 1024
BY_MESH = pl.DeviceIdType.MESH

AWAY = {"u1": 3, "u2": 2, "u3": 1, "d1": 1, "d2": 2, "d3": 3}
ARRIVALS = (
    ("X0", "Y0", "D0a", "D0b", "C", "CX0", "CY0", "CD0")
    + tuple(kind + str(k) for kind in ("Z", "X", "Y", "CZ", "CX", "CY", "CD") for k in (1, 2, 3))
    + tuple("D" + str(k) + half for k in (1, 2, 3) for half in "ab")
)
SIGNALS = {name: i for i, name in enumerate(ARRIVALS)}
for name in tuple(kind + str(k) for kind in "ZXY" for k in (1, 2, 3)):
    SIGNALS[name + "-"] = len(SIGNALS)
FROM_CORE = tuple(name for name in ARRIVALS if name[0] == "C")
PASS_ON = {
    "own": [("X0", "x", ""), ("Y0", "y", ""), ("C", "core", "")],
    "ownz": [("Zd1", "+", ""), ("Zu1", "-", "")],
    "X0": [("D0b", "y", "b"), ("CX0", "core", "")],
    "X0z": [("Xd1", "+", ""), ("Xu1", "-", "")],
    "Y0": [("D0a", "x", "a"), ("CY0", "core", "")],
    "Y0z": [("Yd1", "+", ""), ("Yu1", "-", "")],
    "D0a": [],
    "D0b": [("CD0", "core", "")],
}
for away in AWAY:
    onward = "Z" + away[0] + str(int(away[1]) + 1)
    spread_z = [(onward, "+" if away[0] == "d" else "-", "")] if away[1] < "3" else []
    spread_xy = [("X" + away, "x", ""), ("Y" + away, "y", "")] if away[1] > "1" else []
    PASS_ON["Z" + away] = spread_z + spread_xy + [("CZ" + away, "core", "")]
    PASS_ON["X" + away] = [("D" + away + "b", "y", "b"), ("CX" + away, "core", "")]
    PASS_ON["Y" + away] = [("D" + away + "a", "x", "a"), ("CY" + away, "core", "")]
    PASS_ON["D" + away + "a"] = []
    PASS_ON["D" + away + "b"] = [("CD" + away, "core", "")]


STEPS = tuple(PASS_ON)


def steps_of(*codes):
    return [(code // 100, STEPS[code % 100]) for code in codes]


PLAN = {
    "first": {
        0: steps_of(
            1, 0,
        ),
    },
    "start": {
        0: steps_of(
            100, 101, 23, 4, 200, 8, 5, 2, 13, 28, 202, 3, 25, 104,
        ),
    },
    "masked": {
        0: steps_of(
            10, 29, 33, 201, 14, 30, 108, 18, 24, 6, 7, 9, 15, 26, 20, 35, 19, 123, 34, 106, 102,
            223, 31, 11, 204, 12, 16, 208, 21, 27, 17, 22, 32, 36, 37, 113, 128, 105, 103,
        ) + [(0, name) for name in FROM_CORE],
    },
    "project": {
        0: steps_of(
            228, 213,
        ),
        1: steps_of(
            115, 130,
        ),
    },
    "attend": {
        0: steps_of(
            203, 133, 118,
        ),
        2: steps_of(
            125, 129, 206, 107, 114, 110, 131,
        ),
        3: steps_of(
            124, 135, 116, 134, 120, 109, 205, 207, 119,
        ),
    },
    "first_norm": {
        0: steps_of(
            214, 230, 117, 215, 111, 132, 126,
        ),
        1: steps_of(
            136,
        ),
        2: steps_of(
            233, 127, 121,
        ),
        3: steps_of(
            229, 112, 137, 122, 218,
        ),
    },
    "before up": {
        0: steps_of(

        ) + [(1, name) for name in FROM_CORE],
    },
    "up": {
        0: steps_of(
            209,
        ),
        1: steps_of(
            235, 220, 234, 224, 210, 225,
        ),
        2: steps_of(
            219, 231, 216,
        ),
        3: steps_of(
            221, 211, 236, 212, 217, 237, 222, 232, 226, 227,
        ),
    },
    "before down": {
        0: steps_of(

        ) + [(2, name) for name in FROM_CORE],
    },
}


class Gather:
    def __init__(self, blocks, send, recv):
        self.blocks, self.send, self.recv = blocks, send, recv
        self.d, self.t = lax.axis_index("dp"), lax.axis_index("tensor")
        self.depth = blocks[0].shape[1] // 8
        self.z, self.y = self.d // 2, lax.rem(self.d, 2)
        self.tx = lax.rem(self.t + 2, 4)
        self.tc = self.t + 1 - 2 * lax.rem(self.t, 2)
        self.txc = lax.rem(self.tc + 2, 4)

    def peer(self, kind):
        return {
            "x": (self.d, self.tx),
            "y": (self.z * 2 + 1 - self.y, self.t),
            "core": (self.d, self.tc),
            "+": (self.d + 2, self.t),
            "-": (self.d - 2, self.t),
        }[kind]

    def there_is(self, kind):
        if kind[0] in "+u":
            return self.z <= 3 - int(kind[1:] or 1)
        if kind[0] in "-d":
            return self.z >= int(kind[1:] or 1)
        return None

    @staticmethod
    def away(name):
        for away, k in AWAY.items():
            if away in name:
                return away, name.replace(away, str(k))
        return None, name

    def part(self, group, name, half=""):
        away, signal = self.away(name)
        if name.startswith("own"):
            dp, t = self.d, self.t
        elif name == "C":
            dp, t = self.d, self.tc
        else:
            bare = signal.rstrip("abz")
            half = half or signal[len(bare) :].strip("z")
            kind, k = bare[-2], int(bare[-1])
            if away:
                plane = self.z + int(away[1]) if away[0] == "u" else self.z - int(away[1])
            else:
                plane = lax.rem(self.z - k + 4, 4) if k else self.z
            near, far = (self.tc, self.txc) if name[0] == "C" else (self.t, self.tx)
            dp = plane * 2 + (self.y if kind in "ZX" else 1 - self.y)
            t = near if kind in "ZY" else far
        size = self.depth // 2 if half else self.depth
        first = dp * self.depth + (size if half == "b" else 0)
        return self.blocks[group].at[t, pl.ds(pl.multiple_of(first, 16), size), :]

    def copy(self, group, part, name, to):
        signal = self.away(name)[1]
        return pltpu.make_async_remote_copy(
            src_ref=part,
            dst_ref=part,
            send_sem=self.send.at[group, SIGNALS[signal + "-" if to == "-" else signal]],
            recv_sem=self.recv.at[group, SIGNALS[signal]],
            device_id=self.peer(to),
            device_id_type=BY_MESH,
        )

    def when(self, kind, body):
        there = self.there_is(kind) if kind else None
        if there is None:
            body()
        else:
            pl.when(there)(body)

    def each_copy(self, group, name, act):
        for out, to, half in PASS_ON.get(name, ()):
            source = name[:-1] if name[0] == "D" else name

            def one(out=out, to=to, half=half, source=source):
                act(self.copy(group, self.part(group, source, half), out, to))

            self.when(to, one)

    def step(self, group, name):
        def body():
            if not name.startswith("own") and not name.endswith("z"):
                self.copy(group, self.part(group, name), name, "x").wait_recv()
            self.each_copy(group, name, lambda copy: copy.start())

        self.when(self.away(name)[0], body)

    def finish(self, group):
        for name in PASS_ON:
            self.when(
                self.away(name)[0],
                lambda name=name: self.each_copy(group, name, lambda copy: copy.wait_send()),
            )


def mm(left, right):
    return jnp.dot(left, right, preferred_element_type=WIDE)


def mm_nt(left, right):
    return lax.dot_general(left, right, (((1,), (1,)), ((), ())), preferred_element_type=WIDE)


def mm_tn(left, right):
    return lax.dot_general(left, right, (((0,), (0,)), ((), ())), preferred_element_type=WIDE)


def row_mean(block):
    return jnp.sum(block, axis=-1, keepdims=True) * (1.0 / block.shape[-1])


def gelu_parts(value):
    below = 0.5 + 0.5 * lax.erf(value * 0.7071067811865476)
    bell = jnp.exp(value * value * -0.5) * 0.3989422804014327
    return value * below, below + value * bell


def pair_select(low, high):
    lane = lax.broadcasted_iota(jnp.int32, low.shape, 1)
    return jnp.where(lane < HEAD_DIM, low, pltpu.roll(high, HEAD_DIM, 1))


def kernel(plan, *refs):
    if plan is not None:
        (x_hbm, gout_hbm, wq_ref, wk_ref, wv_ref, wo_ref, up_ref, down_ref, dq_ref, dv_ref, uq_ref, uv_ref) = refs[:12]
        (bq_ref, bv_ref, bup_ref) = refs[12:15]
        vector_refs, (seg_ref, live_ref) = refs[15:21], refs[21:23]
        (out_ref, gin_ref, glq_ref, glv_ref) = refs[23:27]
        (wq, wk, wv, wo, q, k, v, probs, ctx, n1, s1, act, slope, acc, mask, u_t) = refs[27:43]
        (a_ref, b_ref, c_ref, bias, biases, part, near, far) = refs[43:51]
        (send, recv, bias_send, bias_recv, near_send, near_recv, far_send, far_recv) = refs[51:59]
        (x_ref, gout_ref, load) = refs[59:]
    else:
        (x_ref, gout_ref, a_ref, b_ref, c_ref, biases_ref, dq_ref, dv_ref) = refs[:8]
        vector_refs, (seg_ref, live_ref) = refs[8:14], refs[14:16]
        (out_ref, gin_ref, gl_ref) = refs[16:19]
        (wq, wk, wv, wo, q, k, v, probs, ctx, n1, s1, act, slope, acc, mask, u_t, biases) = refs[19:]
    rows, width = x_ref.shape
    seqs = rows // SEQ
    pairs = width // LANES
    groups = a_ref.shape[0]
    out_bias, down_bias, gain1, shift1, gain2, shift2 = (
        jnp.reshape(ref[...], (1, width)) for ref in vector_refs
    )

    if plan is not None:
        gather = Gather((a_ref, b_ref, c_ref), send, recv)
        me_d, me_t = gather.d, gather.t
        dps = width // wq_ref.shape[0]
        depth = wq_ref.shape[0]
        others_t = [lax.rem(me_t + i, groups) for i in range(1, groups)]
        others_d = [lax.rem(me_d + i, dps) for i in range(1, dps)]
        seg_rows = pl.ds(pl.multiple_of(me_t * (rows // LANES), rows // LANES), rows // LANES)
        barrier = pltpu.get_barrier_semaphore()
        neighbours = [(me_d, other) for other in others_t] + [gather.peer("y")]
        for peer in neighbours:
            pl.semaphore_signal(barrier, inc=1, device_id=peer, device_id_type=BY_MESH)
        for kind in "+-":

            @pl.when(gather.there_is(kind))
            def _(kind=kind):
                pl.semaphore_signal(barrier, inc=1, device_id=gather.peer(kind), device_id_type=BY_MESH)

        loads = [
            pltpu.make_async_copy(source, target, load.at[i])
            for i, (source, target) in enumerate(((x_hbm, x_ref), (gout_hbm, gout_ref)))
        ]
        for copy in loads:
            copy.start()

        mine = pl.ds(pl.multiple_of(me_d * depth, depth), depth)
        across = wq_ref.shape[1]
        acc[0:width, 0:across] = mm_tn(dq_ref[...], uq_ref[...])
        acc[0:width, 256 : 256 + across] = mm_tn(dv_ref[...], uv_ref[...])
        query = (wq_ref[...].astype(WIDE) + ADAPTER_SCALE * acc[mine, 0:across]) * SCORE_SCALE
        value = wv_ref[...].astype(WIDE) + ADAPTER_SCALE * acc[mine, 256 : 256 + across]
        key = wk_ref[...].astype(WIDE)
        out_t = jnp.transpose(wo_ref[...].astype(WIDE))
        a_ref[me_t, mine, 0:128] = query[:, 0:128].astype(NARROW)
        a_ref[me_t, mine, 128:256] = key[:, 0:128].astype(NARROW)
        a_ref[me_t, mine, 256:384] = value[:, 0:128].astype(NARROW)
        a_ref[me_t, mine, 384:512] = jnp.concatenate([query[:, 128:], key[:, 128:]], axis=1).astype(NARROW)
        a_ref[me_t, mine, 512:640] = jnp.concatenate([value[:, 128:], out_t[:, 128:]], axis=1).astype(NARROW)
        a_ref[me_t, mine, 640:768] = out_t[:, 0:128].astype(NARROW)
        bias[me_t, 0:1, :] = jnp.reshape(bup_ref[...], (1, width))
        bias[me_t, 1:2, 0:across] = jnp.reshape(bq_ref[...], (1, across)) * SCORE_SCALE
        bias[me_t, 1:2, 256 : 256 + across] = jnp.reshape(bv_ref[...], (1, across))
        outer = lax.rem(gather.z, 3) == 0
        pl.semaphore_wait(barrier, len(neighbours) + jnp.where(outer, 1, 2))

        def bias_copy(i):
            return pltpu.make_async_remote_copy(
                src_ref=bias.at[me_t],
                dst_ref=bias.at[me_t],
                send_sem=bias_send.at[i],
                recv_sem=bias_recv.at[i],
                device_id=(me_d, others_t[i]),
                device_id_type=BY_MESH,
            )

        for group, name in plan.get("first", {0: ()})[0]:
            gather.step(group, name)
        b_ref[me_t, mine, :] = up_ref[...]
        c_ref[me_t, mine, :] = down_ref[...]
        for i in range(len(others_t)):
            bias_copy(i).start()
    else:
        seg_rows = pl.ds(0, rows // LANES)
        biases[...] = biases_ref[...]

    def ticks(place, step=None):
        if plan is None:
            return
        for at, names in plan.get(place, {}).items():
            if step is None:
                for group, name in names:
                    gather.step(group, name)
            else:

                @pl.when(step == at)
                def _():
                    for group, name in names:
                        gather.step(group, name)

    segment_ids = seg_ref[seg_rows, :]
    live_flags = live_ref[seg_rows, :]
    ticks("start")
    place = lax.broadcasted_iota(jnp.int32, (LANES, LANES), 0) == lax.broadcasted_iota(
        jnp.int32, (LANES, LANES), 1
    )
    for seq in range(seqs):
        wide_ids = []
        key_ids = []
        for block in range(4):
            row = seq * 4 + block
            ids = segment_ids[row : row + 1, :].astype(WIDE)
            live = live_flags[row : row + 1, :]
            key = jnp.where(live == 1, ids, -1.0)
            wide_ids.append(ids)
            key_ids.append(jnp.transpose(jnp.broadcast_to(key, (LANES, LANES))))
        for block in range(1, 4):
            start, stop = KEY_SPANS[block]
            for j in range((stop - start) // LANES):
                kb = start // LANES + j
                seen = key_ids[kb] == wide_ids[block]
                if kb == block:
                    seen = seen | place
                at = SPAN_STARTS[block] + j * LANES
                mask[seq, at : at + LANES, :] = jnp.where(seen, 0.0, NEG_FILL)

    if plan is not None:
        loads[0].wait()
    adapters_down = jnp.concatenate([dq_ref[...].astype(WIDE), dv_ref[...].astype(WIDE)], axis=0)
    u_t[...] = mm_nt(adapters_down.astype(NARROW), x_ref[...]).astype(NARROW)

    ticks("masked")

    for group in range(groups):
        at = slice(group * LANES, (group + 1) * LANES)
        wq[:, at] = a_ref[group, :, 0:128]
        wk[:, at] = a_ref[group, :, 128:256]
        wv[:, at] = a_ref[group, :, 256:384]
        wo[:, at] = a_ref[group, :, 640:768]
    for half in range(groups // 2):
        at = slice((groups + half) * LANES, (groups + half + 1) * LANES)
        first = a_ref[2 * half, :, 384:512].astype(WIDE)
        second = a_ref[2 * half + 1, :, 384:512].astype(WIDE)
        wq[:, at] = pair_select(first, second).astype(NARROW)
        wk[:, at] = pair_select(pltpu.roll(first, HEAD_DIM, 1), pltpu.roll(second, HEAD_DIM, 1)).astype(NARROW)
        first = a_ref[2 * half, :, 512:640].astype(WIDE)
        second = a_ref[2 * half + 1, :, 512:640].astype(WIDE)
        wv[:, at] = pair_select(first, second).astype(NARROW)
        wo[:, at] = pair_select(pltpu.roll(first, HEAD_DIM, 1), pltpu.roll(second, HEAD_DIM, 1)).astype(NARROW)

    if plan is not None:
        for i in range(len(others_t)):
            pltpu.make_async_remote_copy(
                src_ref=bias.at[me_t],
                dst_ref=bias.at[lax.rem(me_t + groups - 1 - i, groups)],
                send_sem=bias_send.at[i],
                recv_sem=bias_recv.at[i],
                device_id=(me_d, others_t[i]),
                device_id_type=BY_MESH,
            ).wait_recv()
        for group in range(groups):
            biases[2 + group : 3 + group, :] = bias[group, 0:1, :]
            biases[0:1, group * LANES : (group + 1) * LANES] = bias[group, 1:2, 0:128]
            biases[1:2, group * LANES : (group + 1) * LANES] = bias[group, 1:2, 256:384]
        for half in range(groups // 2):
            at = slice((groups + half) * LANES, (groups + half + 1) * LANES)
            for row, first in ((0, 128), (1, 384)):
                low = jnp.broadcast_to(bias[2 * half, 1:2, first : first + 128], (8, LANES))
                high = jnp.broadcast_to(bias[2 * half + 1, 1:2, first : first + 128], (8, LANES))
                biases[row : row + 1, at] = pair_select(low, high)[0:1]

    def project(step, carry):
        ticks("project", step)
        at = pl.ds(pl.multiple_of(step * 256, 256), 256)
        xs = x_ref[...]
        q[:, at] = (mm(xs, wq[:, at]) + biases[0:1, at]).astype(NARROW)
        k[:, at] = mm(xs, wk[:, at]).astype(NARROW)
        v[:, at] = (mm(xs, wv[:, at]) + biases[1:2, at]).astype(NARROW)
        return carry

    lax.fori_loop(0, width // 256, project, 0)

    lane = lax.broadcasted_iota(jnp.int32, (LANES, LANES), 1)
    together = 3
    steps = seqs * pairs // together

    def stacked(tile):
        none = jnp.zeros_like(tile)
        return jnp.concatenate(
            [jnp.where(lane < HEAD_DIM, tile, none), jnp.where(lane < HEAD_DIM, none, tile)], axis=0
        )

    def merged(tile):
        return jnp.where(lane < HEAD_DIM, tile[:LANES], tile[LANES:]).astype(NARROW)

    def work_of(step, together=together):
        items = []
        for one in range(together):
            index = step * together + one
            seq = index // pairs
            base = pl.multiple_of(seq * SEQ, SEQ)
            at = pl.ds(pl.multiple_of((index - seq * pairs) * LANES, LANES), LANES)
            for block, (start, stop) in enumerate(KEY_SPANS):
                here = pl.ds(base + block * LANES, LANES)
                there = pl.ds(base + start, stop - start)
                span = pl.ds(SPAN_STARTS[block], stop - start)
                items.append((index, seq, here, there, at, span, block))
        return items

    def attend(step, carry):
        ticks("attend", step)
        items = work_of(step)
        scores = [mm_nt(k[there, at], stacked(q[here, at])) for _, _, here, there, at, _, _ in items]
        weights = []
        for (index, seq, _, _, _, span, block), score in zip(items, scores):
            if block:
                shade = mask[seq, span, :]
                score = score + jnp.concatenate([shade, shade], axis=1)
            powers = jnp.exp(score - jnp.max(score, axis=0, keepdims=True))
            total = jnp.sum(powers, axis=0, keepdims=True)
            weights.append((powers * (1.0 / total)).astype(NARROW))
            probs[index, span, :] = weights[-1]
        for (_, _, here, there, at, _, _), weight in zip(items, weights):
            ctx[here, at] = merged(mm_tn(weight, v[there, at]))
        return carry

    lax.fori_loop(0, steps, attend, 0)

    def first_norm(step, carry):
        ticks("first_norm", step)
        at = pl.ds(pl.multiple_of(step * 256, 256), 256)
        r = x_ref[at, :].astype(WIDE) + (mm_nt(ctx[at, :], wo[...]) + out_bias)
        centered = r - row_mean(r)
        inverse = lax.rsqrt(row_mean(centered * centered) + EPSILON)
        normed = centered * inverse
        n1[at, :] = normed
        s1[at, :] = inverse
        out_ref[at, :] = (normed * gain1 + shift1).astype(NARROW)
        return carry

    lax.fori_loop(0, rows // 256, first_norm, 0, unroll=2)

    def up(group, carry):
        ticks("up", group)
        for j in range(width // 256):
            cols = slice(j * 256, (j + 1) * 256)
            at = pl.ds(pl.multiple_of(group * width + j * 256, 256), 256)
            inner = mm(out_ref[...], b_ref[group, :, cols]) + biases[pl.ds(2 + group, 1), cols]
            value, grad = gelu_parts(inner)
            act[:, at] = value.astype(NARROW)
            slope[:, at] = grad.astype(NARROW)
        return carry

    ticks("before up")
    lax.fori_loop(0, groups, up, 0)
    ticks("before down")
    if plan is not None:
        loads[1].wait()

    def second_norm(step, carry):
        at = pl.ds(pl.multiple_of(step * 256, 256), 256)
        r = n1[at, :] * gain1 + shift1 + down_bias
        for group in range(groups):
            r = r + mm_nt(act[at, group * width : (group + 1) * width], c_ref[group])
        centered = r - row_mean(r)
        inverse = lax.rsqrt(row_mean(centered * centered) + EPSILON)
        normed = centered * inverse
        out_ref[at, :] = (normed * gain2 + shift2).astype(NARROW)
        e = gout_ref[at, :].astype(WIDE) * gain2
        acc[at, :] = inverse * (e - row_mean(e) - normed * row_mean(e * normed))
        return carry

    lax.fori_loop(0, rows // 256, second_norm, 0, unroll=2)

    def down_back(step, carry):
        at = pl.ds(pl.multiple_of(step * 256, 256), 256)
        second = acc[at, :]
        low = second.astype(NARROW)
        total = second
        for group in range(groups):
            cols = slice(group * width, (group + 1) * width)
            grad = (mm(low, c_ref[group]) * slope[at, cols].astype(WIDE)).astype(NARROW)
            total = total + mm_nt(grad, b_ref[group])
        normed = n1[at, :]
        e = total * gain1
        first = s1[at, :] * (e - row_mean(e) - normed * row_mean(e * normed))
        acc[at, :] = first
        ctx[at, :] = mm(first.astype(NARROW), wo[...]).astype(NARROW)
        return carry

    lax.fori_loop(0, rows // 256, down_back, 0, unroll=2)

    def attend_back(step, carry):
        items = work_of(step, pairs)
        grads = [stacked(ctx[here, at]) for _, _, here, _, at, _, _ in items]
        rows_q = [stacked(q[here, at]) for _, _, here, _, at, _, _ in items]
        grad_q, grad_k, grad_v = [], {}, {}
        for n, (index, seq, here, there, at, span, block) in enumerate(items):
            weights = probs[index, span, :]
            part = weights.astype(WIDE) * mm_nt(v[there, at], grads[n])
            inside = jnp.sum(part, axis=0, keepdims=True)
            grad_scores = (part - weights.astype(WIDE) * inside).astype(NARROW)
            for_keys = mm(grad_scores, rows_q[n])
            for_values = mm(weights, grads[n])
            grad_q.append(merged(mm_tn(grad_scores, k[there, at])))
            start, stop = KEY_SPANS[block]
            for j in range((stop - start) // LANES):
                rows_here = slice(j * LANES, (j + 1) * LANES)
                key = n // 4, start // LANES + j
                for grad, more in ((grad_k, for_keys), (grad_v, for_values)):
                    grad[key] = grad[key] + more[rows_here] if key in grad else more[rows_here]
        for (_, _, here, _, at, _, _), grad in zip(items, grad_q):
            q[here, at] = grad
        for one, kb in grad_k:
            _, _, here, _, at, _, _ = items[4 * one + kb]
            k[here, at] = grad_k[one, kb].astype(NARROW)
            v[here, at] = grad_v[one, kb].astype(NARROW)
        return carry

    lax.fori_loop(0, seqs, attend_back, 0)

    grad_q = mm(u_t[0:8, :], q[...]) * (ADAPTER_SCALE * SCORE_SCALE)
    grad_v = mm(u_t[8:16, :], v[...]) * ADAPTER_SCALE

    def input_back(step, carry):
        at = pl.ds(pl.multiple_of(step * 256, 256), 256)
        total = acc[at, :] + mm_nt(q[at, :], wq[...])
        total = total + mm_nt(k[at, :], wk[...])
        total = total + mm_nt(v[at, :], wv[...])
        gin_ref[at, :] = total.astype(NARROW)
        return carry

    if plan is None:
        gl_ref[0:8, :] = grad_q
        gl_ref[8:16, :] = grad_v
        lax.fori_loop(0, rows // 256, input_back, 0)
        return

    for group in range(groups):
        for row, grad in ((0, grad_q), (8, grad_v)):
            part[group, row : row + 8, 0:128] = grad[:, group * LANES : (group + 1) * LANES]
            other = groups + group // 2
            part[group, row : row + 8, 128:256] = grad[:, other * LANES : (other + 1) * LANES]

    def near_copy(i, slot):
        return pltpu.make_async_remote_copy(
            src_ref=part.at[others_t[i]],
            dst_ref=near.at[slot],
            send_sem=near_send.at[i],
            recv_sem=near_recv.at[i],
            device_id=(me_d, others_t[i]),
            device_id_type=BY_MESH,
        )

    def far_copy(i, slot):
        return pltpu.make_async_remote_copy(
            src_ref=far.at[me_d],
            dst_ref=far.at[slot],
            send_sem=far_send.at[i],
            recv_sem=far_recv.at[i],
            device_id=(others_d[i], me_t),
            device_id_type=BY_MESH,
        )

    for i in range(len(others_t)):
        near_copy(i, i).start()
    lax.fori_loop(0, rows // 512, input_back, 0)
    total = part[me_t]
    for i in range(len(others_t)):
        near_copy(i, i).wait_recv()
        total = total + near[i]
    far[me_d] = total
    for i in range(len(others_d)):
        far_copy(i, me_d).start()
    lax.fori_loop(rows // 512, rows // 256, input_back, 0)
    for group in range(3):
        gather.finish(group)
    for i in range(len(others_t)):
        bias_copy(i).wait_send()
        near_copy(i, i).wait_send()
    for i in range(len(others_d)):
        far_copy(i, lax.rem(me_d + dps - 1 - i, dps)).wait_recv()
    total = far[0]
    for i in range(1, dps):
        total = total + far[i]
    last = jnp.where(lax.rem(me_t, 2) == 0, total[:, 128:], pltpu.roll(total[:, 128:], HEAD_DIM, 1))
    glq_ref[:, 0:128] = total[0:8, 0:128]
    glv_ref[:, 0:128] = total[8:16, 0:128]
    glq_ref[:, 128:192] = last[0:8, 0:HEAD_DIM]
    glv_ref[:, 128:192] = last[8:16, 0:HEAD_DIM]
    for i in range(len(others_d)):
        far_copy(i, me_d).wait_send()


def scratch(rows, width, hidden):
    pairs = width // LANES
    seqs = rows // SEQ
    square = pltpu.VMEM((width, width), NARROW)
    plane = pltpu.VMEM((rows, width), NARROW)
    return [
        square,
        square,
        square,
        square,
        plane,
        plane,
        plane,
        pltpu.VMEM((seqs * pairs, SPAN_TOTAL, 2 * LANES), NARROW),
        plane,
        pltpu.VMEM((rows, width), WIDE),
        pltpu.VMEM((rows, 1), WIDE),
        pltpu.VMEM((rows, hidden), NARROW),
        pltpu.VMEM((rows, hidden), NARROW),
        pltpu.VMEM((rows, width), WIDE),
        pltpu.VMEM((seqs, SPAN_TOTAL, LANES), WIDE),
        pltpu.VMEM((2 * ADAPTER_RANK, rows), NARROW),
    ]


def run_layer(x, gout, a, b, c, biases, downs, vectors, seg, live):
    rows, width = x.shape
    shape = jax.ShapeDtypeStruct
    hidden = b.shape[0] * b.shape[2]
    return pl.pallas_call(
        functools.partial(kernel, None),
        out_shape=(
            shape((rows, width), NARROW),
            shape((rows, width), NARROW),
            shape((2 * ADAPTER_RANK, width), WIDE),
        ),
        in_specs=[pl.BlockSpec(memory_space=pltpu.VMEM)] * 16,
        out_specs=[pl.BlockSpec(memory_space=pltpu.VMEM)] * 3,
        scratch_shapes=scratch(rows, width, hidden) + [pltpu.VMEM((8, width), WIDE)],
        compiler_params=pltpu.CompilerParams(vmem_limit_bytes=63 << 20),
    )(x, gout, a, b, c, biases, *downs, *vectors, seg, live)


def run_layer_and_gather(x, gout, blocks, adapters, biases, vectors, seg, live):
    rows, width = x.shape
    groups = width // blocks[0].shape[1]
    dps = width // blocks[0].shape[0]
    gathered = pltpu.VMEM((groups, width, width), NARROW)
    signals = pltpu.SemaphoreType.DMA
    operands = (x, gout, *blocks, *adapters, *biases, *vectors, seg, live)
    return pl.pallas_call(
        functools.partial(kernel, PLAN),
        out_shape=(
            pltpu.VMEM((rows, width), NARROW),
            pltpu.VMEM((rows, width), NARROW),
            pltpu.VMEM((ADAPTER_RANK, width // groups), WIDE),
            pltpu.VMEM((ADAPTER_RANK, width // groups), WIDE),
        ),
        in_specs=[pl.BlockSpec(memory_space=pl.ANY)] * 2
        + [pl.BlockSpec(memory_space=pltpu.VMEM)] * (len(operands) - 2),
        out_specs=[pl.BlockSpec(memory_space=pltpu.VMEM)] * 4,
        scratch_shapes=scratch(rows, width, groups * width)
        + [
            gathered,
            gathered,
            gathered,
            pltpu.VMEM((groups, 8, width), WIDE),
            pltpu.VMEM((8, width), WIDE),
            pltpu.VMEM((groups, 2 * ADAPTER_RANK, 2 * LANES), WIDE),
            pltpu.VMEM((groups - 1, 2 * ADAPTER_RANK, 2 * LANES), WIDE),
            pltpu.VMEM((dps, 2 * ADAPTER_RANK, 2 * LANES), WIDE),
            signals((3, len(SIGNALS))),
            signals((3, len(SIGNALS))),
            signals((groups - 1,)),
            signals((groups - 1,)),
            signals((groups - 1,)),
            signals((groups - 1,)),
            signals((dps - 1,)),
            signals((dps - 1,)),
            pltpu.VMEM((rows, width), NARROW),
            pltpu.VMEM((rows, width), NARROW),
            signals((2,)),
        ],
        compiler_params=pltpu.CompilerParams(
            collective_id=0, has_side_effects=True, vmem_limit_bytes=59 << 20
        ),
    )(*operands)


def in_pairs(block, groups):
    parts = block.reshape(block.shape[0], groups, 3, HEAD_DIM)
    front = parts[:, :, :2].reshape(block.shape[0], -1)
    return jnp.concatenate([front, parts[:, :, 2].reshape(block.shape[0], -1)], axis=1)


def from_pairs(block, groups):
    front = block[:, : groups * LANES].reshape(block.shape[0], groups, 2, HEAD_DIM)
    back = block[:, groups * LANES :].reshape(block.shape[0], groups, 1, HEAD_DIM)
    return jnp.concatenate([front, back], axis=2).reshape(block.shape[0], -1)


def body(
    grid,
    layer_input_rows,
    output_gradient,
    query_weight,
    key_weight,
    value_weight,
    output_weight,
    up_weight,
    down_weight,
    query_bias_vector,
    value_bias_vector,
    output_bias_vector,
    up_bias_vector,
    down_bias_vector,
    query_down_frozen,
    value_down_frozen,
    query_up_trained,
    value_up_trained,
    first_norm_gain,
    first_norm_bias,
    second_norm_gain,
    second_norm_bias,
    segments,
    sentence_row_mask,
):
    everyone = ("tensor", "dp")
    rows, width = layer_input_rows.shape
    depth, across = query_weight.shape
    groups = width // across
    vectors = (
        output_bias_vector,
        down_bias_vector,
        first_norm_gain,
        first_norm_bias,
        second_norm_gain,
        second_norm_bias,
    )
    downs = (query_down_frozen.T, value_down_frozen.T)
    segment_rows = segments.reshape(-1, LANES)
    live_rows = sentence_row_mask.reshape(-1, LANES)
    if grid == (8, 4):
        return run_layer_and_gather(
            layer_input_rows,
            output_gradient,
            (query_weight, key_weight, value_weight, output_weight, up_weight, down_weight.T),
            (*downs, query_up_trained, value_up_trained),
            (query_bias_vector, value_bias_vector, up_bias_vector),
            vectors,
            segment_rows,
            live_rows,
        )

    place = lax.axis_index("tensor")
    which = lax.axis_index("dp")

    def folded(weight, down, up):
        own = lax.dynamic_slice_in_dim(down, which * depth, depth, axis=0)
        return weight.astype(WIDE) + ADAPTER_SCALE * mm(own, up)

    wq = (folded(query_weight, query_down_frozen, query_up_trained) * SCORE_SCALE).astype(NARROW)
    wv = folded(value_weight, value_down_frozen, value_up_trained).astype(NARROW)
    wk = key_weight
    wo = output_weight.T
    block_a = jnp.concatenate(
        [wq[:, :128], wk[:, :128], wv[:, :128], wq[:, 128:], wk[:, 128:], wv[:, 128:], wo[:, 128:], wo[:, :128]],
        axis=1,
    )

    def spread(block):
        return lax.all_gather(block, everyone, axis=0, tiled=True).reshape(groups, width, width)

    a, b, c = spread(block_a), spread(up_weight), spread(down_weight.T)
    query_bias = lax.all_gather(query_bias_vector * SCORE_SCALE, "tensor", axis=0, tiled=True)
    value_bias = lax.all_gather(value_bias_vector, "tensor", axis=0, tiled=True)
    up_bias = lax.all_gather(up_bias_vector, "tensor", axis=0, tiled=True)
    biases = jnp.concatenate(
        [
            in_pairs(query_bias[None], groups),
            in_pairs(value_bias[None], groups),
            up_bias.reshape(groups, width),
            jnp.zeros((6 - groups, width), WIDE),
        ],
        axis=0,
    )
    blocks = rows // LANES
    seg = lax.dynamic_slice_in_dim(segment_rows, place * blocks, blocks)
    live = lax.dynamic_slice_in_dim(live_rows, place * blocks, blocks)
    output, grad_input, grads = run_layer(
        layer_input_rows, output_gradient, a, b, c, biases, downs, vectors, seg, live
    )
    grads = from_pairs(lax.psum(grads, everyone), groups)
    grads = lax.dynamic_slice_in_dim(grads, place * across, across, axis=1)
    return output, grad_input, grads[:ADAPTER_RANK], grads[ADAPTER_RANK:]


IN_SPECS = (
    P(("dp", "tensor"), None),
    P(("dp", "tensor"), None),
    P("dp", "tensor"),
    P("dp", "tensor"),
    P("dp", "tensor"),
    P("tensor", "dp"),
    P("dp", "tensor"),
    P("tensor", "dp"),
    P("tensor"),
    P("tensor"),
    P(),
    P("tensor"),
    P(),
    P(),
    P(),
    P(None, "tensor"),
    P(None, "tensor"),
    P(),
    P(),
    P(),
    P(),
    P("dp"),
    P("dp"),
)
OUT_SPECS = (
    P(("dp", "tensor"), None),
    P(("dp", "tensor"), None),
    P(None, "tensor"),
    P(None, "tensor"),
)


def solution(mesh):
    grid = (mesh.shape["dp"], mesh.shape["tensor"])
    layer = functools.partial(body, grid)
    return jax.shard_map(layer, mesh=mesh, in_specs=IN_SPECS, out_specs=OUT_SPECS, check_vma=False)
```

```python
import functools

import jax
import jax.numpy as jnp
from jax import lax
from jax.experimental import pallas as pl
from jax.experimental.pallas import tpu as pltpu
from jax.sharding import PartitionSpec as P

HEAD_DIM = 64
ADAPTER_RANK = 8
ADAPTER_NUMER = 16
SEQ = 512
LANES = 128
EPSILON = 1e-05
NEG_FILL = -1e30
WIDE = jnp.float32
NARROW = jnp.bfloat16
ADAPTER_SCALE = ADAPTER_NUMER / ADAPTER_RANK
SCORE_SCALE = HEAD_DIM**-0.5

KEY_SPANS = ((0, 128), (128, 384), (128, 512), (256, 512))
SPAN_STARTS = (0, 128, 384, 768)
SPAN_TOTAL = 1024
BY_MESH = pl.DeviceIdType.MESH

AWAY = {"u1": 3, "u2": 2, "u3": 1, "d1": 1, "d2": 2, "d3": 3}
ARRIVALS = (
    ("X0", "Y0", "D0a", "D0b", "C", "CX0", "CY0", "CD0")
    + tuple(kind + str(k) for kind in ("Z", "X", "Y", "CZ", "CX", "CY", "CD") for k in (1, 2, 3))
    + tuple("D" + str(k) + half for k in (1, 2, 3) for half in "ab")
)
SIGNALS = {name: i for i, name in enumerate(ARRIVALS)}
for name in tuple(kind + str(k) for kind in "ZXY" for k in (1, 2, 3)):
    SIGNALS[name + "-"] = len(SIGNALS)
FROM_CORE = tuple(name for name in ARRIVALS if name[0] == "C")
PASS_ON = {
    "own": [("X0", "x", ""), ("Y0", "y", ""), ("C", "core", "")],
    "ownz": [("Zd1", "+", ""), ("Zu1", "-", "")],
    "X0": [("D0b", "y", "b"), ("CX0", "core", "")],
    "X0z": [("Xd1", "+", ""), ("Xu1", "-", "")],
    "Y0": [("D0a", "x", "a"), ("CY0", "core", "")],
    "Y0z": [("Yd1", "+", ""), ("Yu1", "-", "")],
    "D0a": [],
    "D0b": [("CD0", "core", "")],
}
for away in AWAY:
    onward = "Z" + away[0] + str(int(away[1]) + 1)
    spread_z = [(onward, "+" if away[0] == "d" else "-", "")] if away[1] < "3" else []
    spread_xy = [("X" + away, "x", ""), ("Y" + away, "y", "")] if away[1] > "1" else []
    PASS_ON["Z" + away] = spread_z + spread_xy + [("CZ" + away, "core", "")]
    PASS_ON["X" + away] = [("D" + away + "b", "y", "b"), ("CX" + away, "core", "")]
    PASS_ON["Y" + away] = [("D" + away + "a", "x", "a"), ("CY" + away, "core", "")]
    PASS_ON["D" + away + "a"] = []
    PASS_ON["D" + away + "b"] = [("CD" + away, "core", "")]


STEPS = tuple(PASS_ON)


def steps_of(*codes):
    return [(code // 100, STEPS[code % 100]) for code in codes]


PLAN = {
    "first": {
        0: steps_of(
            1, 0,
        ),
    },
    "start": {
        0: steps_of(
            100, 101, 23, 4, 200, 8, 5, 2, 13, 28, 202, 3, 25, 104,
        ),
    },
    "masked": {
        0: steps_of(
            10, 29, 33, 201, 14, 30, 108, 18, 24, 6, 7, 9, 15, 26, 20, 35, 19, 123, 34, 106, 102,
            223, 31, 11, 204, 12, 16, 208, 21, 27, 17, 22, 32, 36, 37, 113, 128, 105, 103,
        ) + [(0, name) for name in FROM_CORE],
    },
    "project": {
        0: steps_of(
            228, 213,
        ),
        1: steps_of(
            115, 130,
        ),
    },
    "attend": {
        0: steps_of(
            203, 133, 118,
        ),
        2: steps_of(
            125, 129, 206, 107, 114, 110, 131,
        ),
        3: steps_of(
            124, 135, 116, 134, 120, 109, 205, 207, 119,
        ),
    },
    "first_norm": {
        0: steps_of(
            214, 230, 117, 215, 111, 132, 126,
        ),
        1: steps_of(
            136,
        ),
        2: steps_of(
            233, 127, 121,
        ),
        3: steps_of(
            229, 112, 137, 122, 218,
        ),
    },
    "before up": {
        0: steps_of(

        ) + [(1, name) for name in FROM_CORE],
    },
    "up": {
        0: steps_of(
            209,
        ),
        1: steps_of(
            235, 220, 234, 224, 210, 225,
        ),
        2: steps_of(
            219, 231, 216,
        ),
        3: steps_of(
            221, 211, 236, 212, 217, 237, 222, 232, 226, 227,
        ),
    },
    "before down": {
        0: steps_of(

        ) + [(2, name) for name in FROM_CORE],
    },
}


class Gather:
    def __init__(self, blocks, send, recv):
        self.blocks, self.send, self.recv = blocks, send, recv
        self.d, self.t = lax.axis_index("dp"), lax.axis_index("tensor")
        self.depth = blocks[0].shape[1] // 8
        self.z, self.y = self.d // 2, lax.rem(self.d, 2)
        self.tx = lax.rem(self.t + 2, 4)
        self.tc = self.t + 1 - 2 * lax.rem(self.t, 2)
        self.txc = lax.rem(self.tc + 2, 4)

    def peer(self, kind):
        return {
            "x": (self.d, self.tx),
            "y": (self.z * 2 + 1 - self.y, self.t),
            "core": (self.d, self.tc),
            "+": (self.d + 2, self.t),
            "-": (self.d - 2, self.t),
        }[kind]

    def there_is(self, kind):
        if kind[0] in "+u":
            return self.z <= 3 - int(kind[1:] or 1)
        if kind[0] in "-d":
            return self.z >= int(kind[1:] or 1)
        return None

    @staticmethod
    def away(name):
        for away, k in AWAY.items():
            if away in name:
                return away, name.replace(away, str(k))
        return None, name

    def part(self, group, name, half=""):
        away, signal = self.away(name)
        if name.startswith("own"):
            dp, t = self.d, self.t
        elif name == "C":
            dp, t = self.d, self.tc
        else:
            bare = signal.rstrip("abz")
            half = half or signal[len(bare) :].strip("z")
            kind, k = bare[-2], int(bare[-1])
            if away:
                plane = self.z + int(away[1]) if away[0] == "u" else self.z - int(away[1])
            else:
                plane = lax.rem(self.z - k + 4, 4) if k else self.z
            near, far = (self.tc, self.txc) if name[0] == "C" else (self.t, self.tx)
            dp = plane * 2 + (self.y if kind in "ZX" else 1 - self.y)
            t = near if kind in "ZY" else far
        size = self.depth // 2 if half else self.depth
        first = dp * self.depth + (size if half == "b" else 0)
        return self.blocks[group].at[t, pl.ds(pl.multiple_of(first, 16), size), :]

    def copy(self, group, part, name, to):
        signal = self.away(name)[1]
        return pltpu.make_async_remote_copy(
            src_ref=part,
            dst_ref=part,
            send_sem=self.send.at[group, SIGNALS[signal + "-" if to == "-" else signal]],
            recv_sem=self.recv.at[group, SIGNALS[signal]],
            device_id=self.peer(to),
            device_id_type=BY_MESH,
        )

    def when(self, kind, body):
        there = self.there_is(kind) if kind else None
        if there is None:
            body()
        else:
            pl.when(there)(body)

    def each_copy(self, group, name, act):
        for out, to, half in PASS_ON.get(name, ()):
            source = name[:-1] if name[0] == "D" else name

            def one(out=out, to=to, half=half, source=source):
                act(self.copy(group, self.part(group, source, half), out, to))

            self.when(to, one)

    def step(self, group, name):
        def body():
            if not name.startswith("own") and not name.endswith("z"):
                self.copy(group, self.part(group, name), name, "x").wait_recv()
            self.each_copy(group, name, lambda copy: copy.start())

        self.when(self.away(name)[0], body)

    def finish(self, group):
        for name in PASS_ON:
            self.when(
                self.away(name)[0],
                lambda name=name: self.each_copy(group, name, lambda copy: copy.wait_send()),
            )


def mm(left, right):
    return jnp.dot(left, right, preferred_element_type=WIDE)


def mm_nt(left, right):
    return lax.dot_general(left, right, (((1,), (1,)), ((), ())), preferred_element_type=WIDE)


def mm_tn(left, right):
    return lax.dot_general(left, right, (((0,), (0,)), ((), ())), preferred_element_type=WIDE)


def row_mean(block):
    return jnp.sum(block, axis=-1, keepdims=True) * (1.0 / block.shape[-1])


def gelu_parts(value):
    below = 0.5 + 0.5 * lax.erf(value * 0.7071067811865476)
    bell = jnp.exp(value * value * -0.5) * 0.3989422804014327
    return value * below, below + value * bell


def pair_select(low, high):
    lane = lax.broadcasted_iota(jnp.int32, low.shape, 1)
    return jnp.where(lane < HEAD_DIM, low, pltpu.roll(high, HEAD_DIM, 1))


def kernel(plan, *refs):
    if plan is not None:
        (x_hbm, gout_hbm, wq_ref, wk_ref, wv_ref, wo_ref, up_ref, down_ref, dq_ref, dv_ref, uq_ref, uv_ref) = refs[:12]
        (bq_ref, bv_ref, bup_ref) = refs[12:15]
        vector_refs, (seg_ref, live_ref) = refs[15:21], refs[21:23]
        (out_ref, gin_ref, glq_ref, glv_ref) = refs[23:27]
        (wq, wk, wv, wo, q, k, v, probs, ctx, n1, s1, act, slope, acc, mask, u_t) = refs[27:43]
        (a_ref, b_ref, c_ref, bias, biases, part, near, far) = refs[43:51]
        (send, recv, bias_send, bias_recv, near_send, near_recv, far_send, far_recv) = refs[51:59]
        (x_ref, gout_ref, load) = refs[59:]
    else:
        (x_ref, gout_ref, a_ref, b_ref, c_ref, biases_ref, dq_ref, dv_ref) = refs[:8]
        vector_refs, (seg_ref, live_ref) = refs[8:14], refs[14:16]
        (out_ref, gin_ref, gl_ref) = refs[16:19]
        (wq, wk, wv, wo, q, k, v, probs, ctx, n1, s1, act, slope, acc, mask, u_t, biases) = refs[19:]
    rows, width = x_ref.shape
    seqs = rows // SEQ
    pairs = width // LANES
    groups = a_ref.shape[0]
    out_bias, down_bias, gain1, shift1, gain2, shift2 = (
        jnp.reshape(ref[...], (1, width)) for ref in vector_refs
    )

    if plan is not None:
        gather = Gather((a_ref, b_ref, c_ref), send, recv)
        me_d, me_t = gather.d, gather.t
        dps = width // wq_ref.shape[0]
        depth = wq_ref.shape[0]
        others_t = [lax.rem(me_t + i, groups) for i in range(1, groups)]
        others_d = [lax.rem(me_d + i, dps) for i in range(1, dps)]
        seg_rows = pl.ds(pl.multiple_of(me_t * (rows // LANES), rows // LANES), rows // LANES)
        barrier = pltpu.get_barrier_semaphore()
        neighbours = [(me_d, other) for other in others_t] + [gather.peer("y")]
        for peer in neighbours:
            pl.semaphore_signal(barrier, inc=1, device_id=peer, device_id_type=BY_MESH)
        for kind in "+-":

            @pl.when(gather.there_is(kind))
            def _(kind=kind):
                pl.semaphore_signal(barrier, inc=1, device_id=gather.peer(kind), device_id_type=BY_MESH)

        loads = [
            pltpu.make_async_copy(source, target, load.at[i])
            for i, (source, target) in enumerate(((x_hbm, x_ref), (gout_hbm, gout_ref)))
        ]
        for copy in loads:
            copy.start()

        mine = pl.ds(pl.multiple_of(me_d * depth, depth), depth)
        across = wq_ref.shape[1]
        acc[0:width, 0:across] = mm_tn(dq_ref[...], uq_ref[...])
        acc[0:width, 256 : 256 + across] = mm_tn(dv_ref[...], uv_ref[...])
        query = (wq_ref[...].astype(WIDE) + ADAPTER_SCALE * acc[mine, 0:across]) * SCORE_SCALE
        value = wv_ref[...].astype(WIDE) + ADAPTER_SCALE * acc[mine, 256 : 256 + across]
        key = wk_ref[...].astype(WIDE)
        out_t = jnp.transpose(wo_ref[...].astype(WIDE))
        a_ref[me_t, mine, 0:128] = query[:, 0:128].astype(NARROW)
        a_ref[me_t, mine, 128:256] = key[:, 0:128].astype(NARROW)
        a_ref[me_t, mine, 256:384] = value[:, 0:128].astype(NARROW)
        a_ref[me_t, mine, 384:512] = jnp.concatenate([query[:, 128:], key[:, 128:]], axis=1).astype(NARROW)
        a_ref[me_t, mine, 512:640] = jnp.concatenate([value[:, 128:], out_t[:, 128:]], axis=1).astype(NARROW)
        a_ref[me_t, mine, 640:768] = out_t[:, 0:128].astype(NARROW)
        bias[me_t, 0:1, :] = jnp.reshape(bup_ref[...], (1, width))
        bias[me_t, 1:2, 0:across] = jnp.reshape(bq_ref[...], (1, across)) * SCORE_SCALE
        bias[me_t, 1:2, 256 : 256 + across] = jnp.reshape(bv_ref[...], (1, across))
        outer = lax.rem(gather.z, 3) == 0
        pl.semaphore_wait(barrier, len(neighbours) + jnp.where(outer, 1, 2))

        def bias_copy(i):
            return pltpu.make_async_remote_copy(
                src_ref=bias.at[me_t],
                dst_ref=bias.at[me_t],
                send_sem=bias_send.at[i],
                recv_sem=bias_recv.at[i],
                device_id=(me_d, others_t[i]),
                device_id_type=BY_MESH,
            )

        for group, name in plan.get("first", {0: ()})[0]:
            gather.step(group, name)
        b_ref[me_t, mine, :] = up_ref[...]
        c_ref[me_t, mine, :] = down_ref[...]
        for i in range(len(others_t)):
            bias_copy(i).start()
    else:
        seg_rows = pl.ds(0, rows // LANES)
        biases[...] = biases_ref[...]

    def ticks(place, step=None):
        if plan is None:
            return
        for at, names in plan.get(place, {}).items():
            if step is None:
                for group, name in names:
                    gather.step(group, name)
            else:

                @pl.when(step == at)
                def _():
                    for group, name in names:
                        gather.step(group, name)

    segment_ids = seg_ref[seg_rows, :]
    live_flags = live_ref[seg_rows, :]
    ticks("start")
    place = lax.broadcasted_iota(jnp.int32, (LANES, LANES), 0) == lax.broadcasted_iota(
        jnp.int32, (LANES, LANES), 1
    )
    for seq in range(seqs):
        wide_ids = []
        key_ids = []
        for block in range(4):
            row = seq * 4 + block
            ids = segment_ids[row : row + 1, :].astype(WIDE)
            live = live_flags[row : row + 1, :]
            key = jnp.where(live == 1, ids, -1.0)
            wide_ids.append(ids)
            key_ids.append(jnp.transpose(jnp.broadcast_to(key, (LANES, LANES))))
        for block in range(1, 4):
            start, stop = KEY_SPANS[block]
            for j in range((stop - start) // LANES):
                kb = start // LANES + j
                seen = key_ids[kb] == wide_ids[block]
                if kb == block:
                    seen = seen | place
                at = SPAN_STARTS[block] + j * LANES
                mask[seq, at : at + LANES, :] = jnp.where(seen, 0.0, NEG_FILL)

    if plan is not None:
        loads[0].wait()
    adapters_down = jnp.concatenate([dq_ref[...].astype(WIDE), dv_ref[...].astype(WIDE)], axis=0)
    u_t[...] = mm_nt(adapters_down.astype(NARROW), x_ref[...]).astype(NARROW)

    ticks("masked")

    for group in range(groups):
        at = slice(group * LANES, (group + 1) * LANES)
        wq[:, at] = a_ref[group, :, 0:128]
        wk[:, at] = a_ref[group, :, 128:256]
        wv[:, at] = a_ref[group, :, 256:384]
        wo[:, at] = a_ref[group, :, 640:768]
    for half in range(groups // 2):
        at = slice((groups + half) * LANES, (groups + half + 1) * LANES)
        first = a_ref[2 * half, :, 384:512].astype(WIDE)
        second = a_ref[2 * half + 1, :, 384:512].astype(WIDE)
        wq[:, at] = pair_select(first, second).astype(NARROW)
        wk[:, at] = pair_select(pltpu.roll(first, HEAD_DIM, 1), pltpu.roll(second, HEAD_DIM, 1)).astype(NARROW)
        first = a_ref[2 * half, :, 512:640].astype(WIDE)
        second = a_ref[2 * half + 1, :, 512:640].astype(WIDE)
        wv[:, at] = pair_select(first, second).astype(NARROW)
        wo[:, at] = pair_select(pltpu.roll(first, HEAD_DIM, 1), pltpu.roll(second, HEAD_DIM, 1)).astype(NARROW)

    if plan is not None:
        for i in range(len(others_t)):
            pltpu.make_async_remote_copy(
                src_ref=bias.at[me_t],
                dst_ref=bias.at[lax.rem(me_t + groups - 1 - i, groups)],
                send_sem=bias_send.at[i],
                recv_sem=bias_recv.at[i],
                device_id=(me_d, others_t[i]),
                device_id_type=BY_MESH,
            ).wait_recv()
        for group in range(groups):
            biases[2 + group : 3 + group, :] = bias[group, 0:1, :]
            biases[0:1, group * LANES : (group + 1) * LANES] = bias[group, 1:2, 0:128]
            biases[1:2, group * LANES : (group + 1) * LANES] = bias[group, 1:2, 256:384]
        for half in range(groups // 2):
            at = slice((groups + half) * LANES, (groups + half + 1) * LANES)
            for row, first in ((0, 128), (1, 384)):
                low = jnp.broadcast_to(bias[2 * half, 1:2, first : first + 128], (8, LANES))
                high = jnp.broadcast_to(bias[2 * half + 1, 1:2, first : first + 128], (8, LANES))
                biases[row : row + 1, at] = pair_select(low, high)[0:1]

    def project(step, carry):
        ticks("project", step)
        at = pl.ds(pl.multiple_of(step * 256, 256), 256)
        xs = x_ref[...]
        q[:, at] = (mm(xs, wq[:, at]) + biases[0:1, at]).astype(NARROW)
        k[:, at] = mm(xs, wk[:, at]).astype(NARROW)
        v[:, at] = (mm(xs, wv[:, at]) + biases[1:2, at]).astype(NARROW)
        return carry

    lax.fori_loop(0, width // 256, project, 0)

    lane = lax.broadcasted_iota(jnp.int32, (LANES, LANES), 1)
    together = 3
    steps = seqs * pairs // together

    def stacked(tile):
        none = jnp.zeros_like(tile)
        return jnp.concatenate(
            [jnp.where(lane < HEAD_DIM, tile, none), jnp.where(lane < HEAD_DIM, none, tile)], axis=0
        )

    def merged(tile):
        return jnp.where(lane < HEAD_DIM, tile[:LANES], tile[LANES:]).astype(NARROW)

    def work_of(step, together=together):
        items = []
        for one in range(together):
            index = step * together + one
            seq = index // pairs
            base = pl.multiple_of(seq * SEQ, SEQ)
            at = pl.ds(pl.multiple_of((index - seq * pairs) * LANES, LANES), LANES)
            for block, (start, stop) in enumerate(KEY_SPANS):
                here = pl.ds(base + block * LANES, LANES)
                there = pl.ds(base + start, stop - start)
                span = pl.ds(SPAN_STARTS[block], stop - start)
                items.append((index, seq, here, there, at, span, block))
        return items

    def attend(step, carry):
        ticks("attend", step)
        items = work_of(step)
        scores = [mm_nt(k[there, at], stacked(q[here, at])) for _, _, here, there, at, _, _ in items]
        weights = []
        for (index, seq, _, _, _, span, block), score in zip(items, scores):
            if block:
                shade = mask[seq, span, :]
                score = score + jnp.concatenate([shade, shade], axis=1)
            powers = jnp.exp(score - jnp.max(score, axis=0, keepdims=True))
            total = jnp.sum(powers, axis=0, keepdims=True)
            weights.append((powers * (1.0 / total)).astype(NARROW))
            probs[index, span, :] = weights[-1]
        for (_, _, here, there, at, _, _), weight in zip(items, weights):
            ctx[here, at] = merged(mm_tn(weight, v[there, at]))
        return carry

    lax.fori_loop(0, steps, attend, 0)

    def first_norm(step, carry):
        ticks("first_norm", step)
        at = pl.ds(pl.multiple_of(step * 256, 256), 256)
        r = x_ref[at, :].astype(WIDE) + (mm_nt(ctx[at, :], wo[...]) + out_bias)
        centered = r - row_mean(r)
        inverse = lax.rsqrt(row_mean(centered * centered) + EPSILON)
        normed = centered * inverse
        n1[at, :] = normed
        s1[at, :] = inverse
        out_ref[at, :] = (normed * gain1 + shift1).astype(NARROW)
        return carry

    lax.fori_loop(0, rows // 256, first_norm, 0, unroll=2)

    def up(group, carry):
        ticks("up", group)
        for j in range(width // 256):
            cols = slice(j * 256, (j + 1) * 256)
            at = pl.ds(pl.multiple_of(group * width + j * 256, 256), 256)
            inner = mm(out_ref[...], b_ref[group, :, cols]) + biases[pl.ds(2 + group, 1), cols]
            value, grad = gelu_parts(inner)
            act[:, at] = value.astype(NARROW)
            slope[:, at] = grad.astype(NARROW)
        return carry

    ticks("before up")
    lax.fori_loop(0, groups, up, 0)
    ticks("before down")
    if plan is not None:
        loads[1].wait()

    def second_norm(step, carry):
        at = pl.ds(pl.multiple_of(step * 512, 512), 512)
        r = n1[at, :] * gain1 + shift1 + down_bias
        for group in range(groups):
            r = r + mm_nt(act[at, group * width : (group + 1) * width], c_ref[group])
        centered = r - row_mean(r)
        inverse = lax.rsqrt(row_mean(centered * centered) + EPSILON)
        normed = centered * inverse
        out_ref[at, :] = (normed * gain2 + shift2).astype(NARROW)
        e = gout_ref[at, :].astype(WIDE) * gain2
        acc[at, :] = inverse * (e - row_mean(e) - normed * row_mean(e * normed))
        return carry

    lax.fori_loop(0, rows // 512, second_norm, 0)

    def down_back(step, carry):
        at = pl.ds(pl.multiple_of(step * 512, 512), 512)
        second = acc[at, :]
        low = second.astype(NARROW)
        total = second
        for group in range(groups):
            cols = slice(group * width, (group + 1) * width)
            grad = (mm(low, c_ref[group]) * slope[at, cols].astype(WIDE)).astype(NARROW)
            total = total + mm_nt(grad, b_ref[group])
        normed = n1[at, :]
        e = total * gain1
        first = s1[at, :] * (e - row_mean(e) - normed * row_mean(e * normed))
        acc[at, :] = first
        ctx[at, :] = mm(first.astype(NARROW), wo[...]).astype(NARROW)
        return carry

    lax.fori_loop(0, rows // 512, down_back, 0)

    def attend_back(step, carry):
        items = work_of(step, pairs)
        grads = [stacked(ctx[here, at]) for _, _, here, _, at, _, _ in items]
        rows_q = [stacked(q[here, at]) for _, _, here, _, at, _, _ in items]
        grad_q, grad_k, grad_v = [], {}, {}
        for n, (index, seq, here, there, at, span, block) in enumerate(items):
            weights = probs[index, span, :]
            part = weights.astype(WIDE) * mm_nt(v[there, at], grads[n])
            inside = jnp.sum(part, axis=0, keepdims=True)
            grad_scores = (part - weights.astype(WIDE) * inside).astype(NARROW)
            for_keys = mm(grad_scores, rows_q[n])
            for_values = mm(weights, grads[n])
            grad_q.append(merged(mm_tn(grad_scores, k[there, at])))
            start, stop = KEY_SPANS[block]
            for j in range((stop - start) // LANES):
                rows_here = slice(j * LANES, (j + 1) * LANES)
                key = n // 4, start // LANES + j
                for grad, more in ((grad_k, for_keys), (grad_v, for_values)):
                    grad[key] = grad[key] + more[rows_here] if key in grad else more[rows_here]
        for (_, _, here, _, at, _, _), grad in zip(items, grad_q):
            q[here, at] = grad
        for one, kb in grad_k:
            _, _, here, _, at, _, _ = items[4 * one + kb]
            k[here, at] = grad_k[one, kb].astype(NARROW)
            v[here, at] = grad_v[one, kb].astype(NARROW)
        return carry

    lax.fori_loop(0, seqs, attend_back, 0)

    grad_q = mm(u_t[0:8, :], q[...]) * (ADAPTER_SCALE * SCORE_SCALE)
    grad_v = mm(u_t[8:16, :], v[...]) * ADAPTER_SCALE

    def input_back(step, carry):
        at = pl.ds(pl.multiple_of(step * 256, 256), 256)
        total = acc[at, :] + mm_nt(q[at, :], wq[...])
        total = total + mm_nt(k[at, :], wk[...])
        total = total + mm_nt(v[at, :], wv[...])
        gin_ref[at, :] = total.astype(NARROW)
        return carry

    if plan is None:
        gl_ref[0:8, :] = grad_q
        gl_ref[8:16, :] = grad_v
        lax.fori_loop(0, rows // 256, input_back, 0)
        return

    for group in range(groups):
        for row, grad in ((0, grad_q), (8, grad_v)):
            part[group, row : row + 8, 0:128] = grad[:, group * LANES : (group + 1) * LANES]
            other = groups + group // 2
            part[group, row : row + 8, 128:256] = grad[:, other * LANES : (other + 1) * LANES]

    def near_copy(i, slot):
        return pltpu.make_async_remote_copy(
            src_ref=part.at[others_t[i]],
            dst_ref=near.at[slot],
            send_sem=near_send.at[i],
            recv_sem=near_recv.at[i],
            device_id=(me_d, others_t[i]),
            device_id_type=BY_MESH,
        )

    def far_copy(i, slot):
        return pltpu.make_async_remote_copy(
            src_ref=far.at[me_d],
            dst_ref=far.at[slot],
            send_sem=far_send.at[i],
            recv_sem=far_recv.at[i],
            device_id=(others_d[i], me_t),
            device_id_type=BY_MESH,
        )

    for i in range(len(others_t)):
        near_copy(i, i).start()
    lax.fori_loop(0, rows // 512, input_back, 0)
    total = part[me_t]
    for i in range(len(others_t)):
        near_copy(i, i).wait_recv()
        total = total + near[i]
    far[me_d] = total
    for i in range(len(others_d)):
        far_copy(i, me_d).start()
    lax.fori_loop(rows // 512, rows // 256, input_back, 0)
    for group in range(3):
        gather.finish(group)
    for i in range(len(others_t)):
        bias_copy(i).wait_send()
        near_copy(i, i).wait_send()
    for i in range(len(others_d)):
        far_copy(i, lax.rem(me_d + dps - 1 - i, dps)).wait_recv()
    total = far[0]
    for i in range(1, dps):
        total = total + far[i]
    last = jnp.where(lax.rem(me_t, 2) == 0, total[:, 128:], pltpu.roll(total[:, 128:], HEAD_DIM, 1))
    glq_ref[:, 0:128] = total[0:8, 0:128]
    glv_ref[:, 0:128] = total[8:16, 0:128]
    glq_ref[:, 128:192] = last[0:8, 0:HEAD_DIM]
    glv_ref[:, 128:192] = last[8:16, 0:HEAD_DIM]
    for i in range(len(others_d)):
        far_copy(i, me_d).wait_send()


def scratch(rows, width, hidden):
    pairs = width // LANES
    seqs = rows // SEQ
    square = pltpu.VMEM((width, width), NARROW)
    plane = pltpu.VMEM((rows, width), NARROW)
    return [
        square,
        square,
        square,
        square,
        plane,
        plane,
        plane,
        pltpu.VMEM((seqs * pairs, SPAN_TOTAL, 2 * LANES), NARROW),
        plane,
        pltpu.VMEM((rows, width), WIDE),
        pltpu.VMEM((rows, 1), WIDE),
        pltpu.VMEM((rows, hidden), NARROW),
        pltpu.VMEM((rows, hidden), NARROW),
        pltpu.VMEM((rows, width), WIDE),
        pltpu.VMEM((seqs, SPAN_TOTAL, LANES), WIDE),
        pltpu.VMEM((2 * ADAPTER_RANK, rows), NARROW),
    ]


def run_layer(x, gout, a, b, c, biases, downs, vectors, seg, live):
    rows, width = x.shape
    shape = jax.ShapeDtypeStruct
    hidden = b.shape[0] * b.shape[2]
    return pl.pallas_call(
        functools.partial(kernel, None),
        out_shape=(
            shape((rows, width), NARROW),
            shape((rows, width), NARROW),
            shape((2 * ADAPTER_RANK, width), WIDE),
        ),
        in_specs=[pl.BlockSpec(memory_space=pltpu.VMEM)] * 16,
        out_specs=[pl.BlockSpec(memory_space=pltpu.VMEM)] * 3,
        scratch_shapes=scratch(rows, width, hidden) + [pltpu.VMEM((8, width), WIDE)],
        compiler_params=pltpu.CompilerParams(vmem_limit_bytes=63 << 20),
    )(x, gout, a, b, c, biases, *downs, *vectors, seg, live)


def run_layer_and_gather(x, gout, blocks, adapters, biases, vectors, seg, live):
    rows, width = x.shape
    groups = width // blocks[0].shape[1]
    dps = width // blocks[0].shape[0]
    gathered = pltpu.VMEM((groups, width, width), NARROW)
    signals = pltpu.SemaphoreType.DMA
    operands = (x, gout, *blocks, *adapters, *biases, *vectors, seg, live)
    return pl.pallas_call(
        functools.partial(kernel, PLAN),
        out_shape=(
            pltpu.VMEM((rows, width), NARROW),
            pltpu.VMEM((rows, width), NARROW),
            pltpu.VMEM((ADAPTER_RANK, width // groups), WIDE),
            pltpu.VMEM((ADAPTER_RANK, width // groups), WIDE),
        ),
        in_specs=[pl.BlockSpec(memory_space=pl.ANY)] * 2
        + [pl.BlockSpec(memory_space=pltpu.VMEM)] * (len(operands) - 2),
        out_specs=[pl.BlockSpec(memory_space=pltpu.VMEM)] * 4,
        scratch_shapes=scratch(rows, width, groups * width)
        + [
            gathered,
            gathered,
            gathered,
            pltpu.VMEM((groups, 8, width), WIDE),
            pltpu.VMEM((8, width), WIDE),
            pltpu.VMEM((groups, 2 * ADAPTER_RANK, 2 * LANES), WIDE),
            pltpu.VMEM((groups - 1, 2 * ADAPTER_RANK, 2 * LANES), WIDE),
            pltpu.VMEM((dps, 2 * ADAPTER_RANK, 2 * LANES), WIDE),
            signals((3, len(SIGNALS))),
            signals((3, len(SIGNALS))),
            signals((groups - 1,)),
            signals((groups - 1,)),
            signals((groups - 1,)),
            signals((groups - 1,)),
            signals((dps - 1,)),
            signals((dps - 1,)),
            pltpu.VMEM((rows, width), NARROW),
            pltpu.VMEM((rows, width), NARROW),
            signals((2,)),
        ],
        compiler_params=pltpu.CompilerParams(
            collective_id=0, has_side_effects=True, vmem_limit_bytes=59 << 20
        ),
    )(*operands)


def in_pairs(block, groups):
    parts = block.reshape(block.shape[0], groups, 3, HEAD_DIM)
    front = parts[:, :, :2].reshape(block.shape[0], -1)
    return jnp.concatenate([front, parts[:, :, 2].reshape(block.shape[0], -1)], axis=1)


def from_pairs(block, groups):
    front = block[:, : groups * LANES].reshape(block.shape[0], groups, 2, HEAD_DIM)
    back = block[:, groups * LANES :].reshape(block.shape[0], groups, 1, HEAD_DIM)
    return jnp.concatenate([front, back], axis=2).reshape(block.shape[0], -1)


def body(
    grid,
    layer_input_rows,
    output_gradient,
    query_weight,
    key_weight,
    value_weight,
    output_weight,
    up_weight,
    down_weight,
    query_bias_vector,
    value_bias_vector,
    output_bias_vector,
    up_bias_vector,
    down_bias_vector,
    query_down_frozen,
    value_down_frozen,
    query_up_trained,
    value_up_trained,
    first_norm_gain,
    first_norm_bias,
    second_norm_gain,
    second_norm_bias,
    segments,
    sentence_row_mask,
):
    everyone = ("tensor", "dp")
    rows, width = layer_input_rows.shape
    depth, across = query_weight.shape
    groups = width // across
    vectors = (
        output_bias_vector,
        down_bias_vector,
        first_norm_gain,
        first_norm_bias,
        second_norm_gain,
        second_norm_bias,
    )
    downs = (query_down_frozen.T, value_down_frozen.T)
    segment_rows = segments.reshape(-1, LANES)
    live_rows = sentence_row_mask.reshape(-1, LANES)
    if grid == (8, 4):
        return run_layer_and_gather(
            layer_input_rows,
            output_gradient,
            (query_weight, key_weight, value_weight, output_weight, up_weight, down_weight.T),
            (*downs, query_up_trained, value_up_trained),
            (query_bias_vector, value_bias_vector, up_bias_vector),
            vectors,
            segment_rows,
            live_rows,
        )

    place = lax.axis_index("tensor")
    which = lax.axis_index("dp")

    def folded(weight, down, up):
        own = lax.dynamic_slice_in_dim(down, which * depth, depth, axis=0)
        return weight.astype(WIDE) + ADAPTER_SCALE * mm(own, up)

    wq = (folded(query_weight, query_down_frozen, query_up_trained) * SCORE_SCALE).astype(NARROW)
    wv = folded(value_weight, value_down_frozen, value_up_trained).astype(NARROW)
    wk = key_weight
    wo = output_weight.T
    block_a = jnp.concatenate(
        [wq[:, :128], wk[:, :128], wv[:, :128], wq[:, 128:], wk[:, 128:], wv[:, 128:], wo[:, 128:], wo[:, :128]],
        axis=1,
    )

    def spread(block):
        return lax.all_gather(block, everyone, axis=0, tiled=True).reshape(groups, width, width)

    a, b, c = spread(block_a), spread(up_weight), spread(down_weight.T)
    query_bias = lax.all_gather(query_bias_vector * SCORE_SCALE, "tensor", axis=0, tiled=True)
    value_bias = lax.all_gather(value_bias_vector, "tensor", axis=0, tiled=True)
    up_bias = lax.all_gather(up_bias_vector, "tensor", axis=0, tiled=True)
    biases = jnp.concatenate(
        [
            in_pairs(query_bias[None], groups),
            in_pairs(value_bias[None], groups),
            up_bias.reshape(groups, width),
            jnp.zeros((6 - groups, width), WIDE),
        ],
        axis=0,
    )
    blocks = rows // LANES
    seg = lax.dynamic_slice_in_dim(segment_rows, place * blocks, blocks)
    live = lax.dynamic_slice_in_dim(live_rows, place * blocks, blocks)
    output, grad_input, grads = run_layer(
        layer_input_rows, output_gradient, a, b, c, biases, downs, vectors, seg, live
    )
    grads = from_pairs(lax.psum(grads, everyone), groups)
    grads = lax.dynamic_slice_in_dim(grads, place * across, across, axis=1)
    return output, grad_input, grads[:ADAPTER_RANK], grads[ADAPTER_RANK:]


IN_SPECS = (
    P(("dp", "tensor"), None),
    P(("dp", "tensor"), None),
    P("dp", "tensor"),
    P("dp", "tensor"),
    P("dp", "tensor"),
    P("tensor", "dp"),
    P("dp", "tensor"),
    P("tensor", "dp"),
    P("tensor"),
    P("tensor"),
    P(),
    P("tensor"),
    P(),
    P(),
    P(),
    P(None, "tensor"),
    P(None, "tensor"),
    P(),
    P(),
    P(),
    P(),
    P("dp"),
    P("dp"),
)
OUT_SPECS = (
    P(("dp", "tensor"), None),
    P(("dp", "tensor"), None),
    P(None, "tensor"),
    P(None, "tensor"),
)


def solution(mesh):
    grid = (mesh.shape["dp"], mesh.shape["tensor"])
    layer = functools.partial(body, grid)
    return jax.shard_map(layer, mesh=mesh, in_specs=IN_SPECS, out_specs=OUT_SPECS, check_vma=False)
```
